32 devices in a mesh: fsdp: 8 (over z, y), dp: 4 (over x, core).
Axes of the slice: x: 2, y: 2, z: 4, core: 2. Of those that a mesh axis runs over, the one named last changes fastest.
Arguments:
- tokens: float32 [32768, 768], P(('fsdp', 'dp')), may hold values from -6 to 6
- lengths: int32 [64, 9], P(('fsdp', 'dp')), may hold values from 1 to 128, 512 in all within a row
- cotangent: float32 [32768, 768], P(('fsdp', 'dp')), may hold values from -6 to 6
- ln1_gain: bfloat16 [768], P('fsdp'), may hold values from 0.5 to 1.5
- ln1_bias: bfloat16 [768], P('fsdp'), may hold values from -1.5 to 1.5
- w_qkv: bfloat16 [768, 2304], P('fsdp'), may hold values from -0.21875 to 0.21875
- qkv_bias: bfloat16 [768, 2], P('fsdp'), may hold values from -1.5 to 1.5
- w_out: bfloat16 [768, 768], P('fsdp'), may hold values from -1.75 to 1.75
- out_bias: bfloat16 [768], P('fsdp'), may hold values from -1.5 to 1.5
- scale_attn: bfloat16 [768], P('fsdp'), may hold values from 0.5 to 1.5
- ln2_gain: bfloat16 [768], P('fsdp'), may hold values from 0.5 to 1.5
- ln2_bias: bfloat16 [768], P('fsdp'), may hold values from -1.5 to 1.5
- w_fc1: bfloat16 [768, 3072], P('fsdp'), may hold values from -0.21875 to 0.21875
- fc1_bias: bfloat16 [3072], P('fsdp'), may hold values from -1.5 to 1.5
- w_fc2: bfloat16 [3072, 768], P('fsdp'), may hold values from -0.21875 to 0.21875
- fc2_bias: bfloat16 [768], P('fsdp'), may hold values from -1.5 to 1.5
- scale_ffn: bfloat16 [768], P('fsdp'), may hold values from 0.5 to 1.5
Outputs:
- output: float32 [32768, 768], P(('fsdp', 'dp'))
- grad_tokens: float32 [32768, 768], P(('fsdp', 'dp'))
- grad_ln1_gain: float32 [768], P('fsdp')
- grad_ln1_bias: float32 [768], P('fsdp')
- grad_w_qkv: float32 [768, 2304], P('fsdp')
- grad_qkv_bias: float32 [768, 2], P('fsdp')
- grad_w_out: float32 [768, 768], P('fsdp')
- grad_out_bias: float32 [768], P('fsdp')
- grad_scale_attn: float32 [768], P('fsdp')
- grad_ln2_gain: float32 [768], P('fsdp')
- grad_ln2_bias: float32 [768], P('fsdp')
- grad_w_fc1: float32 [768, 3072], P('fsdp')
- grad_fc1_bias: float32 [3072], P('fsdp')
- grad_w_fc2: float32 [3072, 768], P('fsdp')
- grad_fc2_bias: float32 [768], P('fsdp')
- grad_scale_ffn: float32 [768], P('fsdp')
The draws below stay inside these ranges and needn't reach their ends.
Inputs may be any that keep to these rules, and one draw needn't show every extreme that they name: `lengths`: in each row the 9 entries sum to 512, every entry is at least 1, and the largest entry of each row is exactly 128; the last entry is the padding at the row's end.
All inputs are finite; a program needn't handle non-finite values.
Results may differ from the reference program's by a relative error of at most 0.014.
Values may be sent and summed in bfloat16 or wider, within the bound.
A program may use at most 192 MiB of HBM per device.

```python
import math
import jax
import jax.numpy as jnp
import numpy as np
from jax import lax

D = 768
FF = 3072
HEADS = 12
HEAD_DIM = 64
SLOTS = 512
SEGS = 8
MOST = 128
ROWS = 64
TOKENS = 32768


def with_spikes(drawn, key, source, target, blocks, factor):
    def block_of(axis_at):
        return (jnp.arange(drawn.shape[axis_at]) // (drawn.shape[axis_at] // blocks)).reshape((-1,) + (1,) * (drawn.ndim - 1 - axis_at))

    near = jax.random.permutation(key, blocks)[block_of(target)]
    other_side = (block_of(target) + blocks // 2) % blocks
    return jnp.where((block_of(source) == near) | (block_of(source) == other_side), factor * drawn, drawn)


def level_of(key, extent, split, least, top_value):
    level, own = 1.0, jax.random.fold_in(key, 6)
    for dim, shards_of in split:
        heights = jnp.exp(jax.random.uniform(jax.random.fold_in(own, dim), (shards_of,), jnp.float32, least / len(split), top_value / len(split)))
        level = level * jnp.repeat(heights, extent[dim] // shards_of).reshape([-1 if axis == dim else 1 for axis in range(len(extent))])
    return level


def profile(number_of, total, most, skew):
    portions = [(1 << 20) // math.isqrt(grade ** skew) + 1 for grade in range(2, number_of + 1)]
    rest, counts = total - most - (number_of - 1), [1] * (number_of - 1)
    while rest > 0:
        free = [i for i in range(number_of - 1) if counts[i] < most]
        pool, budget = sum([portions[i] for i in free]), rest
        for i in free:
            more = min(most - counts[i], max(1, budget * portions[i] // pool), rest)
            counts[i] = counts[i] + more
            rest = rest - more
    return np.array([most] + counts)


def ragged(own_key, number_of, total, most, slope):
    if number_of == 2:
        one = jax.random.randint(own_key, (), max(1, total - most), min(most, total - 1) + 1)
        return jnp.stack([one, total - one])
    tallies = jnp.asarray(profile(number_of, total, most, slope), jnp.int32)
    twos = (number_of - 1) // 2
    donor, sink = tallies[1:1 + 2 * twos:2], tallies[2:2 + 2 * twos:2]
    room = jnp.minimum(donor - 1, most - sink)
    shifted = jax.random.randint(jax.random.fold_in(own_key, 1), (twos,), 0, 1 << 20) % (room + 1)
    tallies = tallies.at[1:1 + 2 * twos:2].set(donor - shifted).at[2:2 + 2 * twos:2].set(sink + shifted)
    return tallies[jax.random.permutation(jax.random.fold_in(own_key, 2), number_of)]


def scatter_about(key, shape, deviation, bound, shards=(), dtype=jnp.bfloat16):
    factor_of = level_of(key, shape, shards, -0.22, 0.18) if shards else 1.0
    values = jax.random.normal(key, shape, jnp.float32) * deviation * factor_of
    return jnp.minimum(jnp.maximum(values, -bound), bound).astype(dtype)


def bell_draw_with(own_key, extent, width, bound, pieces, heavy, held_as=jnp.bfloat16):
    values = width * jax.random.normal(own_key, extent, jnp.float32)
    if pieces:
        values = values * level_of(own_key, extent, pieces, -0.22, 0.18)
    return jnp.clip(with_spikes(values, jax.random.fold_in(own_key, 3), *heavy), -bound, bound).astype(held_as)


def setup_inputs(seed: int = 0) -> dict:
    seeds = jax.random.split(jax.random.key(seed), 18)
    return {
        "tokens": bell_draw_with(seeds[0], (TOKENS, D), 1.0, 6.0, ((0, 32),), (0, 1, 32, 2.75), jnp.float32),
        "lengths": jax.vmap(lambda own: ragged(own, SEGS + 1, SLOTS, MOST, 1))(jax.random.split(seeds[1], ROWS)).reshape((ROWS, SEGS + 1)).astype(jnp.int32),
        "cotangent": bell_draw_with(seeds[2], (TOKENS, D), 1.0, 6.0, ((0, 32),), (0, 1, 32, 2.75), jnp.float32),
        "ln1_gain": jnp.clip(1.0 + 0.1 * jax.random.normal(seeds[3], (D,), jnp.float32), 0.5, 1.5).astype(jnp.bfloat16),
        "ln1_bias": scatter_about(seeds[4], (D,), 0.3, 1.5, ((0, 8),)),
        "w_qkv": scatter_about(seeds[5], (D, 3 * D), D ** -0.5, 0.21875, ((0, 8),)),
        "qkv_bias": scatter_about(seeds[6], (D, 2), 0.3, 1.5, ((0, 8),)),
        "w_out": scatter_about(seeds[7], (D, D), (D // 64) ** -0.5, 1.75, ((0, 8),)),
        "out_bias": scatter_about(seeds[8], (D,), 0.3, 1.5, ((0, 8),)),
        "scale_attn": jnp.clip(1.0 + 0.1 * jax.random.normal(seeds[9], (D,), jnp.float32), 0.5, 1.5).astype(jnp.bfloat16),
        "ln2_gain": jnp.clip(1.0 + 0.1 * jax.random.normal(seeds[10], (D,), jnp.float32), 0.5, 1.5).astype(jnp.bfloat16),
        "ln2_bias": scatter_about(seeds[11], (D,), 0.3, 1.5, ((0, 8),)),
        "w_fc1": scatter_about(seeds[12], (D, FF), D ** -0.5, 0.21875, ((0, 8),)),
        "fc1_bias": scatter_about(seeds[13], (FF,), 0.3, 1.5, ((0, 8),)),
        "w_fc2": scatter_about(seeds[14], (FF, D), (FF // 4) ** -0.5, 0.21875, ((0, 8),)),
        "fc2_bias": scatter_about(seeds[15], (D,), 0.3, 1.5, ((0, 8),)),
        "scale_ffn": jnp.clip(1.0 + 0.1 * jax.random.normal(seeds[16], (D,), jnp.float32), 0.5, 1.5).astype(jnp.bfloat16),
    }


@jax.custom_vjp
def low(v):
    return lax.optimization_barrier(v.astype(jnp.bfloat16)).astype(jnp.float32)

@jax.custom_vjp
def low_back(v):
    return v

def low_keep(v):
    return (low(v), None)

def low_pass(kept, grad):
    return (grad,)

def back_keep(v):
    return (v, None)

def back_low(kept, grad):
    return (low(grad),)
low.defvjp(low_keep, low_pass)
low_back.defvjp(back_keep, back_low)
norm_eps = 1e-06
masked_score = -1e+30
highest = lax.Precision.HIGHEST

def layer_norm(values, gain, shift):
    centered = values - lax.optimization_barrier(jnp.mean(values, axis=-1, keepdims=True))
    spread = lax.optimization_barrier(jnp.mean(centered * centered, axis=-1, keepdims=True))
    return centered * lax.rsqrt(spread + norm_eps) * gain + shift

def segment_ids(lengths, slots):
    ends = jnp.cumsum(lengths, axis=-1)
    position = lax.broadcasted_iota(jnp.int32, (lengths.shape[0], slots, lengths.shape[1]), 1)
    return lax.optimization_barrier(jnp.sum((position >= ends[:, None, :]).astype(jnp.int32), axis=-1))

def forward(values, params, segment):
    gain_one, shift_one, qkv_full, bias_qkv, out_full, bias_out, scale_one, gain_two, shift_two, fc1_full, bias_fc1, fc2_full, bias_fc2, scale_two = params
    row_count = segment.shape[0]

    def head_view(array):
        return array.reshape(row_count, SLOTS, HEADS, HEAD_DIM)
    normed_one = low(layer_norm(values, gain_one, shift_one))
    qkv = jnp.dot(normed_one, qkv_full, precision=highest)
    query = low_back(low(qkv[:, :D] + bias_qkv[:, 0]))
    key = low_back(low(qkv[:, D:2 * D]))
    value = low_back(low(qkv[:, 2 * D:] + bias_qkv[:, 1]))
    scores = jnp.einsum('rqhe,rkhe->rhqk', head_view(query), head_view(key), precision=highest) * (1.0 / math.sqrt(HEAD_DIM))
    scores = low_back(scores)
    same = segment[:, None, :, None] == segment[:, None, None, :]
    scores = jnp.where(same, scores, masked_score)
    probs = low(jax.nn.softmax(scores, axis=-1))
    mixed = jnp.einsum('rhqk,rkhe->rqhe', probs, head_view(value), precision=highest).reshape(-1, D)
    mixed = low_back(low(mixed))
    attn_proj = low_back(jnp.dot(mixed, out_full, precision=highest) + bias_out)
    resid = values + scale_one * attn_proj
    normed_two = low(layer_norm(resid, gain_two, shift_two))
    hidden_pre = low_back(jnp.dot(normed_two, fc1_full, precision=highest) + bias_fc1)
    activated = low(jax.nn.gelu(hidden_pre, approximate=False))
    ffn_out = low_back(jnp.dot(activated, fc2_full, precision=highest) + bias_fc2)
    return resid + scale_two * ffn_out

def reference(tokens, lengths, cotangent, ln1_gain, ln1_bias, w_qkv, qkv_bias, w_out, out_bias, scale_attn, ln2_gain, ln2_bias, w_fc1, fc1_bias, w_fc2, fc2_bias, scale_ffn):
    params = tuple((item.astype(jnp.float32) for item in (ln1_gain, ln1_bias, w_qkv, qkv_bias, w_out, out_bias, scale_attn, ln2_gain, ln2_bias, w_fc1, fc1_bias, w_fc2, fc2_bias, scale_ffn)))
    segment = segment_ids(lengths, SLOTS)
    valid = (segment < SEGS).astype(jnp.float32)
    group = math.gcd(ROWS, 8)
    count = ROWS // group
    inputs = tokens.astype(jnp.float32).reshape(count, group * SLOTS, D)
    upstream = (cotangent.astype(jnp.float32).reshape(ROWS, SLOTS, D) * valid[:, :, None]).reshape(count, group * SLOTS, D)
    segments = segment.reshape(count, group, SLOTS)

    def step(totals, item):
        block, grad_out, block_segment = item

        def apply(values, *weights):
            return forward(values, weights, block_segment)
        result, back = jax.vjp(apply, block, *params)
        grads = back(grad_out)
        return (tuple((total + grad for total, grad in zip(totals, grads[1:]))), (result, grads[0]))
    zeros = tuple((jnp.zeros_like(item) for item in params))
    totals, (results, grad_inputs) = lax.scan(step, zeros, (inputs, upstream, segments))
    grad_gain_one, grad_shift_one, grad_qkv, grad_bias_qkv, grad_out, grad_bias_out, grad_scale_one, grad_gain_two, grad_shift_two, grad_fc1, grad_bias_fc1, grad_fc2, grad_bias_fc2, grad_scale_two = totals
    return (results.reshape(TOKENS, D), grad_inputs.reshape(TOKENS, D), grad_gain_one, grad_shift_one, grad_qkv, grad_bias_qkv, grad_out, grad_bias_out, grad_scale_one, grad_gain_two, grad_shift_two, grad_fc1, grad_bias_fc1, grad_fc2, grad_bias_fc2, grad_scale_two)
```

```python
import functools
import math

import jax
import jax.numpy as jnp
from jax import lax
from jax.experimental import pallas as pl
from jax.experimental.pallas import tpu as pltpu
from jax.sharding import PartitionSpec as P

HEAD_DIM = 64
norm_eps = 1e-06
masked_score = -1e30
BF = jnp.bfloat16
F32 = jnp.float32
TILE = 256
QB = 128
VMEM_LIMIT = 67043328

G1_ROW, B1_ROW, QB_ROW, VB_ROW, OB_ROW, SA_ROW, G2_ROW, B2_ROW, FB2_ROW, SF_ROW, FB1_ROW = range(11)
VEC_ROWS = 16


def mm(a, b):
    return lax.dot_general(a, b, (((1,), (0,)), ((), ())), preferred_element_type=F32)


def mm_bt(a, b):
    return lax.dot_general(a, b, (((1,), (1,)), ((), ())), preferred_element_type=F32)


def mm_at(a, b):
    return lax.dot_general(a, b, (((0,), (0,)), ((), ())), preferred_element_type=F32)


def norm_parts(values):
    centered = values - jnp.mean(values, axis=-1, keepdims=True)
    spread = jnp.mean(centered * centered, axis=-1, keepdims=True)
    inv = lax.rsqrt(spread + norm_eps)
    return centered * inv, inv


def window(block, blocks):
    first = max(block - 1, 0)
    last = min(block + 2, blocks)
    return first * QB, (last - first) * QB


def prob_offsets(blocks):
    offsets, total = [], 0
    for block in range(blocks):
        offsets.append(total)
        total += window(block, blocks)[1]
    return offsets, total


def lane_tile(values, times):
    return jnp.concatenate([values] * times, axis=1) if times > 1 else values


def fill_segments(lengths_ref, rows, slots, seg_col, seg_row):
    count = lengths_ref.shape[1]
    for r in range(rows):
        down = lax.broadcasted_iota(jnp.int32, (slots, 128), 0)
        along = lax.broadcasted_iota(jnp.int32, (8, slots), 1)
        col = jnp.zeros((slots, 128), jnp.int32)
        row = jnp.zeros((8, slots), jnp.int32)
        end = jnp.int32(0)
        for j in range(count):
            end = end + lengths_ref[r, j]
            col = col + (down >= end).astype(jnp.int32)
            row = row + (along >= end).astype(jnp.int32)
        seg_col[pl.ds(r * slots, slots), :] = col
        seg_row[r] = row


def attention_forward(rows, slots, pairs, width, qkv, seg_col, seg_row, prob_slot, mixed, r, pair):
    blocks = slots // QB
    offsets, _ = prob_offsets(blocks)
    low = lax.broadcasted_iota(jnp.int32, (QB, 128), 1) < HEAD_DIM
    col = pl.multiple_of(pair * 128, 128)
    base = pl.multiple_of(r * slots, slots)
    zero = jnp.zeros((QB, 128), BF)
    for b in range(blocks):
        start, wide = window(b, blocks)
        q = qkv[pl.ds(base + b * QB, QB), pl.ds(col, 128)]
        k = qkv[pl.ds(base + start, wide), pl.ds(width + col, 128)]
        v = qkv[pl.ds(base + start, wide), pl.ds(2 * width + col, 128)]
        same = lane_tile(seg_col[pl.ds(base + b * QB, QB), :], wide // 128) == seg_row[r, 0:1, start : start + wide]
        q2 = jnp.concatenate([jnp.where(low, q, zero), jnp.where(low, zero, q)], axis=0)
        scores = mm_bt(q2, k)
        scores = jnp.concatenate(
            [jnp.where(same, scores[:QB], masked_score), jnp.where(same, scores[QB:], masked_score)], axis=0
        )
        peak = jnp.max(scores, axis=-1, keepdims=True)
        weights = jnp.exp(scores - peak)
        total = jnp.sum(weights, axis=-1, keepdims=True)
        probs = (weights * (1.0 / total)).astype(BF)
        prob_slot[:, offsets[b] : offsets[b] + wide] = probs
        out = mm(probs, v)
        mixed[pl.ds(base + b * QB, QB), pl.ds(col, 128)] = jnp.where(low, out[:QB], out[QB:]).astype(BF)


def attention_backward(rows, slots, pairs, width, qkv, prob_slot, mixed, grad_mixed, grads, r, pair):
    blocks = slots // QB
    offsets, _ = prob_offsets(blocks)
    low = lax.broadcasted_iota(jnp.int32, (QB, 128), 1) < HEAD_DIM
    low_all = lax.broadcasted_iota(jnp.int32, (slots, 128), 1) < HEAD_DIM
    factor = 1.0 / math.sqrt(HEAD_DIM)
    col = pl.multiple_of(pair * 128, 128)
    base = pl.multiple_of(r * slots, slots)
    zero = jnp.zeros((QB, 128), BF)
    grad_k = [None] * blocks
    grad_v = [None] * blocks
    for b in range(blocks):
        start, wide = window(b, blocks)
        q = qkv[pl.ds(base + b * QB, QB), pl.ds(col, 128)]
        k = qkv[pl.ds(base + start, wide), pl.ds(width + col, 128)]
        v = qkv[pl.ds(base + start, wide), pl.ds(2 * width + col, 128)]
        up = grad_mixed[pl.ds(base + b * QB, QB), pl.ds(col, 128)]
        out = mixed[pl.ds(base + b * QB, QB), pl.ds(col, 128)]
        probs = prob_slot[:, offsets[b] : offsets[b] + wide]
        q2 = jnp.concatenate([jnp.where(low, q, zero), jnp.where(low, zero, q)], axis=0)
        up2 = jnp.concatenate([jnp.where(low, up, zero), jnp.where(low, zero, up)], axis=0)
        out2 = jnp.concatenate([out, out], axis=0)
        inner = jnp.sum(up2.astype(F32) * out2.astype(F32), axis=-1, keepdims=True)
        grad_probs = mm_bt(up2, v)
        grad_scores = (probs.astype(F32) * (grad_probs - inner)).astype(BF)
        grad_q = mm(grad_scores, k) * factor
        grads[pl.ds(base + b * QB, QB), pl.ds(col, 128)] = jnp.where(low, grad_q[:QB], grad_q[QB:]).astype(BF)
        dk = mm_at(grad_scores, q2)
        dv = mm_at(probs, up2)
        for i in range(wide // QB):
            kb = start // QB + i
            piece_k, piece_v = dk[i * QB : (i + 1) * QB], dv[i * QB : (i + 1) * QB]
            grad_k[kb] = piece_k if grad_k[kb] is None else grad_k[kb] + piece_k
            grad_v[kb] = piece_v if grad_v[kb] is None else grad_v[kb] + piece_v
        done = [b - 1] if b > 0 else []
        if b == blocks - 1:
            done.append(b)
        for kb in done:
            grads[pl.ds(base + kb * QB, QB), pl.ds(width + col, 128)] = grad_k[kb].astype(BF)
            grads[pl.ds(base + kb * QB, QB), pl.ds(2 * width + col, 128)] = grad_v[kb].astype(BF)


def fold(values):
    return jnp.sum(values.reshape(values.shape[0] // 8, 8, values.shape[1]), axis=0)


def gelu_parts(values):
    cdf = 0.5 * (1.0 + lax.erf(values * math.sqrt(0.5)))
    pdf = jnp.exp(-0.5 * values * values) * (1.0 / math.sqrt(2.0 * math.pi))
    return values * cdf, cdf + values * pdf


def forward_phases(dims, refs):
    rows, slots, width, hidden = dims
    tokens = rows * slots
    tiles = tokens // TILE
    pairs = width // 128
    vec = refs["vec"]

    def row_of(i):
        return vec[i : i + 1, :].astype(F32)

    def norm_one():
        gain, shift = row_of(G1_ROW), row_of(B1_ROW)

        def body(i, _):
            at = pl.ds(pl.multiple_of(i * TILE, TILE), TILE)
            hat, _inv = norm_parts(refs["tok"][at, :])
            refs["n1"][at, :] = (hat * gain + shift).astype(BF)
            return 0

        lax.fori_loop(0, tiles, body, 0)

    def project():
        q_bias, v_bias = row_of(QB_ROW), row_of(VB_ROW)
        factor = 1.0 / math.sqrt(HEAD_DIM)

        def body(i, _):
            at = pl.ds(pl.multiple_of(i * TILE, TILE), TILE)
            normed = refs["n1"][at, :]
            query = (mm(normed, refs["wa"][:, :width]) + q_bias).astype(BF)
            refs["qkv"][at, :width] = (query.astype(F32) * factor).astype(BF)
            refs["qkv"][at, width : 2 * width] = mm(normed, refs["wa"][:, width : 2 * width]).astype(BF)
            refs["qkv"][at, 2 * width : 3 * width] = (
                mm(normed, refs["wa"][:, 2 * width : 3 * width]) + v_bias
            ).astype(BF)
            return 0

        lax.fori_loop(0, tiles, body, 0)

    def attend(first, last):
        def out_copy(step):
            slot = lax.rem(step, 2)
            return pltpu.make_async_copy(refs["slot"].at[slot], refs["prob_out"].at[step], refs["slot_sem"].at[slot])

        def body(step, _):
            @pl.when(step >= 2)
            def _():
                out_copy(step - 2).wait()

            attention_forward(
                rows, slots, pairs, width, refs["qkv"], refs["seg_col"], refs["seg_row"],
                refs["slot"].at[lax.rem(step, 2)], refs["mixed"], step // pairs, lax.rem(step, pairs),
            )
            out_copy(step).start()
            return 0

        lax.fori_loop(first, last, body, 0)
        if last == rows * pairs:
            out_copy(last - 2).wait()
            out_copy(last - 1).wait()

    def feed_forward():
        out_bias, scale_one = row_of(OB_ROW), row_of(SA_ROW)
        gain, shift = row_of(G2_ROW), row_of(B2_ROW)
        bias_two, scale_two = row_of(FB2_ROW), row_of(SF_ROW)
        parts = hidden // width
        refs["acc"][...] = jnp.zeros_like(refs["acc"])

        def body(i, _):
            at = pl.ds(pl.multiple_of(i * TILE, TILE), TILE)
            attn = mm(refs["mixed"][at, :], refs["wa"][:, 3 * width :]) + out_bias
            resid = refs["tok"][at, :] + scale_one * attn
            refs["resid"][at, :] = resid
            hat, _inv = norm_parts(resid)
            normed = (hat * gain + shift).astype(BF)
            refs["n2"][at, :] = normed
            for c in range(parts):
                cols = slice(c * width, (c + 1) * width)
                pre = mm(normed, refs["w1"][:, cols]) + row_of(FB1_ROW + c)
                act, slope = gelu_parts(pre)
                refs["act"][at, cols] = act.astype(BF)
                refs["slope"][at, cols] = slope.astype(BF)
            ffn = mm(refs["act"][at, :], refs["w2"][...]) + bias_two
            valid = lane_tile(refs["seg_col"][at, :], width // 128) < refs["pad"]
            up = jnp.where(valid, refs["cot"][at, :], 0.0)
            grad = (scale_two * up).astype(BF)
            refs["gffn"][at, :] = grad
            refs["acc"][0] += fold(up * ffn)
            refs["acc"][1] += fold(grad.astype(F32))
            refs["tok"][at, :] = resid + scale_two * ffn
            refs["tile_out"](i)
            return 0

        lax.fori_loop(0, tiles, body, 0)

    return norm_one, project, attend, feed_forward


def backward_phases(dims, refs):
    rows, slots, width, hidden = dims
    tokens = rows * slots
    tiles = tokens // TILE
    pairs = width // 128
    parts = hidden // width
    vec, acc = refs["vec"], refs["acc"]
    half = width // 2

    def row_of(i):
        return vec[i : i + 1, :].astype(F32)

    def weight_two():
        def body(i, _):
            at = pl.ds(pl.multiple_of(i * half, half), half)
            refs["d2"][at, :] = mm_at(refs["act"][:, at], refs["gffn"][...]).astype(BF)
            return 0

        lax.fori_loop(0, hidden // half, body, 0)

    def through_ffn():
        gain, scale_one = row_of(G2_ROW), row_of(SA_ROW)

        def body(i, _):
            at = pl.ds(pl.multiple_of(i * TILE, TILE), TILE)
            grad_ffn = refs["gffn"][at, :]
            for c in range(parts):
                cols = slice(c * width, (c + 1) * width)
                grad_act = mm_bt(grad_ffn, refs["w2"][cols, :])
                pre = (grad_act * refs["slope"][at, cols].astype(F32)).astype(BF)
                refs["slope"][at, cols] = pre
                acc[FB1_ROW + c] += fold(pre.astype(F32))
            grad = mm_bt(refs["slope"][at, :], refs["w1"][...])
            hat, inv = norm_parts(refs["resid"][at, :])
            acc[G2_ROW] += fold(grad * hat)
            acc[B2_ROW] += fold(grad)
            u = grad * gain
            back = inv * (u - jnp.mean(u, axis=-1, keepdims=True) - hat * jnp.mean(u * hat, axis=-1, keepdims=True))
            valid = lane_tile(refs["seg_col"][at, :], width // 128) < refs["pad"]
            grad_resid = jnp.where(valid, refs["cot"][at, :], 0.0) + back
            refs["resid"][at, :] = grad_resid
            grad_proj = (scale_one * grad_resid).astype(BF)
            refs["gproj"][at, :] = grad_proj
            acc[OB_ROW] += fold(grad_proj.astype(F32))
            refs["gmixed"][at, :] = mm_bt(grad_proj, refs["wa"][:, 3 * width :]).astype(BF)
            return 0

        lax.fori_loop(0, tiles, body, 0)

    def weight_one():
        def body(i, _):
            at = pl.ds(pl.multiple_of(i * half, half), half)
            for c in range(parts):
                cols = slice(c * width, (c + 1) * width)
                refs["d1"][at, cols] = mm_at(refs["n2"][:, at], refs["slope"][:, cols]).astype(BF)
            return 0

        lax.fori_loop(0, width // half, body, 0)

    def weight_out():
        def body(i, _):
            at = pl.ds(pl.multiple_of(i * half, half), half)
            grad = mm_at(refs["mixed"][:, at], refs["gproj"][...])
            refs["da"][at, 3 * width :] = grad.astype(BF)
            acc[SA_ROW] += fold(grad * refs["wa"][at, 3 * width :].astype(F32))
            return 0

        lax.fori_loop(0, width // half, body, 0)

    def attend_back(first, last):
        def in_copy(step):
            slot = lax.rem(step, 2)
            return pltpu.make_async_copy(refs["prob_in"].at[step], refs["slot"].at[slot], refs["slot_sem"].at[slot])

        if first == 0:
            in_copy(0).start()

        def body(step, _):
            @pl.when(step + 1 < rows * pairs)
            def _():
                in_copy(step + 1).start()

            in_copy(step).wait()
            attention_backward(
                rows, slots, pairs, width, refs["qkv"], refs["slot"].at[lax.rem(step, 2)], refs["mixed"],
                refs["gmixed"], refs["gqkv"], step // pairs, lax.rem(step, pairs),
            )
            return 0

        lax.fori_loop(first, last, body, 0)

    def weight_qkv():
        def body(i, _):
            at = pl.ds(pl.multiple_of(i * half, half), half)
            for c in range(3):
                cols = slice(c * width, (c + 1) * width)
                refs["da"][at, cols] = mm_at(refs["n1"][:, at], refs["gqkv"][:, cols]).astype(BF)
            return 0

        lax.fori_loop(0, width // half, body, 0)

    def finish_tokens():
        gain = row_of(G1_ROW)

        def body(i, _):
            at = pl.ds(pl.multiple_of(i * TILE, TILE), TILE)
            grad = mm_bt(refs["gqkv"][at, :], refs["wa"][:, : 3 * width])
            hat, inv = norm_parts(refs["tok"][at, :])
            acc[G1_ROW] += fold(grad * hat)
            acc[B1_ROW] += fold(grad)
            acc[QB_ROW] += fold(refs["gqkv"][at, :width].astype(F32))
            acc[VB_ROW] += fold(refs["gqkv"][at, 2 * width :].astype(F32))
            u = grad * gain
            back = inv * (u - jnp.mean(u, axis=-1, keepdims=True) - hat * jnp.mean(u * hat, axis=-1, keepdims=True))
            refs["tok"][at, :] = refs["resid"][at, :] + back
            refs["tile_out"](i)
            return 0

        lax.fori_loop(0, tiles, body, 0)

    def vector_sums():
        lines = [jnp.sum(acc[i], axis=0, keepdims=True) for i in range(VEC_ROWS)]
        lines[SA_ROW] = (lines[SA_ROW] + row_of(OB_ROW) * lines[OB_ROW]) / row_of(SA_ROW)
        return jnp.concatenate(lines, axis=0)

    return weight_two, through_ffn, weight_one, weight_out, attend_back, weight_qkv, finish_tokens, vector_sums


ANY = pl.BlockSpec(memory_space=pl.ANY)
INSIDE = pl.BlockSpec(memory_space=pltpu.VMEM)
SCALARS = pl.BlockSpec(memory_space=pltpu.SMEM)


def forward_kernel(dims, pad, *all_refs):
    rows, slots, width, hidden = dims
    tokens = rows * slots
    tiles = tokens // TILE
    (
        lengths, vec, tok_in, cot_in, wa_in, w1_in, w2_in,
        out, n1_out, qkv_out, prob_out, mixed_out, resid_out, n2_out, act_out, slope_out, gffn_out, acc,
        tok, cot, wa, w1, w2, n1, qkv, slot, mixed, resid, n2, act, slope, gffn, seg_col, seg_row,
        slot_sem, in_sem, out_sem, tile_sem,
    ) = all_refs
    loads = [
        pltpu.make_async_copy(a, b, in_sem.at[i])
        for i, (a, b) in enumerate([(tok_in, tok), (wa_in, wa), (cot_in, cot), (w1_in, w1), (w2_in, w2)])
    ]
    for copy in loads:
        copy.start()

    def tile_copies(i):
        at = pl.ds(pl.multiple_of(i * TILE, TILE), TILE)
        return [
            pltpu.make_async_copy(a.at[at], b.at[at], tile_sem.at[i, j])
            for j, (a, b) in enumerate(
                [(tok, out), (resid, resid_out), (n2, n2_out), (act, act_out), (slope, slope_out), (gffn, gffn_out)]
            )
        ]

    def tile_out(i):
        for copy in tile_copies(i):
            copy.start()

    refs = dict(
        vec=vec, tok=tok, cot=cot, wa=wa, w1=w1, w2=w2, n1=n1, qkv=qkv, slot=slot, mixed=mixed, resid=resid, n2=n2,
        act=act, slope=slope, gffn=gffn, seg_col=seg_col, seg_row=seg_row, slot_sem=slot_sem, prob_out=prob_out,
        acc=acc, pad=pad, tile_out=tile_out,
    )
    norm_one, project, attend, feed_forward = forward_phases(dims, refs)
    fill_segments(lengths, rows, slots, seg_col, seg_row)
    loads[0].wait()
    norm_one()
    stores = [
        pltpu.make_async_copy(a, b, out_sem.at[i])
        for i, (a, b) in enumerate([(n1, n1_out), (qkv, qkv_out), (mixed, mixed_out)])
    ]
    stores[0].start()
    loads[1].wait()
    project()
    stores[1].start()
    attend(0, rows * (width // 128))
    stores[2].start()
    for copy in loads[2:]:
        copy.wait()
    feed_forward()
    for copy in stores:
        copy.wait()

    def finish(i, _):
        for copy in tile_copies(i):
            copy.wait()
        return 0

    lax.fori_loop(0, tiles, finish, 0)


def forward_call(dims, pad):
    rows, slots, width, hidden = dims
    tokens = rows * slots
    tiles, pairs = tokens // TILE, width // 128
    wide = prob_offsets(slots // QB)[1]
    S = jax.ShapeDtypeStruct
    shapes = [
        S((tokens, width), F32), S((tokens, width), BF), S((tokens, 3 * width), BF),
        S((rows * pairs, 2 * QB, wide), BF), S((tokens, width), BF), S((tokens, width), F32), S((tokens, width), BF),
        S((tokens, hidden), BF), S((tokens, hidden), BF), S((tokens, width), BF), S((2, 8, width), F32),
    ]
    V = pltpu.VMEM
    scratch = [
        V((tokens, width), F32), V((tokens, width), F32), V((width, 4 * width), BF), V((width, hidden), BF),
        V((hidden, width), BF), V((tokens, width), BF), V((tokens, 3 * width), BF), V((2, 2 * QB, wide), BF),
        V((tokens, width), BF), V((tokens, width), F32), V((tokens, width), BF), V((tokens, hidden), BF),
        V((tokens, hidden), BF), V((tokens, width), BF), V((tokens, 128), jnp.int32), V((rows, 8, slots), jnp.int32),
        pltpu.SemaphoreType.DMA((2,)), pltpu.SemaphoreType.DMA((5,)), pltpu.SemaphoreType.DMA((3,)),
        pltpu.SemaphoreType.DMA((tiles, 6)),
    ]
    return pl.pallas_call(
        functools.partial(forward_kernel, dims, pad),
        out_shape=shapes,
        in_specs=[SCALARS, INSIDE] + [ANY] * 5,
        out_specs=[ANY] * 10 + [INSIDE],
        scratch_shapes=scratch,
        compiler_params=pltpu.CompilerParams(vmem_limit_bytes=VMEM_LIMIT),
        name="forward",
    )


def backward_kernel(dims, pad, *all_refs):
    rows, slots, width, hidden = dims
    tokens = rows * slots
    tiles, pairs = tokens // TILE, width // 128
    (
        lengths, vec, acc_in, tok_in, cot_in, wa_in, w1_in, w2_in,
        n1_in, qkv_in, prob_in, mixed_in, resid_in, n2_in, act_in, slope_in, gffn_in,
        gtok_out, da_out, d1_out, d2_out, sums,
        tok, cot, wa, w1, w2, n1, qkv, slot, mixed, resid, n2, act, slope, gffn, gproj, gmixed, d2, acc,
        seg_col, seg_row, slot_sem, in_sem, out_sem, tile_sem,
    ) = all_refs
    d1 = act.at[:width]
    da = w1
    pairs_in = [
        (act_in, act), (gffn_in, gffn), (w2_in, w2), (slope_in, slope), (w1_in, w1), (resid_in, resid), (cot_in, cot),
        (wa_in, wa), (n2_in, n2), (mixed_in, mixed), (qkv_in, qkv), (n1_in, n1), (tok_in, tok),
    ]
    loads = [pltpu.make_async_copy(a, b, in_sem.at[i]) for i, (a, b) in enumerate(pairs_in)]
    for copy in loads:
        copy.start()

    def tile_copy(i):
        at = pl.ds(pl.multiple_of(i * TILE, TILE), TILE)
        return pltpu.make_async_copy(tok.at[at], gtok_out.at[at], tile_sem.at[i])

    refs = dict(
        vec=vec, acc=acc, tok=tok, cot=cot, wa=wa, w1=w1, w2=w2, n1=n1, qkv=qkv, gqkv=qkv, slot=slot, mixed=mixed,
        resid=resid, n2=n2, act=act, slope=slope, gffn=gffn, gproj=gproj, gmixed=gmixed, d2=d2, d1=d1, da=da,
        seg_col=seg_col, seg_row=seg_row, slot_sem=slot_sem, prob_in=prob_in, pad=pad,
        tile_out=lambda i: tile_copy(i).start(),
    )
    (
        weight_two, through_ffn, weight_one, weight_out, attend_back, weight_qkv, finish_tokens, vector_sums,
    ) = backward_phases(dims, refs)
    fill_segments(lengths, rows, slots, seg_col, seg_row)
    acc[...] = jnp.zeros_like(acc)
    acc[SF_ROW] = acc_in[0]
    acc[FB2_ROW] = acc_in[1]
    for copy in loads[:2]:
        copy.wait()
    weight_two()
    stores = [
        pltpu.make_async_copy(a, b, out_sem.at[i]) for i, (a, b) in enumerate([(d2, d2_out), (d1, d1_out), (da, da_out)])
    ]
    stores[0].start()
    for copy in loads[2:8]:
        copy.wait()
    through_ffn()
    loads[8].wait()
    weight_one()
    stores[1].start()
    loads[9].wait()
    weight_out()
    loads[10].wait()
    attend_back(0, rows * pairs)
    loads[11].wait()
    weight_qkv()
    stores[2].start()
    loads[12].wait()
    finish_tokens()
    sums[...] = vector_sums()
    for copy in stores:
        copy.wait()

    def finish(i, _):
        tile_copy(i).wait()
        return 0

    lax.fori_loop(0, tiles, finish, 0)


def backward_call(dims, pad):
    rows, slots, width, hidden = dims
    tokens = rows * slots
    tiles, pairs = tokens // TILE, width // 128
    wide = prob_offsets(slots // QB)[1]
    S = jax.ShapeDtypeStruct
    shapes = [
        S((tokens, width), F32), S((width, 4 * width), BF), S((width, hidden), BF), S((hidden, width), BF),
        S((VEC_ROWS, width), F32),
    ]
    V = pltpu.VMEM
    tall = lambda dtype: V((tokens, width), dtype)
    scratch = [
        tall(F32), tall(F32), V((width, 4 * width), BF), V((width, hidden), BF), V((hidden, width), BF), tall(BF),
        V((tokens, 3 * width), BF), V((2, 2 * QB, wide), BF), tall(BF), tall(F32), tall(BF), V((tokens, hidden), BF),
        V((tokens, hidden), BF), tall(BF), tall(BF), tall(BF), V((hidden, width), BF), V((VEC_ROWS, 8, width), F32),
        V((tokens, 128), jnp.int32), V((rows, 8, slots), jnp.int32),
        pltpu.SemaphoreType.DMA((2,)), pltpu.SemaphoreType.DMA((13,)), pltpu.SemaphoreType.DMA((3,)),
        pltpu.SemaphoreType.DMA((tiles,)),
    ]
    return pl.pallas_call(
        functools.partial(backward_kernel, dims, pad),
        out_shape=shapes,
        in_specs=[SCALARS, INSIDE, INSIDE] + [ANY] * 14,
        out_specs=[ANY] * 4 + [INSIDE],
        scratch_shapes=scratch,
        compiler_params=pltpu.CompilerParams(vmem_limit_bytes=VMEM_LIMIT),
        name="backward",
    )


def local(
    fsdp, dp,
    tokens, lengths, cotangent, ln1_gain, ln1_bias, w_qkv, qkv_bias, w_out, out_bias, scale_attn, ln2_gain, ln2_bias,
    w_fc1, fc1_bias, w_fc2, fc2_bias, scale_ffn,
):
    rows = lengths.shape[0]
    slots, width = tokens.shape[0] // rows, tokens.shape[1]
    hidden = w_fc1.shape[1]
    dims = (rows, slots, width, hidden)
    pad = lengths.shape[1] - 1
    me = lax.axis_index("fsdp")
    lines = [
        ln1_gain, ln1_bias, qkv_bias[:, 0], qkv_bias[:, 1], out_bias, scale_attn, ln2_gain, ln2_bias, fc2_bias, scale_ffn,
    ]
    own = jnp.stack(lines, axis=0)
    vec = lax.all_gather(own, "fsdp", axis=1, tiled=True)
    bias_one = lax.all_gather(fc1_bias, "fsdp", axis=0, tiled=True).reshape(-1, width)
    vec = jnp.concatenate([vec, bias_one], axis=0)
    vec = jnp.concatenate([vec, jnp.zeros((VEC_ROWS - vec.shape[0], width), BF)], axis=0)
    full_a = lax.all_gather(jnp.concatenate([w_qkv, w_out], axis=1), "fsdp", axis=0, tiled=True)
    full_1 = lax.all_gather(w_fc1, "fsdp", axis=0, tiled=True)
    full_2 = lax.all_gather(w_fc2, "fsdp", axis=0, tiled=True)
    out, n1, qkv, prob, mixed, resid, n2, act, slope, gffn, acc = forward_call(dims, pad)(
        lengths, vec, tokens, cotangent, full_a, full_1, full_2
    )
    grad_tokens, da, d1, d2, sums = backward_call(dims, pad)(
        lengths, vec, acc, tokens, cotangent, full_a, full_1, full_2, n1, qkv, prob, mixed, resid, n2, act, slope, gffn
    )

    def total(array):
        part = lax.psum_scatter(array, "fsdp", scatter_dimension=0, tiled=True)
        return lax.psum(part, "dp").astype(F32)

    sum_a, sum_1, sum_2 = total(da), total(d1), total(d2)
    sums = lax.psum(sums, ("fsdp", "dp"))
    return finish_outputs(fsdp, dims, me, out, grad_tokens, sum_a, sum_1, sum_2, sums)


def finish_outputs(fsdp, dims, me, out, grad_tokens, sum_a, sum_1, sum_2, sums):
    rows, slots, width, hidden = dims
    piece = width // fsdp
    mine = lax.dynamic_slice(sums, (0, me * piece), (FB1_ROW, piece))
    bias_one = lax.dynamic_slice(sums[FB1_ROW : FB1_ROW + hidden // width].reshape(-1), (me * (hidden // fsdp),), (hidden // fsdp,))
    return (
        out, grad_tokens, mine[G1_ROW], mine[B1_ROW], sum_a[:, : 3 * width],
        jnp.stack([mine[QB_ROW], mine[VB_ROW]], axis=1), sum_a[:, 3 * width :], mine[OB_ROW], mine[SA_ROW],
        mine[G2_ROW], mine[B2_ROW], sum_1, bias_one, sum_2, mine[FB2_ROW], mine[SF_ROW],
    )


def solution(mesh):
    both, one, two = P(("fsdp", "dp"), None), P("fsdp"), P("fsdp", None)
    in_specs = (both, both, both, one, one, two, two, two, one, one, one, one, two, one, two, one, one)
    out_specs = (both, both, one, one, two, two, two, one, one, one, one, two, one, two, one, one)
    run = functools.partial(local, mesh.shape["fsdp"], mesh.shape["dp"])
    return jax.shard_map(run, mesh=mesh, in_specs=in_specs, out_specs=out_specs, check_vma=False)
```

```python
import functools
import math

import jax
import jax.numpy as jnp
from jax import lax
from jax.experimental import pallas as pl
from jax.experimental.pallas import tpu as pltpu
from jax.sharding import PartitionSpec as P

HEAD_DIM = 64
norm_eps = 1e-06
masked_score = -1e30
BF = jnp.bfloat16
F32 = jnp.float32
TILE = 256
QB = 128
VMEM_LIMIT = 67043328

MESH = pl.DeviceIdType.MESH
SHARED = 64

G1_ROW, B1_ROW, QB_ROW, VB_ROW, OB_ROW, SA_ROW, G2_ROW, B2_ROW, FB2_ROW, SF_ROW, FB1_ROW = range(11)
VEC_ROWS = 16


def mm(a, b):
    return lax.dot_general(a, b, (((1,), (0,)), ((), ())), preferred_element_type=F32)


def mm_bt(a, b):
    return lax.dot_general(a, b, (((1,), (1,)), ((), ())), preferred_element_type=F32)


def mm_at(a, b):
    return lax.dot_general(a, b, (((0,), (0,)), ((), ())), preferred_element_type=F32)


def norm_parts(values):
    centered = values - jnp.mean(values, axis=-1, keepdims=True)
    spread = jnp.mean(centered * centered, axis=-1, keepdims=True)
    inv = lax.rsqrt(spread + norm_eps)
    return centered * inv, inv


def window(block, blocks):
    first = max(block - 1, 0)
    last = min(block + 2, blocks)
    return first * QB, (last - first) * QB


def prob_offsets(blocks):
    offsets, total = [], 0
    for block in range(blocks):
        offsets.append(total)
        total += window(block, blocks)[1]
    return offsets, total


def lane_tile(values, times):
    return jnp.concatenate([values] * times, axis=1) if times > 1 else values


def fill_segments(lengths_ref, rows, slots, seg_col, seg_row):
    count = lengths_ref.shape[1]
    for r in range(rows):
        down = lax.broadcasted_iota(jnp.int32, (slots, 128), 0)
        along = lax.broadcasted_iota(jnp.int32, (8, slots), 1)
        col = jnp.zeros((slots, 128), jnp.int32)
        row = jnp.zeros((8, slots), jnp.int32)
        end = jnp.int32(0)
        for j in range(count):
            end = end + lengths_ref[r, j]
            col = col + (down >= end).astype(jnp.int32)
            row = row + (along >= end).astype(jnp.int32)
        seg_col[pl.ds(r * slots, slots), :] = col
        seg_row[r] = row


def attention_forward(rows, slots, pairs, width, qkv, seg_col, seg_row, prob_slot, mixed, r, pair):
    blocks = slots // QB
    offsets, _ = prob_offsets(blocks)
    low = lax.broadcasted_iota(jnp.int32, (QB, 128), 1) < HEAD_DIM
    col = pl.multiple_of(pair * 128, 128)
    base = pl.multiple_of(r * slots, slots)
    zero = jnp.zeros((QB, 128), BF)
    for b in range(blocks):
        start, wide = window(b, blocks)
        q = qkv[pl.ds(base + b * QB, QB), pl.ds(col, 128)]
        k = qkv[pl.ds(base + start, wide), pl.ds(width + col, 128)]
        v = qkv[pl.ds(base + start, wide), pl.ds(2 * width + col, 128)]
        same = lane_tile(seg_col[pl.ds(base + b * QB, QB), :], wide // 128) == seg_row[r, 0:1, start : start + wide]
        q2 = jnp.concatenate([jnp.where(low, q, zero), jnp.where(low, zero, q)], axis=0)
        scores = mm_bt(q2, k)
        scores = jnp.concatenate(
            [jnp.where(same, scores[:QB], masked_score), jnp.where(same, scores[QB:], masked_score)], axis=0
        )
        peak = jnp.max(scores, axis=-1, keepdims=True)
        weights = jnp.exp(scores - peak)
        total = jnp.sum(weights, axis=-1, keepdims=True)
        probs = (weights * (1.0 / total)).astype(BF)
        prob_slot[:, offsets[b] : offsets[b] + wide] = probs
        out = mm(probs, v)
        mixed[pl.ds(base + b * QB, QB), pl.ds(col, 128)] = jnp.where(low, out[:QB], out[QB:]).astype(BF)


def attention_backward(rows, slots, pairs, width, qkv, prob_slot, mixed, grad_mixed, grads, r, pair):
    blocks = slots // QB
    offsets, _ = prob_offsets(blocks)
    low = lax.broadcasted_iota(jnp.int32, (QB, 128), 1) < HEAD_DIM
    low_all = lax.broadcasted_iota(jnp.int32, (slots, 128), 1) < HEAD_DIM
    factor = 1.0 / math.sqrt(HEAD_DIM)
    col = pl.multiple_of(pair * 128, 128)
    base = pl.multiple_of(r * slots, slots)
    zero = jnp.zeros((QB, 128), BF)
    grad_k = [None] * blocks
    grad_v = [None] * blocks
    for b in range(blocks):
        start, wide = window(b, blocks)
        q = qkv[pl.ds(base + b * QB, QB), pl.ds(col, 128)]
        k = qkv[pl.ds(base + start, wide), pl.ds(width + col, 128)]
        v = qkv[pl.ds(base + start, wide), pl.ds(2 * width + col, 128)]
        up = grad_mixed[pl.ds(base + b * QB, QB), pl.ds(col, 128)]
        out = mixed[pl.ds(base + b * QB, QB), pl.ds(col, 128)]
        probs = prob_slot[:, offsets[b] : offsets[b] + wide]
        q2 = jnp.concatenate([jnp.where(low, q, zero), jnp.where(low, zero, q)], axis=0)
        up2 = jnp.concatenate([jnp.where(low, up, zero), jnp.where(low, zero, up)], axis=0)
        out2 = jnp.concatenate([out, out], axis=0)
        inner = jnp.sum(up2.astype(F32) * out2.astype(F32), axis=-1, keepdims=True)
        grad_probs = mm_bt(up2, v)
        grad_scores = (probs.astype(F32) * (grad_probs - inner)).astype(BF)
        grad_q = mm(grad_scores, k) * factor
        grads[pl.ds(base + b * QB, QB), pl.ds(col, 128)] = jnp.where(low, grad_q[:QB], grad_q[QB:]).astype(BF)
        dk = mm_at(grad_scores, q2)
        dv = mm_at(probs, up2)
        for i in range(wide // QB):
            kb = start // QB + i
            piece_k, piece_v = dk[i * QB : (i + 1) * QB], dv[i * QB : (i + 1) * QB]
            grad_k[kb] = piece_k if grad_k[kb] is None else grad_k[kb] + piece_k
            grad_v[kb] = piece_v if grad_v[kb] is None else grad_v[kb] + piece_v
        done = [b - 1] if b > 0 else []
        if b == blocks - 1:
            done.append(b)
        for kb in done:
            grads[pl.ds(base + kb * QB, QB), pl.ds(width + col, 128)] = grad_k[kb].astype(BF)
            grads[pl.ds(base + kb * QB, QB), pl.ds(2 * width + col, 128)] = grad_v[kb].astype(BF)


def fold(values):
    return jnp.sum(values.reshape(values.shape[0] // 8, 8, values.shape[1]), axis=0)


def gelu_parts(values):
    cdf = 0.5 * (1.0 + lax.erf(values * math.sqrt(0.5)))
    pdf = jnp.exp(-0.5 * values * values) * (1.0 / math.sqrt(2.0 * math.pi))
    return values * cdf, cdf + values * pdf


def block(ref, c):
    value = ref[c // 2, c % 2]
    return value.reshape(-1, value.shape[-1])


def hidden_rows(ref, z):
    return jnp.concatenate([ref[x, c, z, y] for y in range(2) for x in range(2) for c in range(2)], axis=0)


def run_hooks(hooks, step):
    for k, turns in sorted(hooks.items()):

        @pl.when(step == k)
        def _(turns=turns):
            for turn in turns:
                turn()


def forward_phases(dims, refs):
    rows, slots, width, hidden = dims
    tokens = rows * slots
    tiles = tokens // TILE
    pairs = width // 128
    vec = refs["vec"]

    def row_of(i):
        return vec[i : i + 1, :].astype(F32)

    def norm_one():
        gain, shift = row_of(G1_ROW), row_of(B1_ROW)

        def body(i, _):
            at = pl.ds(pl.multiple_of(i * TILE, TILE), TILE)
            hat, _inv = norm_parts(refs["tok"][at, :])
            refs["n1"][at, :] = (hat * gain + shift).astype(BF)
            return 0

        lax.fori_loop(0, tiles, body, 0)

    def project():
        q_bias, v_bias = row_of(QB_ROW), row_of(VB_ROW)
        factor = 1.0 / math.sqrt(HEAD_DIM)

        def body(i, _):
            at = pl.ds(pl.multiple_of(i * TILE, TILE), TILE)
            normed = refs["n1"][at, :]
            query = (mm(normed, block(refs["wa"], 0)) + q_bias).astype(BF)
            refs["qkv"][at, :width] = (query.astype(F32) * factor).astype(BF)
            refs["qkv"][at, width : 2 * width] = mm(normed, block(refs["wa"], 1)).astype(BF)
            refs["qkv"][at, 2 * width : 3 * width] = (
                mm(normed, block(refs["wa"], 2)) + v_bias
            ).astype(BF)
            return 0

        lax.fori_loop(0, tiles, body, 0)

    def attend(hooks):
        steps = rows * pairs

        def out_copy(step):
            slot = lax.rem(step, 2)
            return pltpu.make_async_copy(refs["slot"].at[slot], refs["prob_out"].at[step], refs["slot_sem"].at[slot])

        def body(step, _):
            @pl.when(step >= 2)
            def _():
                out_copy(step - 2).wait()

            attention_forward(
                rows, slots, pairs, width, refs["qkv"], refs["seg_col"], refs["seg_row"],
                refs["slot"].at[lax.rem(step, 2)], refs["mixed"], lax.rem(step, rows), lax.div(step, rows),
            )
            out_copy(step).start()
            run_hooks(hooks, step)
            return 0

        lax.fori_loop(0, steps, body, 0)
        out_copy(steps - 2).wait()
        out_copy(steps - 1).wait()

    def feed_one(hooks):
        out_bias, scale_one = row_of(OB_ROW), row_of(SA_ROW)
        gain, shift = row_of(G2_ROW), row_of(B2_ROW)

        def body(i, _):
            at = pl.ds(pl.multiple_of(i * TILE, TILE), TILE)
            attn = mm(refs["mixed"][at, :], block(refs["wa"], 3)) + out_bias
            resid = refs["tok"][at, :] + scale_one * attn
            refs["resid"][at, :] = resid
            hat, _inv = norm_parts(resid)
            normed = (hat * gain + shift).astype(BF)
            refs["n2"][at, :] = normed
            for c in range(hidden // width):
                cols = slice(c * width, (c + 1) * width)
                pre = mm(normed, block(refs["w1"], c)) + row_of(FB1_ROW + c)
                act, slope = gelu_parts(pre)
                refs["act"][at, cols] = act.astype(BF)
                refs["slope"][at, cols] = slope.astype(BF)
            refs["tile_one"](i)
            run_hooks(hooks, i)
            return 0

        lax.fori_loop(0, tiles, body, 0)

    def feed_two():
        bias_two, scale_two = row_of(FB2_ROW), row_of(SF_ROW)
        refs["acc"][...] = jnp.zeros_like(refs["acc"])

        def body(i, _):
            at = pl.ds(pl.multiple_of(i * TILE, TILE), TILE)
            ffn = mm(refs["act"][at, :], jnp.concatenate([hidden_rows(refs["w2"], z) for z in range(4)], axis=0)) + bias_two
            valid = lane_tile(refs["seg_col"][at, :], width // 128) < refs["pad"]
            up = jnp.where(valid, refs["cot"][at, :], 0.0)
            grad = (scale_two * up).astype(BF)
            refs["gffn"][at, :] = grad
            refs["acc"][0] += fold(up * ffn)
            refs["acc"][1] += fold(grad.astype(F32))
            refs["tok"][at, :] = refs["resid"][at, :] + scale_two * ffn
            refs["tile_two"](i)
            return 0

        lax.fori_loop(0, tiles, body, 0)

    return norm_one, project, attend, feed_one, feed_two


def backward_phases(dims, refs):
    rows, slots, width, hidden = dims
    tokens = rows * slots
    tiles = tokens // TILE
    pairs = width // 128
    parts = hidden // width
    vec, acc = refs["vec"], refs["acc"]
    half = width // 2
    piece = width // 8

    def row_of(i):
        return vec[i : i + 1, :].astype(F32)

    def weight_two():
        per = hidden // 8

        def body(i, _):
            at = pl.ds(pl.multiple_of(i * per, per), per)
            grad = mm_at(refs["act"][:, at], refs["gffn"][...]).astype(BF)
            refs["d2"][:, :, lax.div(i, 2), lax.rem(i, 2)] = grad.reshape(2, 2, per // 4, width)
            return 0

        lax.fori_loop(0, 8, body, 0)

    def through_ffn(hooks):
        gain, scale_one = row_of(G2_ROW), row_of(SA_ROW)

        def body(i, _):
            at = pl.ds(pl.multiple_of(i * TILE, TILE), TILE)
            grad_ffn = refs["gffn"][at, :]
            for c in range(parts):
                cols = slice(c * width, (c + 1) * width)
                grad_act = mm_bt(grad_ffn, hidden_rows(refs["w2"], c))
                pre = (grad_act * refs["slope"][at, cols].astype(F32)).astype(BF)
                refs["slope"][at, cols] = pre
                acc[FB1_ROW + c] += fold(pre.astype(F32))
            grad = mm_bt(refs["slope"][at, :], jnp.concatenate([block(refs["w1"], c) for c in range(parts)], axis=1))
            hat, inv = norm_parts(refs["resid"][at, :])
            acc[G2_ROW] += fold(grad * hat)
            acc[B2_ROW] += fold(grad)
            u = grad * gain
            back = inv * (u - jnp.mean(u, axis=-1, keepdims=True) - hat * jnp.mean(u * hat, axis=-1, keepdims=True))
            valid = lane_tile(refs["seg_col"][at, :], width // 128) < refs["pad"]
            grad_resid = jnp.where(valid, refs["cot"][at, :], 0.0) + back
            refs["resid"][at, :] = grad_resid
            grad_proj = (scale_one * grad_resid).astype(BF)
            refs["gproj"][at, :] = grad_proj
            acc[OB_ROW] += fold(grad_proj.astype(F32))
            refs["gmixed"][at, :] = mm_bt(grad_proj, block(refs["wa"], 3)).astype(BF)
            run_hooks(hooks, i)
            return 0

        lax.fori_loop(0, tiles, body, 0)

    def weight_one():
        def body(i, _):
            at = pl.ds(pl.multiple_of(i * half, half), half)
            for c in range(parts):
                cols = slice(c * width, (c + 1) * width)
                grad = mm_at(refs["n2"][:, at], refs["slope"][:, cols]).astype(BF)
                refs["d1"][c // 2, c % 2, pl.ds(i * 2, 2)] = grad.reshape(2, 2, piece, width)
            return 0

        lax.fori_loop(0, 2, body, 0)

    def weight_out():
        def body(i, _):
            at = pl.ds(pl.multiple_of(i * half, half), half)
            grad = mm_at(refs["mixed"][:, at], refs["gproj"][...])
            low = grad.astype(BF)
            for j in range(2):
                refs["da0"][1, j, pl.ds(i * 2, 2)] = low[:, j * half : (j + 1) * half].reshape(2, 2, piece, half)
            w_out = refs["wa"][1, 1, pl.ds(i * 2, 2)].reshape(half, width)
            acc[SA_ROW] += fold(grad * w_out.astype(F32))
            return 0

        lax.fori_loop(0, 2, body, 0)

    def attend_back(first, last, hooks):
        def in_copy(step):
            slot = lax.rem(step, 2)
            return pltpu.make_async_copy(refs["prob_in"].at[step], refs["slot"].at[slot], refs["slot_sem"].at[slot])

        if first == 0:
            in_copy(0).start()

        def body(step, _):
            @pl.when(step + 1 < rows * pairs)
            def _():
                in_copy(step + 1).start()

            in_copy(step).wait()
            attention_backward(
                rows, slots, pairs, width, refs["qkv"], refs["slot"].at[lax.rem(step, 2)], refs["mixed"],
                refs["gmixed"], refs["qkv"], lax.rem(step, rows), lax.div(step, rows),
            )
            run_hooks(hooks, step)
            return 0

        lax.fori_loop(first, last, body, 0)

    def weight_pairs(target, first, count):
        def body(i, _):
            at = pl.ds(pl.multiple_of(i * half, half), half)
            slabs = [
                refs["qkv"][:, part * width + p * 128 : part * width + (p + 1) * 128]
                for p in range(first, first + count)
                for part in range(3)
            ]
            grad = mm_at(refs["n1"][:, at], jnp.concatenate(slabs, axis=1)).astype(BF)
            for j in range(count):
                target[j // 2, j % 2, pl.ds(i * 2, 2)] = grad[:, j * 384 : (j + 1) * 384].reshape(2, 2, piece, 384)
            return 0

        lax.fori_loop(0, 2, body, 0)

    def finish_tokens(hooks):
        gain = row_of(G1_ROW)

        def body(i, _):
            at = pl.ds(pl.multiple_of(i * TILE, TILE), TILE)
            grad = mm_bt(refs["qkv"][at, :], jnp.concatenate([block(refs["wa"], c) for c in range(3)], axis=1))
            hat, inv = norm_parts(refs["tok"][at, :])
            acc[G1_ROW] += fold(grad * hat)
            acc[B1_ROW] += fold(grad)
            acc[QB_ROW] += fold(refs["qkv"][at, :width].astype(F32))
            acc[VB_ROW] += fold(refs["qkv"][at, 2 * width :].astype(F32))
            u = grad * gain
            back = inv * (u - jnp.mean(u, axis=-1, keepdims=True) - hat * jnp.mean(u * hat, axis=-1, keepdims=True))
            refs["tok"][at, :] = refs["resid"][at, :] + back
            refs["tile_out"](i)
            run_hooks(hooks, i)
            return 0

        lax.fori_loop(0, tiles, body, 0)

    def vector_sums():
        lines = [jnp.sum(acc[i], axis=0, keepdims=True) for i in range(VEC_ROWS)]
        lines[SA_ROW] = (lines[SA_ROW] + row_of(OB_ROW) * lines[OB_ROW]) / row_of(SA_ROW)
        return jnp.concatenate(lines, axis=0)

    return weight_two, through_ffn, weight_one, weight_out, attend_back, weight_pairs, finish_tokens, vector_sums


ANY = pl.BlockSpec(memory_space=pl.ANY)
INSIDE = pl.BlockSpec(memory_space=pltpu.VMEM)
SCALARS = pl.BlockSpec(memory_space=pltpu.SMEM)
DMA = pltpu.SemaphoreType.DMA


def position():
    f, d = lax.axis_index("fsdp"), lax.axis_index("dp")
    return lax.div(f, 2), lax.rem(f, 2), lax.div(d, 2), lax.rem(d, 2)


def device(z, y, x, c):
    return (z * 2 + y, x * 2 + c)


def z_partners(z):
    return [z + 1 - 2 * lax.rem(z, 2), 3 - z, lax.rem(z + 2, 4)]


def remote(src, dst, send, recv, target):
    return pltpu.make_async_remote_copy(
        src_ref=src, dst_ref=dst, send_sem=send, recv_sem=recv, device_id=target, device_id_type=MESH
    )


def greet(targets):
    barrier = pltpu.get_barrier_semaphore()
    for target in targets:
        pl.semaphore_signal(barrier, inc=1, device_id=target, device_id_type=MESH)
    pl.semaphore_wait(barrier, len(targets))


class Gather:
    def __init__(self, t, buf, sems, place):
        self.t, self.buf, self.place = t, buf, place
        self.zs, self.zr, self.ys, self.yr, self.xs, self.xr, self.cs, self.cr = sems

    def shard(self, j):
        z, y, _, _ = self.place
        others = z_partners(z)
        if j == 7:
            return z, y
        if j < 3:
            return others[j], y
        return (z if j == 3 else others[j - 4]), 1 - y

    def parts(self, z, y):
        _, _, x, c = self.place
        rows = self.buf.shape[4]
        found = [self.buf.at[x, c, z, y, pl.ds(0, SHARED)]]
        if SHARED < rows:
            found.append(self.buf.at[:, c, z, y, pl.ds(SHARED, rows - SHARED)])
        return found

    def z_sends(self, k):
        z, y, x, c = self.place
        target = device(z_partners(z)[k], y, x, c)
        return [
            remote(ref, ref, self.zs.at[self.t, k, p], self.zr.at[self.t, z, p], target)
            for p, ref in enumerate(self.parts(z, y))
        ]

    def z_receives(self, k):
        z, y, x, c = self.place
        other = z_partners(z)[k]
        return [
            remote(ref, ref, self.zs.at[self.t, k, p], self.zr.at[self.t, other, p], device(other, y, x, c))
            for p, ref in enumerate(self.parts(other, y))
        ]

    def y_copies(self, zs, ys):
        z, y, x, c = self.place
        return [
            remote(ref, ref, self.ys.at[self.t, zs, p], self.yr.at[self.t, zs, p], device(z, 1 - y, x, c))
            for p, ref in enumerate(self.parts(zs, ys))
        ]

    def x_copy(self, j, qx):
        z, y, x, c = self.place
        zs, ys = self.shard(j)
        s = zs * 2 + ys
        ref = self.buf.at[qx, c, zs, ys, pl.ds(0, SHARED)]
        return remote(ref, ref, self.xs.at[self.t, s], self.xr.at[self.t, s], device(z, y, 1 - x, c))

    def c_copy(self, j, qx, qc):
        z, y, x, c = self.place
        zs, ys = self.shard(j)
        s = zs * 2 + ys
        ref = self.buf.at[qx, qc, zs, ys]
        return remote(ref, ref, self.cs.at[self.t, s, qx], self.cr.at[self.t, s, qx], device(z, y, x, 1 - c))

    def send_y(self, j):
        for copy in self.y_copies(*self.shard(j)):
            copy.start()

    def onward(self, j):
        _, _, x, c = self.place
        self.x_copy(j, x).start()
        self.c_copy(j, x, c).start()

    def start(self):
        for k in range(3):
            for copy in self.z_sends(k):
                copy.start()
        self.send_y(7)

    def z_step(self, k):
        for copy in self.z_receives(k):
            copy.wait_recv()
        self.send_y(k)
        self.onward(k)

    def y_step(self, k):
        for copy in self.y_copies(*self.shard(3 + k)):
            copy.wait_recv()
        self.onward(3 + k)

    def x_step(self, j):
        _, _, x, c = self.place
        self.x_copy(j, 1 - x).wait_recv()
        self.c_copy(j, 1 - x, c).start()

    def done(self):
        _, _, x, c = self.place
        for j in range(7):
            for qx in (x, 1 - x):
                self.c_copy(j, qx, 1 - c).wait_recv()

    def finish(self):
        _, _, x, c = self.place
        for k in range(3):
            for copy in self.z_sends(k):
                copy.wait_send()
        for j in (7, 0, 1, 2):
            for copy in self.y_copies(*self.shard(j)):
                copy.wait_send()
        for j in range(7):
            self.x_copy(j, x).wait_send()
            for qx in (x, 1 - x):
                self.c_copy(j, qx, c).wait_send()


def forward_kernel(dims, pad, comm, *all_refs):
    rows, slots, width, hidden = dims
    tokens = rows * slots
    tiles = tokens // TILE
    all_refs = list(all_refs)
    take = lambda n: [all_refs.pop(0) for _ in range(n)]
    lengths, vec_in, tok_in, cot_in = take(4)
    wqkv_in, wout_in, w1_in, w2_in = take(4) if comm else [None] + take(3)
    out, n1_out, qkv_out, prob_out, mixed_out, resid_out, n2_out, act_out, slope_out, gffn_out, acc, vec = take(12)
    weights_out = take(3) if comm else []
    tok, cot, wa, w1, w2, n1, qkv, slot, mixed, resid, n2, act, slope, gffn, seg_col, seg_row = take(16)
    slot_sem, in_sem, out_sem, tile_sem = take(4)
    moves = [(tok_in, tok), (cot_in, cot)]
    if comm:
        place = position()
        z, y, x, c = place
        vec_land, vs, vr = take(3)
        sems = take(8)
        ga, g1, g2 = [Gather(t, buf, sems, place) for t, buf in enumerate((wa, w1, w2))]
        for q in range(4):
            source = wqkv_in.at[:, q * width : (q + 1) * width] if q < 3 else wout_in
            moves.append((source, wa.at[q // 2, q % 2, z, y]))
        for q in range(4):
            moves.append((w1_in.at[:, q * width : (q + 1) * width], w1.at[q // 2, q % 2, z, y]))
        moves.append((w2_in, w2.at[:, :, z, y]))
    else:
        moves += [(wout_in, wa), (w1_in, w1), (w2_in, w2)]
    loads = [pltpu.make_async_copy(a, b, in_sem.at[i]) for i, (a, b) in enumerate(moves)]
    for copy in loads[2:] + loads[:2]:
        copy.start()

    def tile_copies(i, pairs, base):
        at = pl.ds(pl.multiple_of(i * TILE, TILE), TILE)
        return [pltpu.make_async_copy(a.at[at], b.at[at], tile_sem.at[i, base + j]) for j, (a, b) in enumerate(pairs)]

    ones = [(resid, resid_out), (n2, n2_out), (act, act_out), (slope, slope_out)]
    twos = [(tok, out), (gffn, gffn_out)]

    def tile_one(i):
        for copy in tile_copies(i, ones, 0):
            copy.start()

    def tile_two(i):
        for copy in tile_copies(i, twos, len(ones)):
            copy.start()

    refs = dict(
        vec=vec, tok=tok, cot=cot, wa=wa, w1=w1, w2=w2, n1=n1, qkv=qkv, slot=slot, mixed=mixed, resid=resid, n2=n2,
        act=act, slope=slope, gffn=gffn, seg_col=seg_col, seg_row=seg_row, slot_sem=slot_sem, prob_out=prob_out,
        acc=acc, pad=pad, tile_one=tile_one, tile_two=tile_two,
    )
    norm_one, project, attend, feed_one, feed_two = forward_phases(dims, refs)
    pairs_out = [(n1, n1_out), (qkv, qkv_out), (mixed, mixed_out)]
    if comm:
        pairs_out += list(zip((wa, w1, w2), weights_out))
    stores = [pltpu.make_async_copy(a, b, out_sem.at[i]) for i, (a, b) in enumerate(pairs_out)]
    if comm:
        others = z_partners(z)
        peers = [device(o, y, x, c) for o in others] + [device(o, 1 - y, x, c) for o in [z] + others]
        greet(peers + [device(z, y, 1 - x, c), device(z, y, x, 1 - c)])
        mine = z * 2 + y
        vec_sends = [
            remote(vec_in, vec_land.at[mine], vs.at[k], vr.at[mine], peer) for k, peer in enumerate(peers)
        ]
        for copy in vec_sends:
            copy.start()
        for copy in loads[2:]:
            copy.wait()
        ga.start()
        fill_segments(lengths, rows, slots, seg_col, seg_row)
        vec_land[mine] = vec_in[...]
        vec[...] = jnp.zeros_like(vec)
        sources = [(o, y) for o in others] + [(o, 1 - y) for o in [z] + others]
        for k, (zs, ys) in enumerate(sources):
            remote(vec_in, vec_land.at[zs * 2 + ys], vs.at[k], vr.at[zs * 2 + ys], peers[k]).wait_recv()
        spread_vectors(vec_land, vec, width)
        loads[0].wait()
        norm_one()
        stores[0].start()
        for k in range(3):
            ga.z_step(k)
        for k in range(4):
            ga.y_step(k)
        g1.start()
        for j in range(7):
            ga.x_step(j)
        ga.done()
        stores[3].start()
        project()
        stores[1].start()
        hooks = {
            1: [lambda: g1.z_step(0)], 2: [lambda: g1.z_step(1)], 3: [lambda: g1.z_step(2)],
            4: [lambda: g1.y_step(0), lambda: g1.y_step(1)], 5: [lambda: g1.y_step(2), g2.start],
            6: [lambda: g1.y_step(3), lambda: g1.x_step(0), lambda: g1.x_step(1)],
            7: [lambda: g1.x_step(2), lambda: g1.x_step(3)], 8: [lambda: g2.z_step(0), lambda: g1.x_step(4)],
            9: [lambda: g1.x_step(5), lambda: g1.x_step(6)], 10: [lambda: g2.z_step(1)], 11: [lambda: g2.z_step(2)],
        }
        attend(hooks)
        stores[2].start()
        g1.done()
        stores[4].start()
        feed_one({
            0: [lambda: g2.y_step(0), lambda: g2.y_step(1), lambda: g2.y_step(2)],
            1: [lambda: g2.y_step(3)] + [lambda j=j: g2.x_step(j) for j in range(4)],
            2: [lambda j=j: g2.x_step(j) for j in range(4, 7)],
        })
        g2.done()
        stores[5].start()
        loads[1].wait()
        feed_two()
        for gather in (ga, g1, g2):
            gather.finish()
        for copy in vec_sends:
            copy.wait_send()
    else:
        fill_segments(lengths, rows, slots, seg_col, seg_row)
        vec[...] = vec_in[...].astype(F32)
        loads[0].wait()
        norm_one()
        stores[0].start()
        loads[2].wait()
        project()
        stores[1].start()
        attend({})
        stores[2].start()
        for copy in loads[3:] + loads[1:2]:
            copy.wait()
        feed_one({})
        feed_two()
    for copy in stores:
        copy.wait()

    def finish(i, _):
        for copy in tile_copies(i, ones, 0) + tile_copies(i, twos, len(ones)):
            copy.wait()
        return 0

    lax.fori_loop(0, tiles, finish, 0)


def spread_vectors(land, vec, width):
    shards = land.shape[0]
    piece = width // shards
    lines = jnp.concatenate([land[s].astype(F32)[:FB1_ROW, :piece] for s in range(shards)], axis=1)
    vec[:FB1_ROW, :] = lines
    per = 3
    tiles = [land[s, FB1_ROW + j : FB1_ROW + j + 1, :].astype(F32) for s in range(shards) for j in range(per)]
    wide = width // 128
    for r in range(len(tiles) // wide):
        vec[FB1_ROW + r : FB1_ROW + r + 1, :] = jnp.concatenate(tiles[r * wide : (r + 1) * wide], axis=1)


def forward_call(dims, pad, comm):
    rows, slots, width, hidden = dims
    tokens = rows * slots
    tiles, pairs = tokens // TILE, width // 128
    piece = width // 8
    wide = prob_offsets(slots // QB)[1]
    S = jax.ShapeDtypeStruct
    matrix = (2, 2, 4, 2, piece, width)
    shapes = [
        S((tokens, width), F32), S((tokens, width), BF), S((tokens, 3 * width), BF),
        S((rows * pairs, 2 * QB, wide), BF), S((tokens, width), BF), S((tokens, width), F32), S((tokens, width), BF),
        S((tokens, hidden), BF), S((tokens, hidden), BF), S((tokens, width), BF), S((2, 8, width), F32),
        S((VEC_ROWS, width), F32),
    ]
    V = pltpu.VMEM
    scratch = [
        V((tokens, width), F32), V((tokens, width), F32), V(matrix, BF), V(matrix, BF), V(matrix, BF),
        V((tokens, width), BF), V((tokens, 3 * width), BF), V((2, 2 * QB, wide), BF),
        V((tokens, width), BF), V((tokens, width), F32), V((tokens, width), BF), V((tokens, hidden), BF),
        V((tokens, hidden), BF), V((tokens, width), BF), V((tokens, 128), jnp.int32), V((rows, 8, slots), jnp.int32),
        DMA((2,)), DMA((11,)), DMA((6,)), DMA((tiles, 6)),
    ]
    params = dict(vmem_limit_bytes=VMEM_LIMIT)
    if comm:
        shapes += [S(matrix, BF)] * 3
        scratch += [V((8, VEC_ROWS, 128), BF), DMA((7,)), DMA((8,))]
        scratch += [DMA((3, 3, 2)), DMA((3, 4, 2)), DMA((3, 4, 2)), DMA((3, 4, 2)), DMA((3, 8)), DMA((3, 8)),
                    DMA((3, 8, 2)), DMA((3, 8, 2))]
        params.update(collective_id=0, has_side_effects=True)
    return pl.pallas_call(
        functools.partial(forward_kernel, dims, pad, comm),
        out_shape=shapes,
        in_specs=[SCALARS, INSIDE] + [ANY] * (6 if comm else 5),
        out_specs=[ANY] * 10 + [INSIDE, INSIDE] + ([ANY] * 3 if comm else []),
        scratch_shapes=scratch,
        compiler_params=pltpu.CompilerParams(**params),
        name="forward",
    )


class Reduce:
    def __init__(self, t, grad, land, final, sems, place):
        self.t, self.grad, self.final, self.place = t, grad, final, place
        self.from_core, self.from_x, self.from_y, self.from_yx, self.from_xy, self.from_z = land
        self.send, self.recv = sems
        rows = grad.shape[4]
        self.first, self.second = pl.ds(0, rows // 2), pl.ds(rows // 2, rows // 2)

    def copy(self, i, src, dst, target, slot=None):
        slot = i if slot is None else slot
        return remote(src, dst, self.send.at[self.t, i], self.recv.at[self.t, slot], target)

    def core_copy(self):
        z, y, x, c = self.place
        return [
            self.copy(i, self.grad.at[q, 1 - c], self.from_core.at[q], device(z, y, x, 1 - c)) for i, q in enumerate((0, 1))
        ]

    def one_copy(self):
        z, y, x, c = self.place
        g = self.grad
        return [
            self.copy(2, g.at[1 - x, c, :, :, self.first], self.from_x, device(z, y, 1 - x, c)),
            self.copy(3, g.at[:, c, :, 1 - y, self.second], self.from_y, device(z, 1 - y, x, c)),
        ]

    def two_copy(self):
        z, y, x, c = self.place
        g = self.grad
        return [
            self.copy(4, g.at[x, c, :, 1 - y, self.first], self.from_xy, device(z, 1 - y, x, c)),
            self.copy(5, g.at[1 - x, c, :, y, self.second], self.from_yx, device(z, y, 1 - x, c)),
        ]

    def z_copy(self):
        z, y, x, c = self.place
        return [
            self.copy(6 + k, self.grad.at[x, c, o, y], self.from_z.at[k], device(o, y, x, c))
            for k, o in enumerate(z_partners(z))
        ]

    def across_copy(self):
        z, y, x, c = self.place
        own = self.final.at[x, c]
        return self.copy(9, own, own, device(z, y, 1 - x, c))

    def beside_copy(self):
        z, y, x, c = self.place
        own = self.final.at[x, c]
        return self.copy(10, own, own, device(z, y, x, 1 - c))

    def relay_copy(self):
        z, y, x, c = self.place
        other = self.final.at[1 - x, c]
        return self.copy(11, other, other, device(z, y, x, 1 - c))

    def start(self):
        for copy in self.core_copy():
            copy.start()

    def core_done(self):
        z, y, x, c = self.place
        for copy in self.core_copy():
            copy.wait_recv()

        def body(i, _):
            q, zs = lax.div(i, 4), lax.rem(i, 4)
            total = self.grad[q, c, zs].astype(F32) + self.from_core[q, zs].astype(F32)
            self.grad[q, c, zs] = total.astype(BF)
            return 0

        lax.fori_loop(0, 8, body, 0)
        for copy in self.one_copy():
            copy.start()

    def one_done(self):
        z, y, x, c = self.place
        g = self.grad
        for copy in self.one_copy():
            copy.wait_recv()

        def body(zs, _):
            total = g[x, c, zs, :, self.first].astype(F32) + self.from_x[zs].astype(F32)
            g[x, c, zs, :, self.first] = total.astype(BF)
            total = g[:, c, zs, y, self.second].astype(F32) + self.from_y[:, zs].astype(F32)
            g[:, c, zs, y, self.second] = total.astype(BF)
            return 0

        lax.fori_loop(0, 4, body, 0)
        for copy in self.two_copy():
            copy.start()

    def two_done(self):
        z, y, x, c = self.place
        g = self.grad
        for copy in self.two_copy():
            copy.wait_recv()

        def body(zs, _):
            total = g[x, c, zs, y, self.first].astype(F32) + self.from_xy[zs].astype(F32)
            g[x, c, zs, y, self.first] = total.astype(BF)
            total = g[x, c, zs, y, self.second].astype(F32) + self.from_yx[zs].astype(F32)
            g[x, c, zs, y, self.second] = total.astype(BF)
            return 0

        lax.fori_loop(0, 4, body, 0)
        for copy in self.z_copy():
            copy.start()

    def z_done(self):
        z, y, x, c = self.place
        for copy in self.z_copy():
            copy.wait_recv()
        total = self.grad[x, c, z, y].astype(F32)
        for k in range(3):
            total = total + self.from_z[k].astype(F32)
        self.final[x, c] = total.astype(BF)
        self.across_copy().start()
        self.beside_copy().start()

    def relay(self):
        self.across_copy().wait_recv()
        self.relay_copy().start()

    def done(self):
        self.beside_copy().wait_recv()
        self.relay_copy().wait_recv()

    def finish(self):
        copies = self.core_copy() + self.one_copy() + self.two_copy() + self.z_copy()
        for copy in copies + [self.across_copy(), self.beside_copy(), self.relay_copy()]:
            copy.wait_send()


class VectorSum:
    def __init__(self, ref, land, z_land, send, recv, place):
        self.ref, self.land, self.z_land, self.send, self.recv, self.place = ref, land, z_land, send, recv, place
        z, y, x, c = place
        targets = [device(z, y, x, 1 - c), device(z, y, 1 - x, c), device(z, 1 - y, x, c)]
        self.pair = [
            remote(ref.at[i], land.at[i], send.at[i], recv.at[i], target) for i, target in enumerate(targets)
        ]
        self.along = [
            remote(ref.at[3], z_land.at[z], send.at[3 + k], recv.at[3 + z], device(o, y, x, c))
            for k, o in enumerate(z_partners(z))
        ]

    def start(self, value):
        self.ref[0] = value
        self.pair[0].start()

    def step(self, i):
        self.pair[i].wait_recv()
        self.ref[i + 1] = self.ref[i] + self.land[i]
        if i < 2:
            self.pair[i + 1].start()
        else:
            for copy in self.along:
                copy.start()

    def done(self):
        z, y, x, c = self.place
        self.z_land[z] = self.ref[3]
        for k, o in enumerate(z_partners(z)):
            remote(
                self.ref.at[3], self.z_land.at[o], self.send.at[3 + k], self.recv.at[3 + o], device(o, y, x, c)
            ).wait_recv()
        total = self.z_land[0] + self.z_land[1]
        total = total + self.z_land[2]
        return total + self.z_land[3]

    def finish(self):
        for copy in self.pair + self.along:
            copy.wait_send()


def backward_kernel(dims, pad, comm, *all_refs):
    rows, slots, width, hidden = dims
    tokens = rows * slots
    tiles, pairs = tokens // TILE, width // 128
    half = width // 2
    all_refs = list(all_refs)
    take = lambda n: [all_refs.pop(0) for _ in range(n)]
    lengths, vec, acc_in, tok_in, cot_in, wa_in, w1_in, w2_in = take(8)
    n1_in, qkv_in, prob_in, mixed_in, resid_in, n2_in, act_in, slope_in, gffn_in = take(9)
    if comm:
        gtok_out, gqkv_out, gout_out, g1_out, g2_out, sums = take(6)
    else:
        gtok_out, da_out, d1_out, d2_out, sums = take(5)
    cot, wa, w1, w2, slot, mixed, resid, n2, act, slope, gffn, gproj, d2, acc, seg_col, seg_row = take(16)
    slot_sem, in_sem, out_sem, tile_sem = take(4)
    qkv, n1, tok = act.at[:, : 3 * width], act.at[:, 3 * width :], cot
    da0, da1 = w2.at[:, :, :, :, :, :half], w2.at[:, :, :, :, :, half:]
    moves = [
        (act_in, act), (gffn_in, gffn), (w2_in, w2), (slope_in, slope), (w1_in, w1), (resid_in, resid), (cot_in, cot),
        (wa_in, wa), (n2_in, n2), (mixed_in, mixed), (qkv_in, qkv), (n1_in, n1), (tok_in, tok),
    ]
    loads = [pltpu.make_async_copy(a, b, in_sem.at[i]) for i, (a, b) in enumerate(moves)]
    for copy in loads[:10]:
        copy.start()

    def tile_copy(i):
        at = pl.ds(pl.multiple_of(i * TILE, TILE), TILE)
        return pltpu.make_async_copy(tok.at[at], gtok_out.at[at], tile_sem.at[i])

    refs = dict(
        vec=vec, acc=acc, tok=tok, cot=cot, wa=wa, w1=w1, w2=w2, n1=n1, qkv=qkv, slot=slot, mixed=mixed,
        resid=resid, n2=n2, act=act, slope=slope, gffn=gffn, gproj=gproj, gmixed=gffn, d2=d2, d1=w1, da0=da0, da1=da1,
        seg_col=seg_col, seg_row=seg_row, slot_sem=slot_sem, prob_in=prob_in, pad=pad,
        tile_out=lambda i: tile_copy(i).start(),
    )
    (
        weight_two, through_ffn, weight_one, weight_out, attend_back, weight_pairs, finish_tokens, vector_sums,
    ) = backward_phases(dims, refs)
    hooks = [{}, {}, {}, {}]
    stores = []
    if comm:
        place = position()
        z, y, x, c = place
        core_land = take(2)
        lands = [take(5) for _ in range(4)]
        finals = take(4)
        sems = take(2)
        vec_ref, vec_land, vec_z, vec_send, vec_recv, final_sem = take(6)
        core_lands = core_land + [core_land[0].at[..., :half], core_land[0].at[..., half:]]
        chunks = [
            Reduce(t, grad, [core_lands[t]] + lands[t], finals[t], sems, place)
            for t, grad in enumerate((d2, w1, da0, da1))
        ]
        r2, r1, ra, rb = chunks
        vector = VectorSum(vec_ref, vec_land, vec_z, vec_send, vec_recv, place)
        hooks = [
            {1: [r2.core_done]},
            {1: [r1.core_done], 3: [r2.two_done]},
            {5: [ra.core_done], 6: [r1.one_done, r2.z_done], 8: [r2.relay, r1.two_done], 9: [ra.one_done], 11: [r1.z_done]},
            {0: [r1.relay, ra.two_done], 1: [rb.core_done], 2: [ra.z_done], 3: [rb.one_done, ra.relay]},
        ]
        greet([device(o, y, x, c) for o in z_partners(z)]
              + [device(z, 1 - y, x, c), device(z, y, 1 - x, c), device(z, y, x, 1 - c)])
    fill_segments(lengths, rows, slots, seg_col, seg_row)
    acc[...] = jnp.zeros_like(acc)
    acc[SF_ROW] = acc_in[0]
    acc[FB2_ROW] = acc_in[1]
    for copy in loads[:2]:
        copy.wait()
    weight_two()
    for copy in loads[10:12]:
        copy.start()
    if comm:
        r2.start()
    for copy in loads[2:8]:
        copy.wait()
    through_ffn(hooks[0])
    loads[12].start()
    loads[8].wait()
    weight_one()
    if comm:
        r1.start()
        r2.one_done()
    loads[9].wait()
    weight_out()
    loads[10].wait()
    early = rows * 2
    attend_back(0, early, hooks[1])
    loads[11].wait()
    weight_pairs(da0, 0, 2)
    if comm:
        ra.start()
    attend_back(early, rows * pairs, hooks[2])
    weight_pairs(da1, 2, 4)
    if comm:
        rb.start()
    loads[12].wait()
    finish_tokens(hooks[3])
    if comm:
        def deliver(t, pairs_of):
            for i, (a, b) in enumerate(pairs_of):
                copy = pltpu.make_async_copy(a, b, final_sem.at[t, i])
                copy.start()
                stores.append(copy)

        def slabs(t):
            found = []
            for q in range(4):
                ref = finals[t].at[q // 2, q % 2]
                if t == 2 and q >= 2:
                    found.append((ref, gout_out.at[:, (q - 2) * half : (q - 1) * half]))
                else:
                    p = q if t == 2 else q + 2
                    for part in range(3):
                        at = part * width + p * 128
                        found.append((ref.at[:, part * 128 : (part + 1) * 128], gqkv_out.at[:, at : at + 128]))
            return found

        vector.start(vector_sums())
        r2.done()
        deliver(0, [(finals[0], g2_out)])
        vector.step(0)
        r1.done()
        deliver(1, [(finals[1].at[q // 2, q % 2], g1_out.at[:, q * width : (q + 1) * width]) for q in range(4)])
        rb.two_done()
        vector.step(1)
        ra.done()
        deliver(2, slabs(2))
        vector.step(2)
        rb.z_done()
        sums[...] = vector.done()
        rb.relay()
        rb.done()
        deliver(3, slabs(3))
        for chunk in chunks:
            chunk.finish()
        vector.finish()
    else:
        sums[...] = vector_sums()
        stores = [
            pltpu.make_async_copy(a, b, out_sem.at[i])
            for i, (a, b) in enumerate([(d2, d2_out), (w1, d1_out), (w2, da_out)])
        ]
        for copy in stores:
            copy.start()
    for copy in stores:
        copy.wait()

    def finish(i, _):
        tile_copy(i).wait()
        return 0

    lax.fori_loop(0, tiles, finish, 0)


def backward_call(dims, pad, comm):
    rows, slots, width, hidden = dims
    tokens = rows * slots
    tiles, pairs = tokens // TILE, width // 128
    piece, half = width // 8, width // 2
    wide = prob_offsets(slots // QB)[1]
    S = jax.ShapeDtypeStruct
    matrix = (2, 2, 4, 2, piece, width)
    V = pltpu.VMEM
    tall = lambda dtype: V((tokens, width), dtype)
    scratch = [
        tall(F32), V(matrix, BF), V(matrix, BF), V(matrix, BF), V((2, 2 * QB, wide), BF), tall(BF), tall(F32), tall(BF),
        V((tokens, hidden), BF), V((tokens, hidden), BF), tall(BF), tall(BF), V(matrix, BF), V((VEC_ROWS, 8, width), F32),
        V((tokens, 128), jnp.int32), V((rows, 8, slots), jnp.int32), DMA((2,)), DMA((13,)), DMA((3,)), DMA((tiles,)),
    ]
    params = dict(vmem_limit_bytes=VMEM_LIMIT)
    shapes = [S((tokens, width), F32)]
    if comm:
        shapes += [
            S((piece, 3 * width), BF), S((piece, width), BF), S((piece, hidden), BF), S((2, 2, piece, width), BF),
        ]
        scratch += [V((2, 4, 2, piece, width), BF)] * 2
        for cols in (width, width, half, half):
            scratch += [
                V((4, 2, piece // 2, cols), BF), V((2, 4, piece // 2, cols), BF), V((4, piece // 2, cols), BF),
                V((4, piece // 2, cols), BF), V((3, piece, cols), BF),
            ]
        scratch += [V((2, 2, piece, cols), BF) for cols in (width, width, half, half)]
        scratch += [DMA((4, 12)), DMA((4, 12))]
        scratch += [V((4, VEC_ROWS, width), F32), V((3, VEC_ROWS, width), F32), V((4, VEC_ROWS, width), F32)]
        scratch += [DMA((6,)), DMA((7,)), DMA((4, 12))]
        params.update(collective_id=1, has_side_effects=True)
    else:
        shapes += [S(matrix, BF)] * 3
    shapes += [S((VEC_ROWS, width), F32)]
    return pl.pallas_call(
        functools.partial(backward_kernel, dims, pad, comm),
        out_shape=shapes,
        in_specs=[SCALARS, INSIDE, INSIDE] + [ANY] * 14,
        out_specs=[ANY] * (len(shapes) - 1) + [INSIDE],
        scratch_shapes=scratch,
        compiler_params=pltpu.CompilerParams(**params),
        name="backward",
    )


def local(
    fsdp, dp,
    tokens, lengths, cotangent, ln1_gain, ln1_bias, w_qkv, qkv_bias, w_out, out_bias, scale_attn, ln2_gain, ln2_bias,
    w_fc1, fc1_bias, w_fc2, fc2_bias, scale_ffn,
):
    rows = lengths.shape[0]
    slots, width = tokens.shape[0] // rows, tokens.shape[1]
    hidden = w_fc1.shape[1]
    dims = (rows, slots, width, hidden)
    pad = lengths.shape[1] - 1
    piece = width // 8
    comm = fsdp == 8 and dp == 4
    me = lax.axis_index("fsdp")
    lines = [
        ln1_gain, ln1_bias, qkv_bias[:, 0], qkv_bias[:, 1], out_bias, scale_attn, ln2_gain, ln2_bias, fc2_bias, scale_ffn,
    ]
    own = jnp.stack(lines, axis=0)
    if comm:
        own = jnp.concatenate([jnp.pad(own, ((0, 0), (0, 128 - piece))), fc1_bias.reshape(-1, 128)], axis=0)
        own = jnp.pad(own, ((0, VEC_ROWS - own.shape[0]), (0, 0)))
        forward = forward_call(dims, pad, True)(
            lengths, own, tokens, cotangent, w_qkv, w_out, w_fc1, w_fc2.reshape(2, 2, piece, width)
        )
        out, n1, qkv, prob, mixed, resid, n2, act, slope, gffn, acc, vec, full_a, full_1, full_2 = forward
    else:
        vec = lax.all_gather(own, "fsdp", axis=1, tiled=True)
        bias_one = lax.all_gather(fc1_bias, "fsdp", axis=0, tiled=True).reshape(-1, width)
        vec = jnp.concatenate([vec, bias_one], axis=0)
        vec = jnp.concatenate([vec, jnp.zeros((VEC_ROWS - vec.shape[0], width), BF)], axis=0)

        def by_columns(shard):
            full = lax.all_gather(shard, "fsdp", axis=0, tiled=True)
            return full.reshape(4, 2, piece, 2, 2, width).transpose(3, 4, 0, 1, 2, 5)

        full_a = by_columns(jnp.concatenate([w_qkv, w_out], axis=1))
        full_1 = by_columns(w_fc1)
        full_2 = lax.all_gather(w_fc2, "fsdp", axis=0, tiled=True)
        full_2 = full_2.reshape(4, 2, 2, 2, piece, width).transpose(2, 3, 0, 1, 4, 5)
        forward = forward_call(dims, pad, False)(lengths, vec, tokens, cotangent, full_a, full_1, full_2)
        out, n1, qkv, prob, mixed, resid, n2, act, slope, gffn, acc, vec = forward
    backward = backward_call(dims, pad, comm)(
        lengths, vec, acc, tokens, cotangent, full_a, full_1, full_2, n1, qkv, prob, mixed, resid, n2, act, slope, gffn
    )
    if comm:
        grad_tokens, sum_qkv, sum_out, sum_1, sum_2, sums = backward
        sum_2 = sum_2.reshape(-1, width)
    else:
        grad_tokens, da, d1, d2, sums = backward

        def total(array):
            part = lax.psum_scatter(array, "fsdp", scatter_dimension=0, tiled=True)
            return lax.psum(part, "dp")

        d1 = d1.transpose(2, 3, 4, 0, 1, 5).reshape(width, hidden)
        d2 = d2.transpose(2, 3, 0, 1, 4, 5).reshape(hidden, width)
        first = da[..., : width // 2].transpose(2, 3, 4, 0, 1, 5).reshape(width, 4, 3, 128)
        second = da[..., width // 2 :].transpose(2, 3, 4, 0, 1, 5).reshape(width, 4, 3, 128)
        heads = jnp.concatenate([first[:, :2], second], axis=1).transpose(0, 2, 1, 3).reshape(width, 3 * width)
        sum_a = total(jnp.concatenate([heads, first[:, 2:].reshape(width, width)], axis=1))
        sum_qkv, sum_out = sum_a[:, : 3 * width], sum_a[:, 3 * width :]
        sum_1, sum_2 = total(d1), total(d2)
        sums = lax.psum(sums, ("fsdp", "dp"))
    own_piece = width // fsdp
    mine = lax.dynamic_slice(sums, (0, me * own_piece), (FB1_ROW, own_piece))
    bias_sums = sums[FB1_ROW : FB1_ROW + hidden // width].reshape(-1)
    bias_one = lax.dynamic_slice(bias_sums, (me * (hidden // fsdp),), (hidden // fsdp,))
    return (
        out, grad_tokens, mine[G1_ROW], mine[B1_ROW], sum_qkv.astype(F32),
        jnp.stack([mine[QB_ROW], mine[VB_ROW]], axis=1), sum_out.astype(F32), mine[OB_ROW], mine[SA_ROW],
        mine[G2_ROW], mine[B2_ROW], sum_1.astype(F32), bias_one, sum_2.astype(F32), mine[FB2_ROW], mine[SF_ROW],
    )


def solution(mesh):
    both, one, two = P(("fsdp", "dp"), None), P("fsdp"), P("fsdp", None)
    in_specs = (both, both, both, one, one, two, two, two, one, one, one, one, two, one, two, one, one)
    out_specs = (both, both, one, one, two, two, two, one, one, one, one, two, one, two, one, one)
    run = functools.partial(local, mesh.shape["fsdp"], mesh.shape["dp"])
    return jax.shard_map(run, mesh=mesh, in_specs=in_specs, out_specs=out_specs, check_vma=False)
```

```python
import functools
import math

import jax
import jax.numpy as jnp
from jax import lax
from jax.experimental import pallas as pl
from jax.experimental.pallas import tpu as pltpu
from jax.sharding import PartitionSpec as P

HEAD_DIM = 64
norm_eps = 1e-06
masked_score = -1e30
BF = jnp.bfloat16
F32 = jnp.float32
TILE = 256
QB = 128
VMEM_LIMIT = 67043328

MESH = pl.DeviceIdType.MESH
SHARED = 64

G1_ROW, B1_ROW, QB_ROW, VB_ROW, OB_ROW, SA_ROW, G2_ROW, B2_ROW, FB2_ROW, SF_ROW, FB1_ROW = range(11)
VEC_ROWS = 16


def mm(a, b):
    return lax.dot_general(a, b, (((1,), (0,)), ((), ())), preferred_element_type=F32)


def mm_bt(a, b):
    return lax.dot_general(a, b, (((1,), (1,)), ((), ())), preferred_element_type=F32)


def mm_at(a, b):
    return lax.dot_general(a, b, (((0,), (0,)), ((), ())), preferred_element_type=F32)


def norm_parts(values):
    centered = values - jnp.mean(values, axis=-1, keepdims=True)
    spread = jnp.mean(centered * centered, axis=-1, keepdims=True)
    inv = lax.rsqrt(spread + norm_eps)
    return centered * inv, inv


def window(block, blocks):
    first = max(block - 1, 0)
    last = min(block + 2, blocks)
    return first * QB, (last - first) * QB


def prob_offsets(blocks):
    offsets, total = [], 0
    for block in range(blocks):
        offsets.append(total)
        total += window(block, blocks)[1]
    return offsets, total


def lane_tile(values, times):
    return jnp.concatenate([values] * times, axis=1) if times > 1 else values


def fill_segments(lengths_ref, rows, slots, seg_col, seg_row):
    count = lengths_ref.shape[1]
    for r in range(rows):
        down = lax.broadcasted_iota(jnp.int32, (slots, 128), 0)
        along = lax.broadcasted_iota(jnp.int32, (8, slots), 1)
        col = jnp.zeros((slots, 128), jnp.int32)
        row = jnp.zeros((8, slots), jnp.int32)
        end = jnp.int32(0)
        for j in range(count):
            end = end + lengths_ref[r, j]
            col = col + (down >= end).astype(jnp.int32)
            row = row + (along >= end).astype(jnp.int32)
        seg_col[pl.ds(r * slots, slots), :] = col
        seg_row[r] = row


def attention_forward(rows, slots, pairs, width, qkv, seg_col, seg_row, prob_slot, mixed, r, pair):
    blocks = slots // QB
    offsets, _ = prob_offsets(blocks)
    low = lax.broadcasted_iota(jnp.int32, (QB, 128), 1) < HEAD_DIM
    col = pl.multiple_of(pair * 128, 128)
    base = pl.multiple_of(r * slots, slots)
    zero = jnp.zeros((QB, 128), BF)
    for b in range(blocks):
        start, wide = window(b, blocks)
        q = qkv[pl.ds(base + b * QB, QB), pl.ds(col, 128)]
        k = qkv[pl.ds(base + start, wide), pl.ds(width + col, 128)]
        v = qkv[pl.ds(base + start, wide), pl.ds(2 * width + col, 128)]
        same = lane_tile(seg_col[pl.ds(base + b * QB, QB), :], wide // 128) == seg_row[r, 0:1, start : start + wide]
        q2 = jnp.concatenate([jnp.where(low, q, zero), jnp.where(low, zero, q)], axis=0)
        scores = mm_bt(q2, k)
        scores = jnp.concatenate(
            [jnp.where(same, scores[:QB], masked_score), jnp.where(same, scores[QB:], masked_score)], axis=0
        )
        peak = jnp.max(scores, axis=-1, keepdims=True)
        weights = jnp.exp(scores - peak)
        total = jnp.sum(weights, axis=-1, keepdims=True)
        probs = (weights * (1.0 / total)).astype(BF)
        prob_slot[:, offsets[b] : offsets[b] + wide] = probs
        out = mm(probs, v)
        mixed[pl.ds(base + b * QB, QB), pl.ds(col, 128)] = jnp.where(low, out[:QB], out[QB:]).astype(BF)


def attention_backward(rows, slots, pairs, width, qkv, prob_slot, mixed, grad_mixed, grads, r, pair):
    blocks = slots // QB
    offsets, _ = prob_offsets(blocks)
    low = lax.broadcasted_iota(jnp.int32, (QB, 128), 1) < HEAD_DIM
    low_all = lax.broadcasted_iota(jnp.int32, (slots, 128), 1) < HEAD_DIM
    factor = 1.0 / math.sqrt(HEAD_DIM)
    col = pl.multiple_of(pair * 128, 128)
    base = pl.multiple_of(r * slots, slots)
    zero = jnp.zeros((QB, 128), BF)
    grad_k = [None] * blocks
    grad_v = [None] * blocks
    for b in range(blocks):
        start, wide = window(b, blocks)
        q = qkv[pl.ds(base + b * QB, QB), pl.ds(col, 128)]
        k = qkv[pl.ds(base + start, wide), pl.ds(width + col, 128)]
        v = qkv[pl.ds(base + start, wide), pl.ds(2 * width + col, 128)]
        up = grad_mixed[pl.ds(base + b * QB, QB), pl.ds(col, 128)]
        out = mixed[pl.ds(base + b * QB, QB), pl.ds(col, 128)]
        probs = prob_slot[:, offsets[b] : offsets[b] + wide]
        q2 = jnp.concatenate([jnp.where(low, q, zero), jnp.where(low, zero, q)], axis=0)
        up2 = jnp.concatenate([jnp.where(low, up, zero), jnp.where(low, zero, up)], axis=0)
        out2 = jnp.concatenate([out, out], axis=0)
        inner = jnp.sum(up2.astype(F32) * out2.astype(F32), axis=-1, keepdims=True)
        grad_probs = mm_bt(up2, v)
        grad_scores = (probs.astype(F32) * (grad_probs - inner)).astype(BF)
        grad_q = mm(grad_scores, k) * factor
        grads[pl.ds(base + b * QB, QB), pl.ds(col, 128)] = jnp.where(low, grad_q[:QB], grad_q[QB:]).astype(BF)
        dk = mm_at(grad_scores, q2)
        dv = mm_at(probs, up2)
        for i in range(wide // QB):
            kb = start // QB + i
            piece_k, piece_v = dk[i * QB : (i + 1) * QB], dv[i * QB : (i + 1) * QB]
            grad_k[kb] = piece_k if grad_k[kb] is None else grad_k[kb] + piece_k
            grad_v[kb] = piece_v if grad_v[kb] is None else grad_v[kb] + piece_v
        done = [b - 1] if b > 0 else []
        if b == blocks - 1:
            done.append(b)
        for kb in done:
            grads[pl.ds(base + kb * QB, QB), pl.ds(width + col, 128)] = grad_k[kb].astype(BF)
            grads[pl.ds(base + kb * QB, QB), pl.ds(2 * width + col, 128)] = grad_v[kb].astype(BF)


def fold(values):
    return jnp.sum(values.reshape(values.shape[0] // 8, 8, values.shape[1]), axis=0)


def gelu_parts(values):
    cdf = 0.5 * (1.0 + lax.erf(values * math.sqrt(0.5)))
    pdf = jnp.exp(-0.5 * values * values) * (1.0 / math.sqrt(2.0 * math.pi))
    return values * cdf, cdf + values * pdf


def block(ref, c):
    value = ref[c // 2, c % 2]
    return value.reshape(-1, value.shape[-1])


def hidden_rows(ref, z):
    return jnp.concatenate([ref[x, c, z, y] for y in range(2) for x in range(2) for c in range(2)], axis=0)


def run_hooks(hooks, step):
    for k, turns in sorted(hooks.items()):

        @pl.when(step == k)
        def _(turns=turns):
            for turn in turns:
                turn()


def forward_phases(dims, refs):
    rows, slots, width, hidden = dims
    tokens = rows * slots
    tiles = tokens // TILE
    pairs = width // 128
    vec = refs["vec"]

    def row_of(i):
        return vec[i : i + 1, :].astype(F32)

    def norm_one(hooks):
        gain, shift = row_of(G1_ROW), row_of(B1_ROW)

        def body(i, _):
            at = pl.ds(pl.multiple_of(i * TILE, TILE), TILE)
            hat, _inv = norm_parts(refs["tok"][at, :])
            refs["n1"][at, :] = (hat * gain + shift).astype(BF)
            run_hooks(hooks, i)
            return 0

        lax.fori_loop(0, tiles, body, 0)

    def project(hooks):
        q_bias, v_bias = row_of(QB_ROW), row_of(VB_ROW)
        factor = 1.0 / math.sqrt(HEAD_DIM)

        def body(i, _):
            at = pl.ds(pl.multiple_of(i * TILE, TILE), TILE)
            normed = refs["n1"][at, :]
            query = (mm(normed, block(refs["wa"], 0)) + q_bias).astype(BF)
            refs["qkv"][at, :width] = (query.astype(F32) * factor).astype(BF)
            refs["qkv"][at, width : 2 * width] = mm(normed, block(refs["wa"], 1)).astype(BF)
            refs["qkv"][at, 2 * width : 3 * width] = (
                mm(normed, block(refs["wa"], 2)) + v_bias
            ).astype(BF)
            run_hooks(hooks, i)
            return 0

        lax.fori_loop(0, tiles, body, 0)

    def attend(hooks):
        steps = rows * pairs

        def out_copy(step):
            slot = lax.rem(step, 2)
            return pltpu.make_async_copy(refs["slot"].at[slot], refs["prob_out"].at[step], refs["slot_sem"].at[slot])

        def body(step, _):
            @pl.when(step >= 2)
            def _():
                out_copy(step - 2).wait()

            attention_forward(
                rows, slots, pairs, width, refs["qkv"], refs["seg_col"], refs["seg_row"],
                refs["slot"].at[lax.rem(step, 2)], refs["mixed"], lax.rem(step, rows), lax.div(step, rows),
            )
            out_copy(step).start()
            run_hooks(hooks, step)
            return 0

        lax.fori_loop(0, steps, body, 0)
        out_copy(steps - 2).wait()
        out_copy(steps - 1).wait()

    def feed_one(hooks):
        out_bias, scale_one = row_of(OB_ROW), row_of(SA_ROW)
        gain, shift = row_of(G2_ROW), row_of(B2_ROW)

        def body(i, _):
            at = pl.ds(pl.multiple_of(i * TILE, TILE), TILE)
            attn = mm(refs["mixed"][at, :], block(refs["wa"], 3)) + out_bias
            resid = refs["tok"][at, :] + scale_one * attn
            refs["resid"][at, :] = resid
            hat, _inv = norm_parts(resid)
            normed = (hat * gain + shift).astype(BF)
            refs["n2"][at, :] = normed
            for c in range(hidden // width):
                cols = slice(c * width, (c + 1) * width)
                pre = mm(normed, block(refs["w1"], c)) + row_of(FB1_ROW + c)
                act, slope = gelu_parts(pre)
                refs["act"][at, cols] = act.astype(BF)
                refs["slope"][at, cols] = slope.astype(BF)
            refs["tile_one"](i)
            run_hooks(hooks, i)
            return 0

        lax.fori_loop(0, tiles, body, 0)

    def feed_two():
        bias_two, scale_two = row_of(FB2_ROW), row_of(SF_ROW)
        refs["acc"][...] = jnp.zeros_like(refs["acc"])

        def body(i, _):
            at = pl.ds(pl.multiple_of(i * TILE, TILE), TILE)
            ffn = mm(refs["act"][at, :], jnp.concatenate([hidden_rows(refs["w2"], z) for z in range(4)], axis=0)) + bias_two
            valid = lane_tile(refs["seg_col"][at, :], width // 128) < refs["pad"]
            up = jnp.where(valid, refs["cot"][at, :], 0.0)
            grad = (scale_two * up).astype(BF)
            refs["gffn"][at, :] = grad
            refs["acc"][0] += fold(up * ffn)
            refs["acc"][1] += fold(grad.astype(F32))
            refs["tok"][at, :] = refs["resid"][at, :] + scale_two * ffn
            refs["tile_two"](i)
            return 0

        lax.fori_loop(0, tiles, body, 0)

    return norm_one, project, attend, feed_one, feed_two


def backward_phases(dims, refs):
    rows, slots, width, hidden = dims
    tokens = rows * slots
    tiles = tokens // TILE
    pairs = width // 128
    parts = hidden // width
    vec, acc = refs["vec"], refs["acc"]
    half = width // 2
    piece = width // 8

    def row_of(i):
        return vec[i : i + 1, :].astype(F32)

    def weight_two():
        per = hidden // 8

        def body(i, _):
            at = pl.ds(pl.multiple_of(i * per, per), per)
            grad = mm_at(refs["act"][:, at], refs["gffn"][...]).astype(BF)
            refs["d2"][:, :, lax.div(i, 2), lax.rem(i, 2)] = grad.reshape(2, 2, per // 4, width)
            return 0

        lax.fori_loop(0, 8, body, 0)

    def through_ffn(hooks):
        gain, scale_one = row_of(G2_ROW), row_of(SA_ROW)

        def body(i, _):
            at = pl.ds(pl.multiple_of(i * TILE, TILE), TILE)
            grad_ffn = refs["gffn"][at, :]
            for c in range(parts):
                cols = slice(c * width, (c + 1) * width)
                grad_act = mm_bt(grad_ffn, hidden_rows(refs["w2"], c))
                pre = (grad_act * refs["slope"][at, cols].astype(F32)).astype(BF)
                refs["slope"][at, cols] = pre
                acc[FB1_ROW + c] += fold(pre.astype(F32))
            grad = mm_bt(refs["slope"][at, :], jnp.concatenate([block(refs["w1"], c) for c in range(parts)], axis=1))
            hat, inv = norm_parts(refs["resid"][at, :])
            acc[G2_ROW] += fold(grad * hat)
            acc[B2_ROW] += fold(grad)
            u = grad * gain
            back = inv * (u - jnp.mean(u, axis=-1, keepdims=True) - hat * jnp.mean(u * hat, axis=-1, keepdims=True))
            valid = lane_tile(refs["seg_col"][at, :], width // 128) < refs["pad"]
            grad_resid = jnp.where(valid, refs["cot"][at, :], 0.0) + back
            refs["resid"][at, :] = grad_resid
            grad_proj = (scale_one * grad_resid).astype(BF)
            refs["gproj"][at, :] = grad_proj
            acc[OB_ROW] += fold(grad_proj.astype(F32))
            refs["gmixed"][at, :] = mm_bt(grad_proj, block(refs["wa"], 3)).astype(BF)
            run_hooks(hooks, i)
            return 0

        lax.fori_loop(0, tiles, body, 0)

    def weight_one():
        def body(i, _):
            at = pl.ds(pl.multiple_of(i * half, half), half)
            for c in range(parts):
                cols = slice(c * width, (c + 1) * width)
                grad = mm_at(refs["n2"][:, at], refs["slope"][:, cols]).astype(BF)
                refs["d1"][c // 2, c % 2, pl.ds(i * 2, 2)] = grad.reshape(2, 2, piece, width)
            return 0

        lax.fori_loop(0, 2, body, 0)

    def weight_out():
        def body(i, _):
            at = pl.ds(pl.multiple_of(i * half, half), half)
            grad = mm_at(refs["mixed"][:, at], refs["gproj"][...])
            low = grad.astype(BF)
            for j in range(2):
                refs["da0"][1, j, pl.ds(i * 2, 2)] = low[:, j * half : (j + 1) * half].reshape(2, 2, piece, half)
            w_out = refs["wa"][1, 1, pl.ds(i * 2, 2)].reshape(half, width)
            acc[SA_ROW] += fold(grad * w_out.astype(F32))
            return 0

        lax.fori_loop(0, 2, body, 0)

    def attend_back(first, last, hooks):
        def in_copy(step):
            slot = lax.rem(step, 2)
            return pltpu.make_async_copy(refs["prob_in"].at[step], refs["slot"].at[slot], refs["slot_sem"].at[slot])

        if first == 0:
            in_copy(0).start()

        def body(step, _):
            @pl.when(step + 1 < rows * pairs)
            def _():
                in_copy(step + 1).start()

            in_copy(step).wait()
            attention_backward(
                rows, slots, pairs, width, refs["qkv"], refs["slot"].at[lax.rem(step, 2)], refs["mixed"],
                refs["gmixed"], refs["qkv"], lax.rem(step, rows), lax.div(step, rows),
            )
            run_hooks(hooks, step)
            return 0

        lax.fori_loop(first, last, body, 0)

    def weight_pairs(target, first, count):
        def body(i, _):
            at = pl.ds(pl.multiple_of(i * half, half), half)
            slabs = [
                refs["qkv"][:, part * width + p * 128 : part * width + (p + 1) * 128]
                for p in range(first, first + count)
                for part in range(3)
            ]
            grad = mm_at(refs["n1"][:, at], jnp.concatenate(slabs, axis=1)).astype(BF)
            for j in range(count):
                target[j // 2, j % 2, pl.ds(i * 2, 2)] = grad[:, j * 384 : (j + 1) * 384].reshape(2, 2, piece, 384)
            return 0

        lax.fori_loop(0, 2, body, 0)

    def finish_tokens(hooks):
        gain = row_of(G1_ROW)

        def body(i, _):
            at = pl.ds(pl.multiple_of(i * TILE, TILE), TILE)
            grad = mm_bt(refs["qkv"][at, :], jnp.concatenate([block(refs["wa"], c) for c in range(3)], axis=1))
            hat, inv = norm_parts(refs["tok"][at, :])
            acc[G1_ROW] += fold(grad * hat)
            acc[B1_ROW] += fold(grad)
            acc[QB_ROW] += fold(refs["qkv"][at, :width].astype(F32))
            acc[VB_ROW] += fold(refs["qkv"][at, 2 * width :].astype(F32))
            u = grad * gain
            back = inv * (u - jnp.mean(u, axis=-1, keepdims=True) - hat * jnp.mean(u * hat, axis=-1, keepdims=True))
            refs["tok"][at, :] = refs["resid"][at, :] + back
            refs["tile_out"](i)
            run_hooks(hooks, i)
            return 0

        lax.fori_loop(0, tiles, body, 0)

    def vector_sums():
        lines = [jnp.sum(acc[i], axis=0, keepdims=True) for i in range(VEC_ROWS)]
        lines[SA_ROW] = (lines[SA_ROW] + row_of(OB_ROW) * lines[OB_ROW]) / row_of(SA_ROW)
        return jnp.concatenate(lines, axis=0)

    return weight_two, through_ffn, weight_one, weight_out, attend_back, weight_pairs, finish_tokens, vector_sums


ANY = pl.BlockSpec(memory_space=pl.ANY)
INSIDE = pl.BlockSpec(memory_space=pltpu.VMEM)
SCALARS = pl.BlockSpec(memory_space=pltpu.SMEM)
DMA = pltpu.SemaphoreType.DMA


def position():
    f, d = lax.axis_index("fsdp"), lax.axis_index("dp")
    return lax.div(f, 2), lax.rem(f, 2), lax.div(d, 2), lax.rem(d, 2)


def device(z, y, x, c):
    return (z * 2 + y, x * 2 + c)


def z_partners(z):
    return [z + 1 - 2 * lax.rem(z, 2), 3 - z, lax.rem(z + 2, 4)]


def remote(src, dst, send, recv, target):
    return pltpu.make_async_remote_copy(
        src_ref=src, dst_ref=dst, send_sem=send, recv_sem=recv, device_id=target, device_id_type=MESH
    )


def greet(targets):
    barrier = pltpu.get_barrier_semaphore()
    for target in targets:
        pl.semaphore_signal(barrier, inc=1, device_id=target, device_id_type=MESH)
    pl.semaphore_wait(barrier, len(targets))


class Gather:
    def __init__(self, t, buf, sems, place):
        self.t, self.buf, self.place = t, buf, place
        self.zs, self.zr, self.ys, self.yr, self.xs, self.xr, self.cs, self.cr = sems
        z = place[0]
        low = z < 2
        self.others = [z + 1 - 2 * lax.rem(z, 2), jnp.where(low, 2, 1), jnp.where(low, 3, 0)]
        self.inner = jnp.logical_or(z == 1, z == 2)

    def shard(self, j):
        z, y, _, _ = self.place
        if j == 7:
            return z, y
        if j < 3:
            return self.others[j], y
        return (z if j == 3 else self.others[j - 4]), 1 - y

    def part(self, z, y, p):
        _, _, x, c = self.place
        rows = self.buf.shape[4]
        if p == 0:
            return self.buf.at[x, c, z, y, pl.ds(0, SHARED)]
        return self.buf.at[:, c, z, y, pl.ds(SHARED, rows - SHARED)]

    def z_copy(self, origin, i, p, target):
        _, y, x, c = self.place
        ref = self.part(origin, y, p)
        return remote(ref, ref, self.zs.at[self.t, i, p], self.zr.at[self.t, origin, p], device(target, y, x, c))

    def outward(self, k, p):
        z = self.place[0]
        return self.z_copy(self.others[k], 2 + k, p, 3 - z if k == 0 else self.others[0])

    def y_copy(self, j, p):
        z, y, x, c = self.place
        zs, ys = self.shard(j)
        ref = self.part(zs, ys, p)
        return remote(ref, ref, self.ys.at[self.t, zs, p], self.yr.at[self.t, zs, p], device(z, 1 - y, x, c))

    def x_copy(self, j, qx):
        z, y, x, c = self.place
        zs, ys = self.shard(j)
        s = zs * 2 + ys
        ref = self.buf.at[qx, c, zs, ys, pl.ds(0, SHARED)]
        return remote(ref, ref, self.xs.at[self.t, s], self.xr.at[self.t, s], device(z, y, 1 - x, c))

    def c_copy(self, j, qx, qc):
        z, y, x, c = self.place
        zs, ys = self.shard(j)
        s = zs * 2 + ys
        ref = self.buf.at[qx, qc, zs, ys]
        return remote(ref, ref, self.cs.at[self.t, s, qx], self.cr.at[self.t, s, qx], device(z, y, x, 1 - c))

    def onward(self, j, p):
        _, _, x, c = self.place
        if p == 0:
            self.x_copy(j, x).start()
        else:
            self.c_copy(j, x, c).start()

    def send_z(self):
        z = self.place[0]
        for p in range(2):
            self.z_copy(z, 0, p, self.others[0]).start()

        @pl.when(self.inner)
        def _():
            for p in range(2):
                self.z_copy(z, 1, p, 3 - z).start()

    def send_y(self):
        for p in range(2):
            self.y_copy(7, p).start()

    def z_step(self, k, p):
        self.z_copy(self.others[k], 0, p, self.others[0]).wait_recv()

        @pl.when(self.inner)
        def _():
            self.outward(k, p).start()

        self.y_copy(k, p).start()
        self.onward(k, p)

    def y_step(self, k, p):
        self.y_copy(3 + k, p).wait_recv()
        self.onward(3 + k, p)

    def x_step(self, j):
        _, _, x, c = self.place
        self.x_copy(j, 1 - x).wait_recv()
        self.c_copy(j, 1 - x, c).start()

    def done(self):
        _, _, x, c = self.place
        for j in range(7):
            for qx in (x, 1 - x):
                self.c_copy(j, qx, 1 - c).wait_recv()

    def finish(self):
        z, _, x, c = self.place
        for p in range(2):
            self.z_copy(z, 0, p, self.others[0]).wait_send()

        @pl.when(self.inner)
        def _():
            for p in range(2):
                self.z_copy(z, 1, p, 3 - z).wait_send()
                for k in range(3):
                    self.outward(k, p).wait_send()

        for j in (7, 0, 1, 2):
            for p in range(2):
                self.y_copy(j, p).wait_send()
        for j in range(7):
            self.x_copy(j, x).wait_send()
            for qx in (x, 1 - x):
                self.c_copy(j, qx, c).wait_send()


START_TURNS = ("asz", "asy")
NORM_TURNS = {
    0: ("az00", "az10"),
    1: ("az11", "ay00", "ay01"),
    2: ("az20", "az01", "ax0", "az21", "bsz", "bsy", "ay10", "ax1", "ay20", "ax2", "ax3", "ay21"),
    3: ("ay30", "ay11", "ax5", "ay31", "bz10", "ax4", "ax6", "bz00", "by00", "bz01", "bz11"),
}
PROJECT_TURNS = {
    0: ("by01",),
    1: ("bz20",),
    3: ("by10", "bz21", "csz", "by20", "bx1"),
}
ATTEND_TURNS = {
    0: ("bx2", "csy"),
    1: ("bx0",),
    2: ("bx3",),
    4: ("by30", "by11", "cz10"),
    6: ("by21", "cz00"),
    7: ("by31", "bx6", "cz01", "cy00"),
    8: ("bx5",),
    9: ("cz20", "bx4"),
    11: ("cy10", "cz21", "cy01"),
}
FEED_TURNS = {
    0: ("cx3", "cx2", "cy20", "cy30", "cx0", "cz11", "cx1"),
    2: ("cy21", "cy31", "cy11", "cx6", "cx4", "cx5"),
}


def turn(gathers, name):
    gather, kind = gathers["abc".index(name[0])], name[1:]
    if kind == "sz":
        return gather.send_z
    if kind == "sy":
        return gather.send_y
    if kind[0] == "x":
        return functools.partial(gather.x_step, int(kind[1]))
    step = gather.z_step if kind[0] == "z" else gather.y_step
    return functools.partial(step, int(kind[1]), int(kind[2]))


def turns(gathers, table):
    return {k: [turn(gathers, name) for name in names] for k, names in table.items()}


def forward_kernel(dims, pad, comm, *all_refs):
    rows, slots, width, hidden = dims
    tokens = rows * slots
    tiles = tokens // TILE
    all_refs = list(all_refs)
    take = lambda n: [all_refs.pop(0) for _ in range(n)]
    lengths, vec_in, tok_in, cot_in = take(4)
    wqkv_in, wout_in, w1_in, w2_in = take(4) if comm else [None] + take(3)
    out, n1_out, qkv_out, prob_out, mixed_out, resid_out, n2_out, act_out, slope_out, gffn_out, acc, vec = take(12)
    weights_out = take(3) if comm else []
    tok, cot, wa, w1, w2, n1, qkv, slot, mixed, resid, n2, act, slope, gffn, seg_col, seg_row = take(16)
    slot_sem, in_sem, out_sem, tile_sem = take(4)
    moves = [(tok_in, tok), (cot_in, cot)]
    if comm:
        place = position()
        z, y, x, c = place
        vec_land, vs, vr = take(3)
        sems = take(8)
        ga, g1, g2 = [Gather(t, buf, sems, place) for t, buf in enumerate((wa, w1, w2))]
        for q in range(4):
            source = wqkv_in.at[:, q * width : (q + 1) * width] if q < 3 else wout_in
            moves.append((source, wa.at[q // 2, q % 2, z, y]))
        for q in range(4):
            moves.append((w1_in.at[:, q * width : (q + 1) * width], w1.at[q // 2, q % 2, z, y]))
        moves.append((w2_in, w2.at[:, :, z, y]))
    else:
        moves += [(wout_in, wa), (w1_in, w1), (w2_in, w2)]
    loads = [pltpu.make_async_copy(a, b, in_sem.at[i]) for i, (a, b) in enumerate(moves)]
    for copy in loads[2:] + loads[:2]:
        copy.start()

    def tile_copies(i, pairs, base):
        at = pl.ds(pl.multiple_of(i * TILE, TILE), TILE)
        return [pltpu.make_async_copy(a.at[at], b.at[at], tile_sem.at[i, base + j]) for j, (a, b) in enumerate(pairs)]

    ones = [(resid, resid_out), (n2, n2_out), (act, act_out), (slope, slope_out)]
    twos = [(tok, out), (gffn, gffn_out)]

    def tile_one(i):
        for copy in tile_copies(i, ones, 0):
            copy.start()

    def tile_two(i):
        for copy in tile_copies(i, twos, len(ones)):
            copy.start()

    refs = dict(
        vec=vec, tok=tok, cot=cot, wa=wa, w1=w1, w2=w2, n1=n1, qkv=qkv, slot=slot, mixed=mixed, resid=resid, n2=n2,
        act=act, slope=slope, gffn=gffn, seg_col=seg_col, seg_row=seg_row, slot_sem=slot_sem, prob_out=prob_out,
        acc=acc, pad=pad, tile_one=tile_one, tile_two=tile_two,
    )
    norm_one, project, attend, feed_one, feed_two = forward_phases(dims, refs)
    pairs_out = [(n1, n1_out), (qkv, qkv_out), (mixed, mixed_out)]
    if comm:
        pairs_out += list(zip((wa, w1, w2), weights_out))
    stores = [pltpu.make_async_copy(a, b, out_sem.at[i]) for i, (a, b) in enumerate(pairs_out)]
    if comm:
        others = z_partners(z)
        peers = [device(o, y, x, c) for o in others] + [device(o, 1 - y, x, c) for o in [z] + others]
        greet(peers + [device(z, y, 1 - x, c), device(z, y, x, 1 - c)])
        mine = z * 2 + y
        vec_sends = [
            remote(vec_in, vec_land.at[mine], vs.at[k], vr.at[mine], peer) for k, peer in enumerate(peers)
        ]
        for copy in vec_sends:
            copy.start()
        gathers = (ga, g1, g2)
        for copy in loads[2:6]:
            copy.wait()
        for name in START_TURNS:
            turn(gathers, name)()
        fill_segments(lengths, rows, slots, seg_col, seg_row)
        vec_land[mine] = vec_in[...]
        vec[...] = jnp.zeros_like(vec)
        sources = [(o, y) for o in others] + [(o, 1 - y) for o in [z] + others]
        for k, (zs, ys) in enumerate(sources):
            remote(vec_in, vec_land.at[zs * 2 + ys], vs.at[k], vr.at[zs * 2 + ys], peers[k]).wait_recv()
        spread_vectors(vec_land, vec, width)
        for copy in loads[6:]:
            copy.wait()
        loads[0].wait()
        norm_one(turns(gathers, NORM_TURNS))
        stores[0].start()
        ga.done()
        stores[3].start()
        project(turns(gathers, PROJECT_TURNS))
        stores[1].start()
        attend(turns(gathers, ATTEND_TURNS))
        stores[2].start()
        g1.done()
        stores[4].start()
        feed_one(turns(gathers, FEED_TURNS))
        g2.done()
        stores[5].start()
        loads[1].wait()
        feed_two()
        for gather in (ga, g1, g2):
            gather.finish()
        for copy in vec_sends:
            copy.wait_send()
    else:
        fill_segments(lengths, rows, slots, seg_col, seg_row)
        vec[...] = vec_in[...].astype(F32)
        loads[0].wait()
        norm_one({})
        stores[0].start()
        loads[2].wait()
        project({})
        stores[1].start()
        attend({})
        stores[2].start()
        for copy in loads[3:] + loads[1:2]:
            copy.wait()
        feed_one({})
        feed_two()
    for copy in stores:
        copy.wait()

    def finish(i, _):
        for copy in tile_copies(i, ones, 0) + tile_copies(i, twos, len(ones)):
            copy.wait()
        return 0

    lax.fori_loop(0, tiles, finish, 0)


def spread_vectors(land, vec, width):
    shards = land.shape[0]
    piece = width // shards
    lines = jnp.concatenate([land[s].astype(F32)[:FB1_ROW, :piece] for s in range(shards)], axis=1)
    vec[:FB1_ROW, :] = lines
    per = 3
    tiles = [land[s, FB1_ROW + j : FB1_ROW + j + 1, :].astype(F32) for s in range(shards) for j in range(per)]
    wide = width // 128
    for r in range(len(tiles) // wide):
        vec[FB1_ROW + r : FB1_ROW + r + 1, :] = jnp.concatenate(tiles[r * wide : (r + 1) * wide], axis=1)


def forward_call(dims, pad, comm):
    rows, slots, width, hidden = dims
    tokens = rows * slots
    tiles, pairs = tokens // TILE, width // 128
    piece = width // 8
    wide = prob_offsets(slots // QB)[1]
    S = jax.ShapeDtypeStruct
    matrix = (2, 2, 4, 2, piece, width)
    shapes = [
        S((tokens, width), F32), S((tokens, width), BF), S((tokens, 3 * width), BF),
        S((rows * pairs, 2 * QB, wide), BF), S((tokens, width), BF), S((tokens, width), F32), S((tokens, width), BF),
        S((tokens, hidden), BF), S((tokens, hidden), BF), S((tokens, width), BF), S((2, 8, width), F32),
        S((VEC_ROWS, width), F32),
    ]
    V = pltpu.VMEM
    scratch = [
        V((tokens, width), F32), V((tokens, width), F32), V(matrix, BF), V(matrix, BF), V(matrix, BF),
        V((tokens, width), BF), V((tokens, 3 * width), BF), V((2, 2 * QB, wide), BF),
        V((tokens, width), BF), V((tokens, width), F32), V((tokens, width), BF), V((tokens, hidden), BF),
        V((tokens, hidden), BF), V((tokens, width), BF), V((tokens, 128), jnp.int32), V((rows, 8, slots), jnp.int32),
        DMA((2,)), DMA((11,)), DMA((6,)), DMA((tiles, 6)),
    ]
    params = dict(vmem_limit_bytes=VMEM_LIMIT)
    if comm:
        shapes += [S(matrix, BF)] * 3
        scratch += [V((8, VEC_ROWS, 128), BF), DMA((7,)), DMA((8,))]
        scratch += [DMA((3, 5, 2)), DMA((3, 4, 2)), DMA((3, 4, 2)), DMA((3, 4, 2)), DMA((3, 8)), DMA((3, 8)),
                    DMA((3, 8, 2)), DMA((3, 8, 2))]
        params.update(collective_id=0, has_side_effects=True)
    return pl.pallas_call(
        functools.partial(forward_kernel, dims, pad, comm),
        out_shape=shapes,
        in_specs=[SCALARS, INSIDE] + [ANY] * (6 if comm else 5),
        out_specs=[ANY] * 10 + [INSIDE, INSIDE] + ([ANY] * 3 if comm else []),
        scratch_shapes=scratch,
        compiler_params=pltpu.CompilerParams(**params),
        name="forward",
    )


class Reduce:
    def __init__(self, t, grad, land, final, sems, place):
        self.t, self.grad, self.final, self.place = t, grad, final, place
        self.from_core, self.from_x, self.from_y, self.from_yx, self.from_xy, self.from_z = land
        self.send, self.recv = sems
        rows = grad.shape[4]
        self.first, self.second = pl.ds(0, rows // 2), pl.ds(rows // 2, rows // 2)

    def copy(self, i, src, dst, target, slot=None):
        slot = i if slot is None else slot
        return remote(src, dst, self.send.at[self.t, i], self.recv.at[self.t, slot], target)

    def core_copy(self):
        z, y, x, c = self.place
        return [
            self.copy(i, self.grad.at[q, 1 - c], self.from_core.at[q], device(z, y, x, 1 - c)) for i, q in enumerate((0, 1))
        ]

    def one_copy(self):
        z, y, x, c = self.place
        g = self.grad
        return [
            self.copy(2, g.at[1 - x, c, :, :, self.first], self.from_x, device(z, y, 1 - x, c)),
            self.copy(3, g.at[:, c, :, 1 - y, self.second], self.from_y, device(z, 1 - y, x, c)),
        ]

    def two_copy(self):
        z, y, x, c = self.place
        g = self.grad
        return [
            self.copy(4, g.at[x, c, :, 1 - y, self.first], self.from_xy, device(z, 1 - y, x, c)),
            self.copy(5, g.at[1 - x, c, :, y, self.second], self.from_yx, device(z, y, 1 - x, c)),
        ]

    def z_copy(self):
        z, y, x, c = self.place
        return [
            self.copy(6 + k, self.grad.at[x, c, o, y], self.from_z.at[k], device(o, y, x, c))
            for k, o in enumerate(z_partners(z))
        ]

    def across_copy(self):
        z, y, x, c = self.place
        own = self.final.at[x, c]
        return self.copy(9, own, own, device(z, y, 1 - x, c))

    def beside_copy(self):
        z, y, x, c = self.place
        own = self.final.at[x, c]
        return self.copy(10, own, own, device(z, y, x, 1 - c))

    def relay_copy(self):
        z, y, x, c = self.place
        other = self.final.at[1 - x, c]
        return self.copy(11, other, other, device(z, y, x, 1 - c))

    def start(self):
        for copy in self.core_copy():
            copy.start()

    def core_done(self):
        z, y, x, c = self.place
        for copy in self.core_copy():
            copy.wait_recv()

        def body(i, _):
            q, zs = lax.div(i, 4), lax.rem(i, 4)
            total = self.grad[q, c, zs].astype(F32) + self.from_core[q, zs].astype(F32)
            self.grad[q, c, zs] = total.astype(BF)
            return 0

        lax.fori_loop(0, 8, body, 0)
        for copy in self.one_copy():
            copy.start()

    def one_done(self):
        z, y, x, c = self.place
        g = self.grad
        for copy in self.one_copy():
            copy.wait_recv()

        def body(zs, _):
            total = g[x, c, zs, :, self.first].astype(F32) + self.from_x[zs].astype(F32)
            g[x, c, zs, :, self.first] = total.astype(BF)
            total = g[:, c, zs, y, self.second].astype(F32) + self.from_y[:, zs].astype(F32)
            g[:, c, zs, y, self.second] = total.astype(BF)
            return 0

        lax.fori_loop(0, 4, body, 0)
        for copy in self.two_copy():
            copy.start()

    def two_done(self):
        z, y, x, c = self.place
        g = self.grad
        for copy in self.two_copy():
            copy.wait_recv()

        def body(zs, _):
            total = g[x, c, zs, y, self.first].astype(F32) + self.from_xy[zs].astype(F32)
            g[x, c, zs, y, self.first] = total.astype(BF)
            total = g[x, c, zs, y, self.second].astype(F32) + self.from_yx[zs].astype(F32)
            g[x, c, zs, y, self.second] = total.astype(BF)
            return 0

        lax.fori_loop(0, 4, body, 0)
        for copy in self.z_copy():
            copy.start()

    def z_done(self):
        z, y, x, c = self.place
        for copy in self.z_copy():
            copy.wait_recv()
        total = self.grad[x, c, z, y].astype(F32)
        for k in range(3):
            total = total + self.from_z[k].astype(F32)
        self.final[x, c] = total.astype(BF)
        self.across_copy().start()
        self.beside_copy().start()

    def relay(self):
        self.across_copy().wait_recv()
        self.relay_copy().start()

    def done(self):
        self.beside_copy().wait_recv()
        self.relay_copy().wait_recv()

    def finish(self):
        copies = self.core_copy() + self.one_copy() + self.two_copy() + self.z_copy()
        for copy in copies + [self.across_copy(), self.beside_copy(), self.relay_copy()]:
            copy.wait_send()


class VectorSum:
    def __init__(self, ref, land, z_land, send, recv, place):
        self.ref, self.land, self.z_land, self.send, self.recv, self.place = ref, land, z_land, send, recv, place
        z, y, x, c = place
        targets = [device(z, y, x, 1 - c), device(z, y, 1 - x, c), device(z, 1 - y, x, c)]
        self.pair = [
            remote(ref.at[i], land.at[i], send.at[i], recv.at[i], target) for i, target in enumerate(targets)
        ]
        self.along = [
            remote(ref.at[3], z_land.at[z], send.at[3 + k], recv.at[3 + z], device(o, y, x, c))
            for k, o in enumerate(z_partners(z))
        ]

    def start(self, value):
        self.ref[0] = value
        self.pair[0].start()

    def step(self, i):
        self.pair[i].wait_recv()
        self.ref[i + 1] = self.ref[i] + self.land[i]
        if i < 2:
            self.pair[i + 1].start()
        else:
            for copy in self.along:
                copy.start()

    def done(self):
        z, y, x, c = self.place
        self.z_land[z] = self.ref[3]
        for k, o in enumerate(z_partners(z)):
            remote(
                self.ref.at[3], self.z_land.at[o], self.send.at[3 + k], self.recv.at[3 + o], device(o, y, x, c)
            ).wait_recv()
        total = self.z_land[0] + self.z_land[1]
        total = total + self.z_land[2]
        return total + self.z_land[3]

    def finish(self):
        for copy in self.pair + self.along:
            copy.wait_send()


def backward_kernel(dims, pad, comm, *all_refs):
    rows, slots, width, hidden = dims
    tokens = rows * slots
    tiles, pairs = tokens // TILE, width // 128
    half = width // 2
    all_refs = list(all_refs)
    take = lambda n: [all_refs.pop(0) for _ in range(n)]
    lengths, vec, acc_in, tok_in, cot_in, wa_in, w1_in, w2_in = take(8)
    n1_in, qkv_in, prob_in, mixed_in, resid_in, n2_in, act_in, slope_in, gffn_in = take(9)
    if comm:
        gtok_out, gqkv_out, gout_out, g1_out, g2_out, sums = take(6)
    else:
        gtok_out, da_out, d1_out, d2_out, sums = take(5)
    cot, wa, w1, w2, slot, mixed, resid, n2, act, slope, gffn, gproj, d2, acc, seg_col, seg_row = take(16)
    slot_sem, in_sem, out_sem, tile_sem = take(4)
    qkv, n1, tok = act.at[:, : 3 * width], act.at[:, 3 * width :], cot
    da0, da1 = w2.at[:, :, :, :, :, :half], w2.at[:, :, :, :, :, half:]
    moves = [
        (act_in, act), (gffn_in, gffn), (w2_in, w2), (slope_in, slope), (w1_in, w1), (resid_in, resid), (cot_in, cot),
        (wa_in, wa), (n2_in, n2), (mixed_in, mixed), (qkv_in, qkv), (n1_in, n1), (tok_in, tok),
    ]
    loads = [pltpu.make_async_copy(a, b, in_sem.at[i]) for i, (a, b) in enumerate(moves)]
    for copy in loads[:10]:
        copy.start()

    def tile_copy(i):
        at = pl.ds(pl.multiple_of(i * TILE, TILE), TILE)
        return pltpu.make_async_copy(tok.at[at], gtok_out.at[at], tile_sem.at[i])

    refs = dict(
        vec=vec, acc=acc, tok=tok, cot=cot, wa=wa, w1=w1, w2=w2, n1=n1, qkv=qkv, slot=slot, mixed=mixed,
        resid=resid, n2=n2, act=act, slope=slope, gffn=gffn, gproj=gproj, gmixed=gffn, d2=d2, d1=w1, da0=da0, da1=da1,
        seg_col=seg_col, seg_row=seg_row, slot_sem=slot_sem, prob_in=prob_in, pad=pad,
        tile_out=lambda i: tile_copy(i).start(),
    )
    (
        weight_two, through_ffn, weight_one, weight_out, attend_back, weight_pairs, finish_tokens, vector_sums,
    ) = backward_phases(dims, refs)
    hooks = [{}, {}, {}, {}]
    stores = []
    if comm:
        place = position()
        z, y, x, c = place
        core_land = take(2)
        lands = [take(5) for _ in range(4)]
        finals = take(4)
        sems = take(2)
        vec_ref, vec_land, vec_z, vec_send, vec_recv, final_sem = take(6)
        core_lands = core_land + [core_land[0].at[..., :half], core_land[0].at[..., half:]]
        chunks = [
            Reduce(t, grad, [core_lands[t]] + lands[t], finals[t], sems, place)
            for t, grad in enumerate((d2, w1, da0, da1))
        ]
        r2, r1, ra, rb = chunks
        vector = VectorSum(vec_ref, vec_land, vec_z, vec_send, vec_recv, place)
        hooks = [
            {1: [r2.core_done]},
            {1: [r1.core_done], 3: [r2.two_done]},
            {5: [ra.core_done], 6: [r1.one_done, r2.z_done], 8: [r2.relay, r1.two_done], 9: [ra.one_done], 11: [r1.z_done]},
            {0: [r1.relay, ra.two_done], 1: [rb.core_done], 2: [ra.z_done], 3: [rb.one_done, ra.relay]},
        ]
        greet([device(o, y, x, c) for o in z_partners(z)]
              + [device(z, 1 - y, x, c), device(z, y, 1 - x, c), device(z, y, x, 1 - c)])
    fill_segments(lengths, rows, slots, seg_col, seg_row)
    acc[...] = jnp.zeros_like(acc)
    acc[SF_ROW] = acc_in[0]
    acc[FB2_ROW] = acc_in[1]
    for copy in loads[:2]:
        copy.wait()
    weight_two()
    for copy in loads[10:12]:
        copy.start()
    if comm:
        r2.start()
    for copy in loads[2:8]:
        copy.wait()
    through_ffn(hooks[0])
    loads[12].start()
    loads[8].wait()
    weight_one()
    if comm:
        r1.start()
        r2.one_done()
    loads[9].wait()
    weight_out()
    loads[10].wait()
    early = rows * 2
    attend_back(0, early, hooks[1])
    loads[11].wait()
    weight_pairs(da0, 0, 2)
    if comm:
        ra.start()
    attend_back(early, rows * pairs, hooks[2])
    weight_pairs(da1, 2, 4)
    if comm:
        rb.start()
    loads[12].wait()
    finish_tokens(hooks[3])
    if comm:
        def deliver(t, pairs_of):
            for i, (a, b) in enumerate(pairs_of):
                copy = pltpu.make_async_copy(a, b, final_sem.at[t, i])
                copy.start()
                stores.append(copy)

        def slabs(t):
            found = []
            for q in range(4):
                ref = finals[t].at[q // 2, q % 2]
                if t == 2 and q >= 2:
                    found.append((ref, gout_out.at[:, (q - 2) * half : (q - 1) * half]))
                else:
                    p = q if t == 2 else q + 2
                    for part in range(3):
                        at = part * width + p * 128
                        found.append((ref.at[:, part * 128 : (part + 1) * 128], gqkv_out.at[:, at : at + 128]))
            return found

        vector.start(vector_sums())
        r2.done()
        deliver(0, [(finals[0], g2_out)])
        vector.step(0)
        r1.done()
        deliver(1, [(finals[1].at[q // 2, q % 2], g1_out.at[:, q * width : (q + 1) * width]) for q in range(4)])
        rb.two_done()
        vector.step(1)
        ra.done()
        deliver(2, slabs(2))
        vector.step(2)
        rb.z_done()
        sums[...] = vector.done()
        rb.relay()
        rb.done()
        deliver(3, slabs(3))
        for chunk in chunks:
            chunk.finish()
        vector.finish()
    else:
        sums[...] = vector_sums()
        stores = [
            pltpu.make_async_copy(a, b, out_sem.at[i])
            for i, (a, b) in enumerate([(d2, d2_out), (w1, d1_out), (w2, da_out)])
        ]
        for copy in stores:
            copy.start()
    for copy in stores:
        copy.wait()

    def finish(i, _):
        tile_copy(i).wait()
        return 0

    lax.fori_loop(0, tiles, finish, 0)


def backward_call(dims, pad, comm):
    rows, slots, width, hidden = dims
    tokens = rows * slots
    tiles, pairs = tokens // TILE, width // 128
    piece, half = width // 8, width // 2
    wide = prob_offsets(slots // QB)[1]
    S = jax.ShapeDtypeStruct
    matrix = (2, 2, 4, 2, piece, width)
    V = pltpu.VMEM
    tall = lambda dtype: V((tokens, width), dtype)
    scratch = [
        tall(F32), V(matrix, BF), V(matrix, BF), V(matrix, BF), V((2, 2 * QB, wide), BF), tall(BF), tall(F32), tall(BF),
        V((tokens, hidden), BF), V((tokens, hidden), BF), tall(BF), tall(BF), V(matrix, BF), V((VEC_ROWS, 8, width), F32),
        V((tokens, 128), jnp.int32), V((rows, 8, slots), jnp.int32), DMA((2,)), DMA((13,)), DMA((3,)), DMA((tiles,)),
    ]
    params = dict(vmem_limit_bytes=VMEM_LIMIT)
    shapes = [S((tokens, width), F32)]
    if comm:
        shapes += [
            S((piece, 3 * width), BF), S((piece, width), BF), S((piece, hidden), BF), S((2, 2, piece, width), BF),
        ]
        scratch += [V((2, 4, 2, piece, width), BF)] * 2
        for cols in (width, width, half, half):
            scratch += [
                V((4, 2, piece // 2, cols), BF), V((2, 4, piece // 2, cols), BF), V((4, piece // 2, cols), BF),
                V((4, piece // 2, cols), BF), V((3, piece, cols), BF),
            ]
        scratch += [V((2, 2, piece, cols), BF) for cols in (width, width, half, half)]
        scratch += [DMA((4, 12)), DMA((4, 12))]
        scratch += [V((4, VEC_ROWS, width), F32), V((3, VEC_ROWS, width), F32), V((4, VEC_ROWS, width), F32)]
        scratch += [DMA((6,)), DMA((7,)), DMA((4, 12))]
        params.update(collective_id=1, has_side_effects=True)
    else:
        shapes += [S(matrix, BF)] * 3
    shapes += [S((VEC_ROWS, width), F32)]
    return pl.pallas_call(
        functools.partial(backward_kernel, dims, pad, comm),
        out_shape=shapes,
        in_specs=[SCALARS, INSIDE, INSIDE] + [ANY] * 14,
        out_specs=[ANY] * (len(shapes) - 1) + [INSIDE],
        scratch_shapes=scratch,
        compiler_params=pltpu.CompilerParams(**params),
        name="backward",
    )


def local(
    fsdp, dp,
    tokens, lengths, cotangent, ln1_gain, ln1_bias, w_qkv, qkv_bias, w_out, out_bias, scale_attn, ln2_gain, ln2_bias,
    w_fc1, fc1_bias, w_fc2, fc2_bias, scale_ffn,
):
    rows = lengths.shape[0]
    slots, width = tokens.shape[0] // rows, tokens.shape[1]
    hidden = w_fc1.shape[1]
    dims = (rows, slots, width, hidden)
    pad = lengths.shape[1] - 1
    piece = width // 8
    comm = fsdp == 8 and dp == 4
    me = lax.axis_index("fsdp")
    lines = [
        ln1_gain, ln1_bias, qkv_bias[:, 0], qkv_bias[:, 1], out_bias, scale_attn, ln2_gain, ln2_bias, fc2_bias, scale_ffn,
    ]
    own = jnp.stack(lines, axis=0)
    if comm:
        own = jnp.concatenate([jnp.pad(own, ((0, 0), (0, 128 - piece))), fc1_bias.reshape(-1, 128)], axis=0)
        own = jnp.pad(own, ((0, VEC_ROWS - own.shape[0]), (0, 0)))
        forward = forward_call(dims, pad, True)(
            lengths, own, tokens, cotangent, w_qkv, w_out, w_fc1, w_fc2.reshape(2, 2, piece, width)
        )
        out, n1, qkv, prob, mixed, resid, n2, act, slope, gffn, acc, vec, full_a, full_1, full_2 = forward
    else:
        vec = lax.all_gather(own, "fsdp", axis=1, tiled=True)
        bias_one = lax.all_gather(fc1_bias, "fsdp", axis=0, tiled=True).reshape(-1, width)
        vec = jnp.concatenate([vec, bias_one], axis=0)
        vec = jnp.concatenate([vec, jnp.zeros((VEC_ROWS - vec.shape[0], width), BF)], axis=0)

        def by_columns(shard):
            full = lax.all_gather(shard, "fsdp", axis=0, tiled=True)
            return full.reshape(4, 2, piece, 2, 2, width).transpose(3, 4, 0, 1, 2, 5)

        full_a = by_columns(jnp.concatenate([w_qkv, w_out], axis=1))
        full_1 = by_columns(w_fc1)
        full_2 = lax.all_gather(w_fc2, "fsdp", axis=0, tiled=True)
        full_2 = full_2.reshape(4, 2, 2, 2, piece, width).transpose(2, 3, 0, 1, 4, 5)
        forward = forward_call(dims, pad, False)(lengths, vec, tokens, cotangent, full_a, full_1, full_2)
        out, n1, qkv, prob, mixed, resid, n2, act, slope, gffn, acc, vec = forward
    backward = backward_call(dims, pad, comm)(
        lengths, vec, acc, tokens, cotangent, full_a, full_1, full_2, n1, qkv, prob, mixed, resid, n2, act, slope, gffn
    )
    if comm:
        grad_tokens, sum_qkv, sum_out, sum_1, sum_2, sums = backward
        sum_2 = sum_2.reshape(-1, width)
    else:
        grad_tokens, da, d1, d2, sums = backward

        def total(array):
            part = lax.psum_scatter(array, "fsdp", scatter_dimension=0, tiled=True)
            return lax.psum(part, "dp")

        d1 = d1.transpose(2, 3, 4, 0, 1, 5).reshape(width, hidden)
        d2 = d2.transpose(2, 3, 0, 1, 4, 5).reshape(hidden, width)
        first = da[..., : width // 2].transpose(2, 3, 4, 0, 1, 5).reshape(width, 4, 3, 128)
        second = da[..., width // 2 :].transpose(2, 3, 4, 0, 1, 5).reshape(width, 4, 3, 128)
        heads = jnp.concatenate([first[:, :2], second], axis=1).transpose(0, 2, 1, 3).reshape(width, 3 * width)
        sum_a = total(jnp.concatenate([heads, first[:, 2:].reshape(width, width)], axis=1))
        sum_qkv, sum_out = sum_a[:, : 3 * width], sum_a[:, 3 * width :]
        sum_1, sum_2 = total(d1), total(d2)
        sums = lax.psum(sums, ("fsdp", "dp"))
    own_piece = width // fsdp
    mine = lax.dynamic_slice(sums, (0, me * own_piece), (FB1_ROW, own_piece))
    bias_sums = sums[FB1_ROW : FB1_ROW + hidden // width].reshape(-1)
    bias_one = lax.dynamic_slice(bias_sums, (me * (hidden // fsdp),), (hidden // fsdp,))
    return (
        out, grad_tokens, mine[G1_ROW], mine[B1_ROW], sum_qkv.astype(F32),
        jnp.stack([mine[QB_ROW], mine[VB_ROW]], axis=1), sum_out.astype(F32), mine[OB_ROW], mine[SA_ROW],
        mine[G2_ROW], mine[B2_ROW], sum_1.astype(F32), bias_one, sum_2.astype(F32), mine[FB2_ROW], mine[SF_ROW],
    )


def solution(mesh):
    both, one, two = P(("fsdp", "dp"), None), P("fsdp"), P("fsdp", None)
    in_specs = (both, both, both, one, one, two, two, two, one, one, one, one, two, one, two, one, one)
    out_specs = (both, both, one, one, two, two, two, one, one, one, one, two, one, two, one, one)
    run = functools.partial(local, mesh.shape["fsdp"], mesh.shape["dp"])
    return jax.shard_map(run, mesh=mesh, in_specs=in_specs, out_specs=out_specs, check_vma=False)
```

```python
import functools
import math

import jax
import jax.numpy as jnp
from jax import lax
from jax.experimental import pallas as pl
from jax.experimental.pallas import tpu as pltpu
from jax.sharding import PartitionSpec as P

HEAD_DIM = 64
norm_eps = 1e-06
masked_score = -1e30
BF = jnp.bfloat16
F32 = jnp.float32
TILE = 256
QB = 128
VMEM_LIMIT = 67043328

MESH = pl.DeviceIdType.MESH
SHARED = 64

G1_ROW, B1_ROW, QB_ROW, VB_ROW, OB_ROW, SA_ROW, G2_ROW, B2_ROW, FB2_ROW, SF_ROW, FB1_ROW = range(11)
VEC_ROWS = 16


def mm(a, b):
    return lax.dot_general(a, b, (((1,), (0,)), ((), ())), preferred_element_type=F32)


def mm_bt(a, b):
    return lax.dot_general(a, b, (((1,), (1,)), ((), ())), preferred_element_type=F32)


def mm_at(a, b):
    return lax.dot_general(a, b, (((0,), (0,)), ((), ())), preferred_element_type=F32)


def norm_parts(values):
    centered = values - jnp.mean(values, axis=-1, keepdims=True)
    spread = jnp.mean(centered * centered, axis=-1, keepdims=True)
    inv = lax.rsqrt(spread + norm_eps)
    return centered * inv, inv


def window(block, blocks):
    first = max(block - 1, 0)
    last = min(block + 2, blocks)
    return first * QB, (last - first) * QB


def prob_offsets(blocks):
    offsets, total = [], 0
    for block in range(blocks):
        offsets.append(total)
        total += window(block, blocks)[1]
    return offsets, total


def lane_tile(values, times):
    return jnp.concatenate([values] * times, axis=1) if times > 1 else values


def fill_segments(lengths_ref, rows, slots, seg_col, seg_row):
    count = lengths_ref.shape[1]
    for r in range(rows):
        down = lax.broadcasted_iota(jnp.int32, (slots, 128), 0)
        along = lax.broadcasted_iota(jnp.int32, (8, slots), 1)
        col = jnp.zeros((slots, 128), jnp.int32)
        row = jnp.zeros((8, slots), jnp.int32)
        end = jnp.int32(0)
        for j in range(count):
            end = end + lengths_ref[r, j]
            col = col + (down >= end).astype(jnp.int32)
            row = row + (along >= end).astype(jnp.int32)
        seg_col[pl.ds(r * slots, slots), :] = col
        seg_row[r] = row


def attention_forward(rows, slots, pairs, width, qkv, seg_col, seg_row, prob_slot, mixed, r, pair):
    blocks = slots // QB
    offsets, _ = prob_offsets(blocks)
    low = lax.broadcasted_iota(jnp.int32, (QB, 128), 1) < HEAD_DIM
    col = pl.multiple_of(pair * 128, 128)
    base = pl.multiple_of(r * slots, slots)
    zero = jnp.zeros((QB, 128), BF)
    for b in range(blocks):
        start, wide = window(b, blocks)
        q = qkv[pl.ds(base + b * QB, QB), pl.ds(col, 128)]
        k = qkv[pl.ds(base + start, wide), pl.ds(width + col, 128)]
        v = qkv[pl.ds(base + start, wide), pl.ds(2 * width + col, 128)]
        same = lane_tile(seg_col[pl.ds(base + b * QB, QB), :], wide // 128) == seg_row[r, 0:1, start : start + wide]
        q2 = jnp.concatenate([jnp.where(low, q, zero), jnp.where(low, zero, q)], axis=0)
        scores = mm_bt(q2, k)
        scores = jnp.concatenate(
            [jnp.where(same, scores[:QB], masked_score), jnp.where(same, scores[QB:], masked_score)], axis=0
        )
        peak = jnp.max(scores, axis=-1, keepdims=True)
        weights = jnp.exp(scores - peak)
        total = jnp.sum(weights, axis=-1, keepdims=True)
        probs = (weights * (1.0 / total)).astype(BF)
        prob_slot[:, offsets[b] : offsets[b] + wide] = probs
        out = mm(probs, v)
        mixed[pl.ds(base + b * QB, QB), pl.ds(col, 128)] = jnp.where(low, out[:QB], out[QB:]).astype(BF)


def attention_backward(rows, slots, pairs, width, qkv, prob_slot, mixed, grad_mixed, grads, r, pair):
    blocks = slots // QB
    offsets, _ = prob_offsets(blocks)
    low = lax.broadcasted_iota(jnp.int32, (QB, 128), 1) < HEAD_DIM
    low_all = lax.broadcasted_iota(jnp.int32, (slots, 128), 1) < HEAD_DIM
    factor = 1.0 / math.sqrt(HEAD_DIM)
    col = pl.multiple_of(pair * 128, 128)
    base = pl.multiple_of(r * slots, slots)
    zero = jnp.zeros((QB, 128), BF)
    grad_k = [None] * blocks
    grad_v = [None] * blocks
    for b in range(blocks):
        start, wide = window(b, blocks)
        q = qkv[pl.ds(base + b * QB, QB), pl.ds(col, 128)]
        k = qkv[pl.ds(base + start, wide), pl.ds(width + col, 128)]
        v = qkv[pl.ds(base + start, wide), pl.ds(2 * width + col, 128)]
        up = grad_mixed[pl.ds(base + b * QB, QB), pl.ds(col, 128)]
        out = mixed[pl.ds(base + b * QB, QB), pl.ds(col, 128)]
        probs = prob_slot[:, offsets[b] : offsets[b] + wide]
        q2 = jnp.concatenate([jnp.where(low, q, zero), jnp.where(low, zero, q)], axis=0)
        up2 = jnp.concatenate([jnp.where(low, up, zero), jnp.where(low, zero, up)], axis=0)
        out2 = jnp.concatenate([out, out], axis=0)
        inner = jnp.sum(up2.astype(F32) * out2.astype(F32), axis=-1, keepdims=True)
        grad_probs = mm_bt(up2, v)
        grad_scores = (probs.astype(F32) * (grad_probs - inner)).astype(BF)
        grad_q = mm(grad_scores, k) * factor
        grads[pl.ds(base + b * QB, QB), pl.ds(col, 128)] = jnp.where(low, grad_q[:QB], grad_q[QB:]).astype(BF)
        dk = mm_at(grad_scores, q2)
        dv = mm_at(probs, up2)
        for i in range(wide // QB):
            kb = start // QB + i
            piece_k, piece_v = dk[i * QB : (i + 1) * QB], dv[i * QB : (i + 1) * QB]
            grad_k[kb] = piece_k if grad_k[kb] is None else grad_k[kb] + piece_k
            grad_v[kb] = piece_v if grad_v[kb] is None else grad_v[kb] + piece_v
        done = [b - 1] if b > 0 else []
        if b == blocks - 1:
            done.append(b)
        for kb in done:
            grads[pl.ds(base + kb * QB, QB), pl.ds(width + col, 128)] = grad_k[kb].astype(BF)
            grads[pl.ds(base + kb * QB, QB), pl.ds(2 * width + col, 128)] = grad_v[kb].astype(BF)


def fold(values):
    return jnp.sum(values.reshape(values.shape[0] // 8, 8, values.shape[1]), axis=0)


def gelu_parts(values):
    cdf = 0.5 * (1.0 + lax.erf(values * math.sqrt(0.5)))
    pdf = jnp.exp(-0.5 * values * values) * (1.0 / math.sqrt(2.0 * math.pi))
    return values * cdf, cdf + values * pdf


def block(ref, c):
    value = ref[c // 2, c % 2]
    return value.reshape(-1, value.shape[-1])


def hidden_rows(ref, z):
    return jnp.concatenate([ref[x, c, z, y] for y in range(2) for x in range(2) for c in range(2)], axis=0)


def run_hooks(hooks, step):
    for k, turns in sorted(hooks.items()):

        @pl.when(step == k)
        def _(turns=turns):
            for turn in turns:
                turn()


def forward_phases(dims, refs):
    rows, slots, width, hidden = dims
    tokens = rows * slots
    tiles = tokens // TILE
    pairs = width // 128
    vec = refs["vec"]

    def row_of(i):
        return vec[i : i + 1, :].astype(F32)

    def norm_one(hooks):
        gain, shift = row_of(G1_ROW), row_of(B1_ROW)

        def body(i, _):
            at = pl.ds(pl.multiple_of(i * TILE, TILE), TILE)
            hat, _inv = norm_parts(refs["tok"][at, :])
            refs["n1"][at, :] = (hat * gain + shift).astype(BF)
            run_hooks(hooks, i)
            return 0

        lax.fori_loop(0, tiles, body, 0)

    def project(hooks):
        q_bias, v_bias = row_of(QB_ROW), row_of(VB_ROW)
        factor = 1.0 / math.sqrt(HEAD_DIM)

        def body(i, _):
            at = pl.ds(pl.multiple_of(i * TILE, TILE), TILE)
            normed = refs["n1"][at, :]
            query = (mm(normed, block(refs["wa"], 0)) + q_bias).astype(BF)
            refs["qkv"][at, :width] = (query.astype(F32) * factor).astype(BF)
            refs["qkv"][at, width : 2 * width] = mm(normed, block(refs["wa"], 1)).astype(BF)
            refs["qkv"][at, 2 * width : 3 * width] = (
                mm(normed, block(refs["wa"], 2)) + v_bias
            ).astype(BF)
            run_hooks(hooks, i)
            return 0

        lax.fori_loop(0, tiles, body, 0)

    def attend(hooks):
        steps = rows * pairs

        def out_copy(step):
            slot = lax.rem(step, 2)
            return pltpu.make_async_copy(refs["slot"].at[slot], refs["prob_out"].at[step], refs["slot_sem"].at[slot])

        def body(step, _):
            @pl.when(step >= 2)
            def _():
                out_copy(step - 2).wait()

            attention_forward(
                rows, slots, pairs, width, refs["qkv"], refs["seg_col"], refs["seg_row"],
                refs["slot"].at[lax.rem(step, 2)], refs["mixed"], lax.rem(step, rows), lax.div(step, rows),
            )
            out_copy(step).start()
            run_hooks(hooks, step)
            return 0

        lax.fori_loop(0, steps, body, 0)
        out_copy(steps - 2).wait()
        out_copy(steps - 1).wait()

    def feed_one(hooks):
        out_bias, scale_one = row_of(OB_ROW), row_of(SA_ROW)
        gain, shift = row_of(G2_ROW), row_of(B2_ROW)

        def body(i, _):
            at = pl.ds(pl.multiple_of(i * TILE, TILE), TILE)
            attn = mm(refs["mixed"][at, :], block(refs["wa"], 3)) + out_bias
            resid = refs["tok"][at, :] + scale_one * attn
            refs["resid"][at, :] = resid
            hat, _inv = norm_parts(resid)
            normed = (hat * gain + shift).astype(BF)
            refs["n2"][at, :] = normed
            for c in range(hidden // width):
                cols = slice(c * width, (c + 1) * width)
                pre = mm(normed, block(refs["w1"], c)) + row_of(FB1_ROW + c)
                act, slope = gelu_parts(pre)
                refs["act"][at, cols] = act.astype(BF)
                refs["slope"][at, cols] = slope.astype(BF)
            refs["tile_one"](i)
            run_hooks(hooks, i)
            return 0

        lax.fori_loop(0, tiles, body, 0)

    def feed_two():
        bias_two, scale_two = row_of(FB2_ROW), row_of(SF_ROW)
        refs["acc"][...] = jnp.zeros_like(refs["acc"])

        def body(i, _):
            at = pl.ds(pl.multiple_of(i * TILE, TILE), TILE)
            ffn = mm(refs["act"][at, :], jnp.concatenate([hidden_rows(refs["w2"], z) for z in range(4)], axis=0)) + bias_two
            valid = lane_tile(refs["seg_col"][at, :], width // 128) < refs["pad"]
            up = jnp.where(valid, refs["cot"][at, :], 0.0)
            grad = (scale_two * up).astype(BF)
            refs["gffn"][at, :] = grad
            refs["acc"][0] += fold(up * ffn)
            refs["acc"][1] += fold(grad.astype(F32))
            refs["tok"][at, :] = refs["resid"][at, :] + scale_two * ffn
            refs["tile_two"](i)
            return 0

        lax.fori_loop(0, tiles, body, 0)

    return norm_one, project, attend, feed_one, feed_two


def backward_phases(dims, refs):
    rows, slots, width, hidden = dims
    tokens = rows * slots
    tiles = tokens // TILE
    pairs = width // 128
    parts = hidden // width
    vec, acc = refs["vec"], refs["acc"]
    half = width // 2
    piece = width // 8

    def row_of(i):
        return vec[i : i + 1, :].astype(F32)

    def weight_two():
        per = hidden // 8

        def body(i, _):
            at = pl.ds(pl.multiple_of(i * per, per), per)
            grad = mm_at(refs["act"][:, at], refs["gffn"][...]).astype(BF)
            refs["d2"][:, :, lax.div(i, 2), lax.rem(i, 2)] = grad.reshape(2, 2, per // 4, width)
            return 0

        lax.fori_loop(0, 8, body, 0)

    def through_ffn(hooks):
        gain, scale_one = row_of(G2_ROW), row_of(SA_ROW)

        def body(i, _):
            at = pl.ds(pl.multiple_of(i * TILE, TILE), TILE)
            grad_ffn = refs["gffn"][at, :]
            for c in range(parts):
                cols = slice(c * width, (c + 1) * width)
                grad_act = mm_bt(grad_ffn, hidden_rows(refs["w2"], c))
                pre = (grad_act * refs["slope"][at, cols].astype(F32)).astype(BF)
                refs["slope"][at, cols] = pre
                acc[FB1_ROW + c] += fold(pre.astype(F32))
            grad = mm_bt(refs["slope"][at, :], jnp.concatenate([block(refs["w1"], c) for c in range(parts)], axis=1))
            hat, inv = norm_parts(refs["resid"][at, :])
            acc[G2_ROW] += fold(grad * hat)
            acc[B2_ROW] += fold(grad)
            u = grad * gain
            back = inv * (u - jnp.mean(u, axis=-1, keepdims=True) - hat * jnp.mean(u * hat, axis=-1, keepdims=True))
            valid = lane_tile(refs["seg_col"][at, :], width // 128) < refs["pad"]
            grad_resid = jnp.where(valid, refs["cot"][at, :], 0.0) + back
            refs["resid"][at, :] = grad_resid
            grad_proj = (scale_one * grad_resid).astype(BF)
            refs["gproj"][at, :] = grad_proj
            acc[OB_ROW] += fold(grad_proj.astype(F32))
            refs["gmixed"][at, :] = mm_bt(grad_proj, block(refs["wa"], 3)).astype(BF)
            run_hooks(hooks, i)
            return 0

        lax.fori_loop(0, tiles, body, 0)

    def weight_one(side):
        def body(i, _):
            at = pl.ds(pl.multiple_of(i * half, half), half)
            for c in range(parts):
                first = c * width + side * half
                grad = mm_at(refs["n2"][:, at], refs["slope"][:, first : first + half]).astype(BF)
                refs["d1"][c // 2, c % 2, pl.ds(i * 2, 2), :, :, side * half : (side + 1) * half] = grad.reshape(
                    2, 2, piece, half
                )
            return 0

        lax.fori_loop(0, 2, body, 0)

    def weight_out():
        def body(i, _):
            at = pl.ds(pl.multiple_of(i * half, half), half)
            grad = mm_at(refs["mixed"][:, at], refs["gproj"][...])
            low = grad.astype(BF)
            for j in range(2):
                refs["da0"][1, j, pl.ds(i * 2, 2)] = low[:, j * half : (j + 1) * half].reshape(2, 2, piece, half)
            w_out = refs["wa"][1, 1, pl.ds(i * 2, 2)].reshape(half, width)
            acc[SA_ROW] += fold(grad * w_out.astype(F32))
            return 0

        lax.fori_loop(0, 2, body, 0)

    def attend_back(first, last, hooks):
        def in_copy(step):
            slot = lax.rem(step, 2)
            return pltpu.make_async_copy(refs["prob_in"].at[step], refs["slot"].at[slot], refs["slot_sem"].at[slot])

        if first == 0:
            in_copy(0).start()

        def body(step, _):
            @pl.when(step + 1 < rows * pairs)
            def _():
                in_copy(step + 1).start()

            in_copy(step).wait()
            attention_backward(
                rows, slots, pairs, width, refs["qkv"], refs["slot"].at[lax.rem(step, 2)], refs["mixed"],
                refs["gmixed"], refs["qkv"], lax.rem(step, rows), lax.div(step, rows),
            )
            run_hooks(hooks, step)
            return 0

        lax.fori_loop(first, last, body, 0)

    def weight_slabs(target, slabs, per):
        wide = per * 128

        def body(i, _):
            at = pl.ds(pl.multiple_of(i * half, half), half)
            found = [refs["qkv"][:, part * width + p * 128 : part * width + (p + 1) * 128] for part, p in slabs]
            grad = mm_at(refs["n1"][:, at], jnp.concatenate(found, axis=1)).astype(BF)
            for j in range(len(slabs) // per):
                target[j // 2, j % 2, pl.ds(i * 2, 2)] = grad[:, j * wide : (j + 1) * wide].reshape(2, 2, piece, wide)
            return 0

        lax.fori_loop(0, 2, body, 0)

    def finish_tokens(hooks):
        gain = row_of(G1_ROW)

        def body(i, _):
            at = pl.ds(pl.multiple_of(i * TILE, TILE), TILE)
            grad = mm_bt(refs["qkv"][at, :], jnp.concatenate([block(refs["wa"], c) for c in range(3)], axis=1))
            hat, inv = norm_parts(refs["tok"][at, :])
            acc[G1_ROW] += fold(grad * hat)
            acc[B1_ROW] += fold(grad)
            acc[QB_ROW] += fold(refs["qkv"][at, :width].astype(F32))
            acc[VB_ROW] += fold(refs["qkv"][at, 2 * width :].astype(F32))
            u = grad * gain
            back = inv * (u - jnp.mean(u, axis=-1, keepdims=True) - hat * jnp.mean(u * hat, axis=-1, keepdims=True))
            refs["tok"][at, :] = refs["resid"][at, :] + back
            refs["tile_out"](i)
            run_hooks(hooks, i)
            return 0

        lax.fori_loop(0, tiles, body, 0)

    def vector_sums():
        lines = [jnp.sum(acc[i], axis=0, keepdims=True) for i in range(VEC_ROWS)]
        lines[SA_ROW] = (lines[SA_ROW] + row_of(OB_ROW) * lines[OB_ROW]) / row_of(SA_ROW)
        return jnp.concatenate(lines, axis=0)

    return weight_two, through_ffn, weight_one, weight_out, attend_back, weight_slabs, finish_tokens, vector_sums


ANY = pl.BlockSpec(memory_space=pl.ANY)
INSIDE = pl.BlockSpec(memory_space=pltpu.VMEM)
SCALARS = pl.BlockSpec(memory_space=pltpu.SMEM)
DMA = pltpu.SemaphoreType.DMA


def position():
    f, d = lax.axis_index("fsdp"), lax.axis_index("dp")
    return lax.div(f, 2), lax.rem(f, 2), lax.div(d, 2), lax.rem(d, 2)


def device(z, y, x, c):
    return (z * 2 + y, x * 2 + c)


def z_partners(z):
    return [z + 1 - 2 * lax.rem(z, 2), 3 - z, lax.rem(z + 2, 4)]


def remote(src, dst, send, recv, target):
    return pltpu.make_async_remote_copy(
        src_ref=src, dst_ref=dst, send_sem=send, recv_sem=recv, device_id=target, device_id_type=MESH
    )


def greet(targets):
    barrier = pltpu.get_barrier_semaphore()
    for target in targets:
        pl.semaphore_signal(barrier, inc=1, device_id=target, device_id_type=MESH)
    pl.semaphore_wait(barrier, len(targets))


class Gather:
    def __init__(self, t, buf, sems, place):
        self.t, self.buf, self.place = t, buf, place
        self.zs, self.zr, self.ys, self.yr, self.xs, self.xr, self.cs, self.cr = sems
        z = place[0]
        low = z < 2
        self.others = [z + 1 - 2 * lax.rem(z, 2), jnp.where(low, 2, 1), jnp.where(low, 3, 0)]
        self.inner = jnp.logical_or(z == 1, z == 2)

    def shard(self, j):
        z, y, _, _ = self.place
        if j == 7:
            return z, y
        if j < 3:
            return self.others[j], y
        return (z if j == 3 else self.others[j - 4]), 1 - y

    def part(self, z, y, p):
        _, _, x, c = self.place
        rows = self.buf.shape[4]
        if p == 0:
            return self.buf.at[x, c, z, y, pl.ds(0, SHARED)]
        return self.buf.at[:, c, z, y, pl.ds(SHARED, rows - SHARED)]

    def z_copy(self, origin, i, p, target):
        _, y, x, c = self.place
        ref = self.part(origin, y, p)
        return remote(ref, ref, self.zs.at[self.t, i, p], self.zr.at[self.t, origin, p], device(target, y, x, c))

    def outward(self, k, p):
        z = self.place[0]
        return self.z_copy(self.others[k], 2 + k, p, 3 - z if k == 0 else self.others[0])

    def y_copy(self, j, p):
        z, y, x, c = self.place
        zs, ys = self.shard(j)
        ref = self.part(zs, ys, p)
        return remote(ref, ref, self.ys.at[self.t, zs, p], self.yr.at[self.t, zs, p], device(z, 1 - y, x, c))

    def x_copy(self, j, qx):
        z, y, x, c = self.place
        zs, ys = self.shard(j)
        s = zs * 2 + ys
        ref = self.buf.at[qx, c, zs, ys, pl.ds(0, SHARED)]
        return remote(ref, ref, self.xs.at[self.t, s], self.xr.at[self.t, s], device(z, y, 1 - x, c))

    def c_copy(self, j, qx, qc):
        z, y, x, c = self.place
        zs, ys = self.shard(j)
        s = zs * 2 + ys
        ref = self.buf.at[qx, qc, zs, ys]
        return remote(ref, ref, self.cs.at[self.t, s, qx], self.cr.at[self.t, s, qx], device(z, y, x, 1 - c))

    def onward(self, j, p):
        _, _, x, c = self.place
        if p == 0:
            self.x_copy(j, x).start()
        else:
            self.c_copy(j, x, c).start()

    def send_z(self):
        z = self.place[0]
        for p in range(2):
            self.z_copy(z, 0, p, self.others[0]).start()

        @pl.when(self.inner)
        def _():
            for p in range(2):
                self.z_copy(z, 1, p, 3 - z).start()

    def send_y(self):
        for p in range(2):
            self.y_copy(7, p).start()

    def z_step(self, k, p):
        self.z_copy(self.others[k], 0, p, self.others[0]).wait_recv()

        @pl.when(self.inner)
        def _():
            self.outward(k, p).start()

        self.y_copy(k, p).start()
        self.onward(k, p)

    def y_step(self, k, p):
        self.y_copy(3 + k, p).wait_recv()
        self.onward(3 + k, p)

    def x_step(self, j):
        _, _, x, c = self.place
        self.x_copy(j, 1 - x).wait_recv()
        self.c_copy(j, 1 - x, c).start()

    def done(self):
        _, _, x, c = self.place
        for j in range(7):
            for qx in (x, 1 - x):
                self.c_copy(j, qx, 1 - c).wait_recv()

    def finish(self):
        z, _, x, c = self.place
        for p in range(2):
            self.z_copy(z, 0, p, self.others[0]).wait_send()

        @pl.when(self.inner)
        def _():
            for p in range(2):
                self.z_copy(z, 1, p, 3 - z).wait_send()
                for k in range(3):
                    self.outward(k, p).wait_send()

        for j in (7, 0, 1, 2):
            for p in range(2):
                self.y_copy(j, p).wait_send()
        for j in range(7):
            self.x_copy(j, x).wait_send()
            for qx in (x, 1 - x):
                self.c_copy(j, qx, c).wait_send()


START_TURNS = ("asz", "asy")
NORM_TURNS = {
    0: ("az00", "az10"),
    1: ("az11", "ay00", "ay01"),
    2: ("az20", "az01", "ax0", "az21", "bsz", "bsy", "ay10", "ax1", "ay20", "ax2", "ax3", "ay21"),
    3: ("ay30", "ay11", "ax5", "ay31", "bz10", "ax4", "ax6", "bz00", "by00", "bz01", "bz11"),
}
PROJECT_TURNS = {
    0: ("by01",),
    1: ("bz20",),
    3: ("by10", "bz21", "csz", "by20", "bx1"),
}
ATTEND_TURNS = {
    0: ("bx2", "csy"),
    1: ("bx0",),
    2: ("bx3",),
    4: ("by30", "by11", "cz10"),
    6: ("by21", "cz00"),
    7: ("by31", "bx6", "cz01", "cy00"),
    8: ("bx5",),
    9: ("cz20", "bx4"),
    11: ("cy10", "cz21", "cy01"),
}
FEED_TURNS = {
    0: ("cx3", "cx2", "cy20", "cy30", "cx0", "cz11", "cx1"),
    2: ("cy21", "cy31", "cy11", "cx6", "cx4", "cx5"),
}


def turn(gathers, name):
    gather, kind = gathers["abc".index(name[0])], name[1:]
    if kind == "sz":
        return gather.send_z
    if kind == "sy":
        return gather.send_y
    if kind[0] == "x":
        return functools.partial(gather.x_step, int(kind[1]))
    step = gather.z_step if kind[0] == "z" else gather.y_step
    return functools.partial(step, int(kind[1]), int(kind[2]))


def turns(gathers, table):
    return {k: [turn(gathers, name) for name in names] for k, names in table.items()}


def forward_kernel(dims, pad, comm, *all_refs):
    rows, slots, width, hidden = dims
    tokens = rows * slots
    tiles = tokens // TILE
    all_refs = list(all_refs)
    take = lambda n: [all_refs.pop(0) for _ in range(n)]
    lengths, vec_in, tok_in, cot_in = take(4)
    wqkv_in, wout_in, w1_in, w2_in = take(4) if comm else [None] + take(3)
    out, n1_out, qkv_out, prob_out, mixed_out, resid_out, n2_out, act_out, slope_out, gffn_out, acc, vec = take(12)
    weights_out = take(3) if comm else []
    tok, cot, wa, w1, w2, n1, qkv, slot, mixed, resid, n2, act, slope, gffn, seg_col, seg_row = take(16)
    slot_sem, in_sem, out_sem, tile_sem = take(4)
    moves = [(tok_in, tok), (cot_in, cot)]
    if comm:
        place = position()
        z, y, x, c = place
        vec_land, vs, vr = take(3)
        sems = take(8)
        ga, g1, g2 = [Gather(t, buf, sems, place) for t, buf in enumerate((wa, w1, w2))]
        for q in range(4):
            source = wqkv_in.at[:, q * width : (q + 1) * width] if q < 3 else wout_in
            moves.append((source, wa.at[q // 2, q % 2, z, y]))
        for q in range(4):
            moves.append((w1_in.at[:, q * width : (q + 1) * width], w1.at[q // 2, q % 2, z, y]))
        moves.append((w2_in, w2.at[:, :, z, y]))
    else:
        moves += [(wout_in, wa), (w1_in, w1), (w2_in, w2)]
    loads = [pltpu.make_async_copy(a, b, in_sem.at[i]) for i, (a, b) in enumerate(moves)]
    for copy in loads[2:] + loads[:2]:
        copy.start()

    def tile_copies(i, pairs, base):
        at = pl.ds(pl.multiple_of(i * TILE, TILE), TILE)
        return [pltpu.make_async_copy(a.at[at], b.at[at], tile_sem.at[i, base + j]) for j, (a, b) in enumerate(pairs)]

    ones = [(resid, resid_out), (n2, n2_out), (act, act_out), (slope, slope_out)]
    twos = [(tok, out), (gffn, gffn_out)]

    def tile_one(i):
        for copy in tile_copies(i, ones, 0):
            copy.start()

    def tile_two(i):
        for copy in tile_copies(i, twos, len(ones)):
            copy.start()

    refs = dict(
        vec=vec, tok=tok, cot=cot, wa=wa, w1=w1, w2=w2, n1=n1, qkv=qkv, slot=slot, mixed=mixed, resid=resid, n2=n2,
        act=act, slope=slope, gffn=gffn, seg_col=seg_col, seg_row=seg_row, slot_sem=slot_sem, prob_out=prob_out,
        acc=acc, pad=pad, tile_one=tile_one, tile_two=tile_two,
    )
    norm_one, project, attend, feed_one, feed_two = forward_phases(dims, refs)
    pairs_out = [(n1, n1_out), (qkv, qkv_out), (mixed, mixed_out)]
    if comm:
        pairs_out += list(zip((wa, w1, w2), weights_out))
    stores = [pltpu.make_async_copy(a, b, out_sem.at[i]) for i, (a, b) in enumerate(pairs_out)]
    if comm:
        others = z_partners(z)
        peers = [device(o, y, x, c) for o in others] + [device(o, 1 - y, x, c) for o in [z] + others]
        greet(peers + [device(z, y, 1 - x, c), device(z, y, x, 1 - c)])
        mine = z * 2 + y
        vec_sends = [
            remote(vec_in, vec_land.at[mine], vs.at[k], vr.at[mine], peer) for k, peer in enumerate(peers)
        ]
        for copy in vec_sends:
            copy.start()
        gathers = (ga, g1, g2)
        for copy in loads[2:6]:
            copy.wait()
        for name in START_TURNS:
            turn(gathers, name)()
        fill_segments(lengths, rows, slots, seg_col, seg_row)
        vec_land[mine] = vec_in[...]
        vec[...] = jnp.zeros_like(vec)
        sources = [(o, y) for o in others] + [(o, 1 - y) for o in [z] + others]
        for k, (zs, ys) in enumerate(sources):
            remote(vec_in, vec_land.at[zs * 2 + ys], vs.at[k], vr.at[zs * 2 + ys], peers[k]).wait_recv()
        spread_vectors(vec_land, vec, width)
        for copy in loads[6:]:
            copy.wait()
        loads[0].wait()
        norm_one(turns(gathers, NORM_TURNS))
        stores[0].start()
        ga.done()
        stores[3].start()
        project(turns(gathers, PROJECT_TURNS))
        stores[1].start()
        attend(turns(gathers, ATTEND_TURNS))
        stores[2].start()
        g1.done()
        stores[4].start()
        feed_one(turns(gathers, FEED_TURNS))
        g2.done()
        stores[5].start()
        loads[1].wait()
        feed_two()
        for gather in (ga, g1, g2):
            gather.finish()
        for copy in vec_sends:
            copy.wait_send()
    else:
        fill_segments(lengths, rows, slots, seg_col, seg_row)
        vec[...] = vec_in[...].astype(F32)
        loads[0].wait()
        norm_one({})
        stores[0].start()
        loads[2].wait()
        project({})
        stores[1].start()
        attend({})
        stores[2].start()
        for copy in loads[3:] + loads[1:2]:
            copy.wait()
        feed_one({})
        feed_two()
    for copy in stores:
        copy.wait()

    def finish(i, _):
        for copy in tile_copies(i, ones, 0) + tile_copies(i, twos, len(ones)):
            copy.wait()
        return 0

    lax.fori_loop(0, tiles, finish, 0)


def spread_vectors(land, vec, width):
    shards = land.shape[0]
    piece = width // shards
    lines = jnp.concatenate([land[s].astype(F32)[:FB1_ROW, :piece] for s in range(shards)], axis=1)
    vec[:FB1_ROW, :] = lines
    per = 3
    tiles = [land[s, FB1_ROW + j : FB1_ROW + j + 1, :].astype(F32) for s in range(shards) for j in range(per)]
    wide = width // 128
    for r in range(len(tiles) // wide):
        vec[FB1_ROW + r : FB1_ROW + r + 1, :] = jnp.concatenate(tiles[r * wide : (r + 1) * wide], axis=1)


def forward_call(dims, pad, comm):
    rows, slots, width, hidden = dims
    tokens = rows * slots
    tiles, pairs = tokens // TILE, width // 128
    piece = width // 8
    wide = prob_offsets(slots // QB)[1]
    S = jax.ShapeDtypeStruct
    matrix = (2, 2, 4, 2, piece, width)
    shapes = [
        S((tokens, width), F32), S((tokens, width), BF), S((tokens, 3 * width), BF),
        S((rows * pairs, 2 * QB, wide), BF), S((tokens, width), BF), S((tokens, width), F32), S((tokens, width), BF),
        S((tokens, hidden), BF), S((tokens, hidden), BF), S((tokens, width), BF), S((2, 8, width), F32),
        S((VEC_ROWS, width), F32),
    ]
    V = pltpu.VMEM
    scratch = [
        V((tokens, width), F32), V((tokens, width), F32), V(matrix, BF), V(matrix, BF), V(matrix, BF),
        V((tokens, width), BF), V((tokens, 3 * width), BF), V((2, 2 * QB, wide), BF),
        V((tokens, width), BF), V((tokens, width), F32), V((tokens, width), BF), V((tokens, hidden), BF),
        V((tokens, hidden), BF), V((tokens, width), BF), V((tokens, 128), jnp.int32), V((rows, 8, slots), jnp.int32),
        DMA((2,)), DMA((11,)), DMA((6,)), DMA((tiles, 6)),
    ]
    params = dict(vmem_limit_bytes=VMEM_LIMIT)
    if comm:
        shapes += [S(matrix, BF)] * 3
        scratch += [V((8, VEC_ROWS, 128), BF), DMA((7,)), DMA((8,))]
        scratch += [DMA((3, 5, 2)), DMA((3, 4, 2)), DMA((3, 4, 2)), DMA((3, 4, 2)), DMA((3, 8)), DMA((3, 8)),
                    DMA((3, 8, 2)), DMA((3, 8, 2))]
        params.update(collective_id=0, has_side_effects=True)
    return pl.pallas_call(
        functools.partial(forward_kernel, dims, pad, comm),
        out_shape=shapes,
        in_specs=[SCALARS, INSIDE] + [ANY] * (6 if comm else 5),
        out_specs=[ANY] * 10 + [INSIDE, INSIDE] + ([ANY] * 3 if comm else []),
        scratch_shapes=scratch,
        compiler_params=pltpu.CompilerParams(**params),
        name="forward",
    )


class Reduce:
    def __init__(self, t, grad, land, final, sems, place):
        self.t, self.grad, self.final, self.place = t, grad, final, place
        self.from_core, self.from_x, self.from_y, self.from_yx, self.from_xy, self.from_z = land
        self.send, self.recv = sems
        rows = grad.shape[4]
        self.first, self.second = pl.ds(0, rows // 2), pl.ds(rows // 2, rows // 2)

    def copy(self, i, src, dst, target, slot=None):
        slot = i if slot is None else slot
        return remote(src, dst, self.send.at[self.t, i], self.recv.at[self.t, slot], target)

    def core_copy(self):
        z, y, x, c = self.place
        return [
            self.copy(i, self.grad.at[q, 1 - c], self.from_core.at[q], device(z, y, x, 1 - c)) for i, q in enumerate((0, 1))
        ]

    def one_copy(self):
        z, y, x, c = self.place
        g = self.grad
        return [
            self.copy(2, g.at[1 - x, c, :, :, self.first], self.from_x, device(z, y, 1 - x, c)),
            self.copy(3, g.at[:, c, :, 1 - y, self.second], self.from_y, device(z, 1 - y, x, c)),
        ]

    def two_copy(self):
        z, y, x, c = self.place
        g = self.grad
        return [
            self.copy(4, g.at[x, c, :, 1 - y, self.first], self.from_xy, device(z, 1 - y, x, c)),
            self.copy(5, g.at[1 - x, c, :, y, self.second], self.from_yx, device(z, y, 1 - x, c)),
        ]

    def z_copy(self):
        z, y, x, c = self.place
        return [
            self.copy(6 + k, self.grad.at[x, c, o, y], self.from_z.at[k], device(o, y, x, c))
            for k, o in enumerate(z_partners(z))
        ]

    def across_copy(self):
        z, y, x, c = self.place
        own = self.final.at[x, c]
        return self.copy(9, own, own, device(z, y, 1 - x, c))

    def beside_copy(self):
        z, y, x, c = self.place
        own = self.final.at[x, c]
        return self.copy(10, own, own, device(z, y, x, 1 - c))

    def relay_copy(self):
        z, y, x, c = self.place
        other = self.final.at[1 - x, c]
        return self.copy(11, other, other, device(z, y, x, 1 - c))

    def start(self):
        for copy in self.core_copy():
            copy.start()

    def core_done(self):
        z, y, x, c = self.place
        for copy in self.core_copy():
            copy.wait_recv()

        def body(i, _):
            q, zs = lax.div(i, 4), lax.rem(i, 4)
            total = self.grad[q, c, zs].astype(F32) + self.from_core[q, zs].astype(F32)
            self.grad[q, c, zs] = total.astype(BF)
            return 0

        lax.fori_loop(0, 8, body, 0)
        for copy in self.one_copy():
            copy.start()

    def one_done(self):
        z, y, x, c = self.place
        g = self.grad
        for copy in self.one_copy():
            copy.wait_recv()

        def body(zs, _):
            total = g[x, c, zs, :, self.first].astype(F32) + self.from_x[zs].astype(F32)
            g[x, c, zs, :, self.first] = total.astype(BF)
            total = g[:, c, zs, y, self.second].astype(F32) + self.from_y[:, zs].astype(F32)
            g[:, c, zs, y, self.second] = total.astype(BF)
            return 0

        lax.fori_loop(0, 4, body, 0)
        for copy in self.two_copy():
            copy.start()

    def two_done(self):
        z, y, x, c = self.place
        g = self.grad
        for copy in self.two_copy():
            copy.wait_recv()

        def body(zs, _):
            total = g[x, c, zs, y, self.first].astype(F32) + self.from_xy[zs].astype(F32)
            g[x, c, zs, y, self.first] = total.astype(BF)
            total = g[x, c, zs, y, self.second].astype(F32) + self.from_yx[zs].astype(F32)
            g[x, c, zs, y, self.second] = total.astype(BF)
            return 0

        lax.fori_loop(0, 4, body, 0)
        for copy in self.z_copy():
            copy.start()

    def z_done(self):
        z, y, x, c = self.place
        for copy in self.z_copy():
            copy.wait_recv()
        total = self.grad[x, c, z, y].astype(F32)
        for k in range(3):
            total = total + self.from_z[k].astype(F32)
        self.final[x, c] = total.astype(BF)
        self.across_copy().start()
        self.beside_copy().start()

    def relay(self):
        self.across_copy().wait_recv()
        self.relay_copy().start()

    def done(self):
        self.beside_copy().wait_recv()
        self.relay_copy().wait_recv()

    def finish(self):
        copies = self.core_copy() + self.one_copy() + self.two_copy() + self.z_copy()
        for copy in copies + [self.across_copy(), self.beside_copy(), self.relay_copy()]:
            copy.wait_send()


class VectorSum:
    def __init__(self, ref, land, z_land, send, recv, place):
        self.ref, self.land, self.z_land, self.send, self.recv, self.place = ref, land, z_land, send, recv, place
        z, y, x, c = place
        targets = [device(z, y, x, 1 - c), device(z, y, 1 - x, c), device(z, 1 - y, x, c)]
        self.pair = [
            remote(ref.at[i], land.at[i], send.at[i], recv.at[i], target) for i, target in enumerate(targets)
        ]
        self.along = [
            remote(ref.at[3], z_land.at[z], send.at[3 + k], recv.at[3 + z], device(o, y, x, c))
            for k, o in enumerate(z_partners(z))
        ]

    def start(self, value):
        self.ref[0] = value
        self.pair[0].start()

    def step(self, i):
        self.pair[i].wait_recv()
        self.ref[i + 1] = self.ref[i] + self.land[i]
        if i < 2:
            self.pair[i + 1].start()
        else:
            for copy in self.along:
                copy.start()

    def done(self):
        z, y, x, c = self.place
        self.z_land[z] = self.ref[3]
        for k, o in enumerate(z_partners(z)):
            remote(
                self.ref.at[3], self.z_land.at[o], self.send.at[3 + k], self.recv.at[3 + o], device(o, y, x, c)
            ).wait_recv()
        total = self.z_land[0] + self.z_land[1]
        total = total + self.z_land[2]
        return total + self.z_land[3]

    def finish(self):
        for copy in self.pair + self.along:
            copy.wait_send()


CHUNKS = ("2a", "2b", "1a", "1b", "a", "b", "c")
AFTER_PHASE = {
    "two": ("2a.start",),
    "one": ("2b.one", "1a.start"),
    "other": ("1a.core",),
    "out": ("1b.start",),
    "a": ("a.start",),
    "c": ("c.start", "b.core"),
    "end": ("1b.z", "c.one", "v.start", "b.two", "v.0", "1b.relay", "2b.z", "c.two", "1a.z", "v.1", "1b.done", "a.z",
        "v.2", "b.z", "c.z", "2a.relay", "a.relay", "2b.relay", "c.relay", "1a.relay", "a.done", "b.relay", "b.done",
        "2a.done", "1a.done", "v.done", "c.done", "2b.done"),
}
WITHIN_PHASE = {
    "ffn": {
        0: ("2a.core",),
        1: ("2b.start",),
        2: ("2b.core", "2a.one"),
    },
    "attend": {
        0: ("2b.two",),
        2: ("1b.core",),
        3: ("1a.one",),
        5: ("2a.two", "a.core"),
        7: ("1a.two", "1b.one"),
        9: ("2a.z",),
        10: ("b.start", "1b.two", "a.one"),
    },
    "tokens": {
        0: ("c.core", "a.two"),
        2: ("b.one",),
    },
}


def backward_kernel(dims, pad, comm, *all_refs):
    rows, slots, width, hidden = dims
    tokens = rows * slots
    tiles, pairs = tokens // TILE, width // 128
    half = width // 2
    all_refs = list(all_refs)
    take = lambda n: [all_refs.pop(0) for _ in range(n)]
    lengths, vec, acc_in, tok_in, cot_in, wa_in, w1_in, w2_in = take(8)
    n1_in, qkv_in, prob_in, mixed_in, resid_in, n2_in, act_in, slope_in, gffn_in = take(9)
    if comm:
        gtok_out, gqkv_out, gout_out, g1_out, g2_out, sums = take(6)
    else:
        gtok_out, da_out, d1_out, d2_out, sums = take(5)
    cot, wa, w1, w2, slot, mixed, resid, n2, act, slope, gffn, gproj, d2, acc, seg_col, seg_row = take(16)
    slot_sem, in_sem, out_sem, tile_sem = take(4)
    qkv, n1, tok = act.at[:, : 3 * width], act.at[:, 3 * width :], cot
    da0, da1 = w2.at[:, :, :, :, :, :half], w2.at[:, :, :, :, :, half:]
    pair_slabs = [(part, p) for p in range(pairs) for part in range(3)]
    ahead, late = pair_slabs[:6], pair_slabs[6:]
    moves = [
        (act_in, act), (gffn_in, gffn), (w2_in, w2), (slope_in, slope), (w1_in, w1), (resid_in, resid), (cot_in, cot),
        (wa_in, wa), (n2_in, n2), (mixed_in, mixed), (qkv_in, qkv), (n1_in, n1), (tok_in, tok),
    ]
    loads = [pltpu.make_async_copy(a, b, in_sem.at[i]) for i, (a, b) in enumerate(moves)]
    for copy in loads[:10]:
        copy.start()

    def tile_copy(i):
        at = pl.ds(pl.multiple_of(i * TILE, TILE), TILE)
        return pltpu.make_async_copy(tok.at[at], gtok_out.at[at], tile_sem.at[i])

    refs = dict(
        vec=vec, acc=acc, tok=tok, cot=cot, wa=wa, w1=w1, w2=w2, n1=n1, qkv=qkv, slot=slot, mixed=mixed,
        resid=resid, n2=n2, act=act, slope=slope, gffn=gffn, gproj=gproj, gmixed=gffn, d2=d2, d1=w1, da0=da0, da1=da1,
        seg_col=seg_col, seg_row=seg_row, slot_sem=slot_sem, prob_in=prob_in, pad=pad,
        tile_out=lambda i: tile_copy(i).start(),
    )
    (
        weight_two, through_ffn, weight_one, weight_out, attend_back, weight_slabs, finish_tokens, vector_sums,
    ) = backward_phases(dims, refs)
    stores = []
    if comm:
        place = position()
        z, y, x, c = place
        core_land = take(2)
        lands = [take(5) for _ in CHUNKS]
        finals = take(len(CHUNKS))
        sems = take(2)
        vec_ref, vec_land, vec_z, vec_send, vec_recv, final_sem = take(6)
        sides = [(0, half), (half, half), (0, half), (half, half), (0, half), (half, 256), (half + 256, 128)]
        chunks = {}
        for t, (name, (first, wide)) in enumerate(zip(CHUNKS, sides)):
            side = (slice(None),) * 5 + (slice(first, first + wide),)
            grad, land = (d2, w1, w2)[t // 2 if t < 4 else 2], core_land[1 if name in ("1a", "1b") else 0]
            chunks[name] = Reduce(t, grad.at[side], [land.at[side[1:]]] + lands[t], finals[t], sems, place)
        vector = VectorSum(vec_ref, vec_land, vec_z, vec_send, vec_recv, place)
        greet([device(o, y, x, c) for o in z_partners(z)]
              + [device(z, 1 - y, x, c), device(z, y, 1 - x, c), device(z, y, x, 1 - c)])

    def targets(name):
        final = finals[CHUNKS.index(name)]
        if name in ("2a", "2b"):
            first = half * (name == "2b")
            return [(final, g2_out.at[:, :, :, first : first + half])]
        found = []
        for q in range(4):
            ref = final.at[q // 2, q % 2]
            if name in ("1a", "1b"):
                first = q * width + half * (name == "1b")
                found.append((ref, g1_out.at[:, first : first + half]))
            elif name == "a" and q >= 2:
                found.append((ref, gout_out.at[:, (q - 2) * half : (q - 1) * half]))
            else:
                slabs = {"a": ahead[q * 3 : q * 3 + 3], "b": late[q * 2 : q * 2 + 2], "c": late[8 + q : 9 + q]}[name]
                for j, (part, p) in enumerate(slabs):
                    at = part * width + p * 128
                    found.append((ref.at[:, j * 128 : (j + 1) * 128], gqkv_out.at[:, at : at + 128]))
        return found

    def deliver(name):
        chunks[name].done()
        for i, (a, b) in enumerate(targets(name)):
            copy = pltpu.make_async_copy(a, b, final_sem.at[CHUNKS.index(name), i])
            copy.start()
            stores.append(copy)

    def sum_vectors():
        sums[...] = vector.done()

    def turn_of(name):
        chunk, step = name.split(".")
        if chunk == "v":
            if step == "start":
                return lambda: vector.start(vector_sums())
            return sum_vectors if step == "done" else functools.partial(vector.step, int(step))
        if step == "done":
            return functools.partial(deliver, chunk)
        methods = dict(start="start", core="core_done", one="one_done", two="two_done", z="z_done", relay="relay")
        return getattr(chunks[chunk], methods[step])

    def after(phase):
        if comm:
            for name in AFTER_PHASE.get(phase, ()):
                turn_of(name)()

    def within(phase, first, last):
        table = WITHIN_PHASE.get(phase, {}) if comm else {}
        return {k: [turn_of(name) for name in names] for k, names in table.items() if first <= k < last}

    fill_segments(lengths, rows, slots, seg_col, seg_row)
    acc[...] = jnp.zeros_like(acc)
    acc[SF_ROW] = acc_in[0]
    acc[FB2_ROW] = acc_in[1]
    for copy in loads[:2]:
        copy.wait()
    weight_two()
    for copy in loads[10:12]:
        copy.start()
    after("two")
    for copy in loads[2:8]:
        copy.wait()
    through_ffn(within("ffn", 0, tiles))
    loads[12].start()
    loads[8].wait()
    for side in range(2):
        weight_one(side)
        after(("one", "other")[side])
    loads[9].wait()
    weight_out()
    after("out")
    loads[10].wait()
    early, most = rows * 2, rows * 5
    attend_back(0, early, within("attend", 0, early))
    loads[11].wait()
    weight_slabs(da0, ahead, 3)
    after("a")
    if comm:
        attend_back(early, most, within("attend", early, most))
        weight_slabs(da1.at[:, :, :, :, :, :256], late[:8], 2)
        after("b")
        attend_back(most, rows * pairs, within("attend", most, rows * pairs))
        weight_slabs(da1.at[:, :, :, :, :, 256:], late[8:], 1)
        after("c")
    else:
        attend_back(early, rows * pairs, {})
        weight_slabs(da1, late, 3)
    loads[12].wait()
    finish_tokens(within("tokens", 0, tiles))
    if comm:
        after("end")
        for chunk in chunks.values():
            chunk.finish()
        vector.finish()
    else:
        sums[...] = vector_sums()
        stores = [
            pltpu.make_async_copy(a, b, out_sem.at[i])
            for i, (a, b) in enumerate([(d2, d2_out), (w1, d1_out), (w2, da_out)])
        ]
        for copy in stores:
            copy.start()
    for copy in stores:
        copy.wait()

    def finish(i, _):
        tile_copy(i).wait()
        return 0

    lax.fori_loop(0, tiles, finish, 0)


def backward_call(dims, pad, comm):
    rows, slots, width, hidden = dims
    tokens = rows * slots
    tiles, pairs = tokens // TILE, width // 128
    piece, half = width // 8, width // 2
    wide = prob_offsets(slots // QB)[1]
    S = jax.ShapeDtypeStruct
    matrix = (2, 2, 4, 2, piece, width)
    V = pltpu.VMEM
    tall = lambda dtype: V((tokens, width), dtype)
    scratch = [
        tall(F32), V(matrix, BF), V(matrix, BF), V(matrix, BF), V((2, 2 * QB, wide), BF), tall(BF), tall(F32), tall(BF),
        V((tokens, hidden), BF), V((tokens, hidden), BF), tall(BF), tall(BF), V(matrix, BF), V((VEC_ROWS, 8, width), F32),
        V((tokens, 128), jnp.int32), V((rows, 8, slots), jnp.int32), DMA((2,)), DMA((13,)), DMA((3,)), DMA((tiles,)),
    ]
    params = dict(vmem_limit_bytes=VMEM_LIMIT)
    shapes = [S((tokens, width), F32)]
    if comm:
        shapes += [
            S((piece, 3 * width), BF), S((piece, width), BF), S((piece, hidden), BF), S((2, 2, piece, width), BF),
        ]
        scratch += [V((2, 4, 2, piece, width), BF)] * 2
        columns = (half,) * 5 + (256, 128)
        for cols in columns:
            scratch += [
                V((4, 2, piece // 2, cols), BF), V((2, 4, piece // 2, cols), BF), V((4, piece // 2, cols), BF),
                V((4, piece // 2, cols), BF), V((3, piece, cols), BF),
            ]
        scratch += [V((2, 2, piece, cols), BF) for cols in columns]
        scratch += [DMA((7, 12)), DMA((7, 12))]
        scratch += [V((4, VEC_ROWS, width), F32), V((3, VEC_ROWS, width), F32), V((4, VEC_ROWS, width), F32)]
        scratch += [DMA((6,)), DMA((7,)), DMA((7, 8))]
        params.update(collective_id=1, has_side_effects=True)
    else:
        shapes += [S(matrix, BF)] * 3
    shapes += [S((VEC_ROWS, width), F32)]
    return pl.pallas_call(
        functools.partial(backward_kernel, dims, pad, comm),
        out_shape=shapes,
        in_specs=[SCALARS, INSIDE, INSIDE] + [ANY] * 14,
        out_specs=[ANY] * (len(shapes) - 1) + [INSIDE],
        scratch_shapes=scratch,
        compiler_params=pltpu.CompilerParams(**params),
        name="backward",
    )


def local(
    fsdp, dp,
    tokens, lengths, cotangent, ln1_gain, ln1_bias, w_qkv, qkv_bias, w_out, out_bias, scale_attn, ln2_gain, ln2_bias,
    w_fc1, fc1_bias, w_fc2, fc2_bias, scale_ffn,
):
    rows = lengths.shape[0]
    slots, width = tokens.shape[0] // rows, tokens.shape[1]
    hidden = w_fc1.shape[1]
    dims = (rows, slots, width, hidden)
    pad = lengths.shape[1] - 1
    piece = width // 8
    comm = fsdp == 8 and dp == 4
    me = lax.axis_index("fsdp")
    lines = [
        ln1_gain, ln1_bias, qkv_bias[:, 0], qkv_bias[:, 1], out_bias, scale_attn, ln2_gain, ln2_bias, fc2_bias, scale_ffn,
    ]
    own = jnp.stack(lines, axis=0)
    if comm:
        own = jnp.concatenate([jnp.pad(own, ((0, 0), (0, 128 - piece))), fc1_bias.reshape(-1, 128)], axis=0)
        own = jnp.pad(own, ((0, VEC_ROWS - own.shape[0]), (0, 0)))
        forward = forward_call(dims, pad, True)(
            lengths, own, tokens, cotangent, w_qkv, w_out, w_fc1, w_fc2.reshape(2, 2, piece, width)
        )
        out, n1, qkv, prob, mixed, resid, n2, act, slope, gffn, acc, vec, full_a, full_1, full_2 = forward
    else:
        vec = lax.all_gather(own, "fsdp", axis=1, tiled=True)
        bias_one = lax.all_gather(fc1_bias, "fsdp", axis=0, tiled=True).reshape(-1, width)
        vec = jnp.concatenate([vec, bias_one], axis=0)
        vec = jnp.concatenate([vec, jnp.zeros((VEC_ROWS - vec.shape[0], width), BF)], axis=0)

        def by_columns(shard):
            full = lax.all_gather(shard, "fsdp", axis=0, tiled=True)
            return full.reshape(4, 2, piece, 2, 2, width).transpose(3, 4, 0, 1, 2, 5)

        full_a = by_columns(jnp.concatenate([w_qkv, w_out], axis=1))
        full_1 = by_columns(w_fc1)
        full_2 = lax.all_gather(w_fc2, "fsdp", axis=0, tiled=True)
        full_2 = full_2.reshape(4, 2, 2, 2, piece, width).transpose(2, 3, 0, 1, 4, 5)
        forward = forward_call(dims, pad, False)(lengths, vec, tokens, cotangent, full_a, full_1, full_2)
        out, n1, qkv, prob, mixed, resid, n2, act, slope, gffn, acc, vec = forward
    backward = backward_call(dims, pad, comm)(
        lengths, vec, acc, tokens, cotangent, full_a, full_1, full_2, n1, qkv, prob, mixed, resid, n2, act, slope, gffn
    )
    if comm:
        grad_tokens, sum_qkv, sum_out, sum_1, sum_2, sums = backward
        sum_2 = sum_2.reshape(-1, width)
    else:
        grad_tokens, da, d1, d2, sums = backward

        def total(array):
            part = lax.psum_scatter(array, "fsdp", scatter_dimension=0, tiled=True)
            return lax.psum(part, "dp")

        d1 = d1.transpose(2, 3, 4, 0, 1, 5).reshape(width, hidden)
        d2 = d2.transpose(2, 3, 0, 1, 4, 5).reshape(hidden, width)
        first = da[..., : width // 2].transpose(2, 3, 4, 0, 1, 5).reshape(width, 4, 3, 128)
        second = da[..., width // 2 :].transpose(2, 3, 4, 0, 1, 5).reshape(width, 4, 3, 128)
        heads = jnp.concatenate([first[:, :2], second], axis=1).transpose(0, 2, 1, 3).reshape(width, 3 * width)
        sum_a = total(jnp.concatenate([heads, first[:, 2:].reshape(width, width)], axis=1))
        sum_qkv, sum_out = sum_a[:, : 3 * width], sum_a[:, 3 * width :]
        sum_1, sum_2 = total(d1), total(d2)
        sums = lax.psum(sums, ("fsdp", "dp"))
    own_piece = width // fsdp
    mine = lax.dynamic_slice(sums, (0, me * own_piece), (FB1_ROW, own_piece))
    bias_sums = sums[FB1_ROW : FB1_ROW + hidden // width].reshape(-1)
    bias_one = lax.dynamic_slice(bias_sums, (me * (hidden // fsdp),), (hidden // fsdp,))
    return (
        out, grad_tokens, mine[G1_ROW], mine[B1_ROW], sum_qkv.astype(F32),
        jnp.stack([mine[QB_ROW], mine[VB_ROW]], axis=1), sum_out.astype(F32), mine[OB_ROW], mine[SA_ROW],
        mine[G2_ROW], mine[B2_ROW], sum_1.astype(F32), bias_one, sum_2.astype(F32), mine[FB2_ROW], mine[SF_ROW],
    )


def solution(mesh):
    both, one, two = P(("fsdp", "dp"), None), P("fsdp"), P("fsdp", None)
    in_specs = (both, both, both, one, one, two, two, two, one, one, one, one, two, one, two, one, one)
    out_specs = (both, both, one, one, two, two, two, one, one, one, one, two, one, two, one, one)
    run = functools.partial(local, mesh.shape["fsdp"], mesh.shape["dp"])
    return jax.shard_map(run, mesh=mesh, in_specs=in_specs, out_specs=out_specs, check_vma=False)
```

```python
import functools
import math

import jax
import jax.numpy as jnp
from jax import lax
from jax.experimental import pallas as pl
from jax.experimental.pallas import tpu as pltpu
from jax.sharding import PartitionSpec as P

HEAD_DIM = 64
norm_eps = 1e-06
masked_score = -1e30
BF = jnp.bfloat16
F32 = jnp.float32
TILE = 256
QB = 128
VMEM_LIMIT = 67043328

MESH = pl.DeviceIdType.MESH
SHARED = 64

G1_ROW, B1_ROW, QB_ROW, VB_ROW, OB_ROW, SA_ROW, G2_ROW, B2_ROW, FB2_ROW, SF_ROW, FB1_ROW = range(11)
VEC_ROWS = 16
VECTOR_ROWS = range(10)


def mm(a, b):
    return lax.dot_general(a, b, (((1,), (0,)), ((), ())), preferred_element_type=F32)


def mm_bt(a, b):
    return lax.dot_general(a, b, (((1,), (1,)), ((), ())), preferred_element_type=F32)


def mm_at(a, b):
    return lax.dot_general(a, b, (((0,), (0,)), ((), ())), preferred_element_type=F32)


def norm_parts(values):
    centered = values - jnp.mean(values, axis=-1, keepdims=True)
    spread = jnp.mean(centered * centered, axis=-1, keepdims=True)
    inv = lax.rsqrt(spread + norm_eps)
    return centered * inv, inv


def window(block, blocks):
    first = max(block - 1, 0)
    last = min(block + 2, blocks)
    return first * QB, (last - first) * QB


def prob_offsets(blocks):
    offsets, total = [], 0
    for block in range(blocks):
        offsets.append(total)
        total += window(block, blocks)[1]
    return offsets, total


def lane_tile(values, times):
    return jnp.concatenate([values] * times, axis=1) if times > 1 else values


def fill_segments(lengths_ref, rows, slots, seg_col, seg_row):
    count = lengths_ref.shape[1]
    for r in range(rows):
        down = lax.broadcasted_iota(jnp.int32, (slots, 128), 0)
        along = lax.broadcasted_iota(jnp.int32, (8, slots), 1)
        col = jnp.zeros((slots, 128), jnp.int32)
        row = jnp.zeros((8, slots), jnp.int32)
        end = jnp.int32(0)
        for j in range(count):
            end = end + lengths_ref[r, j]
            col = col + (down >= end).astype(jnp.int32)
            row = row + (along >= end).astype(jnp.int32)
        seg_col[pl.ds(r * slots, slots), :] = col
        seg_row[r] = row


def attention_forward(rows, slots, pairs, width, qkv, seg_col, seg_row, prob_slot, mixed, r, pair):
    blocks = slots // QB
    offsets, _ = prob_offsets(blocks)
    low = lax.broadcasted_iota(jnp.int32, (QB, 128), 1) < HEAD_DIM
    col = pl.multiple_of(pair * 128, 128)
    base = pl.multiple_of(r * slots, slots)
    zero = jnp.zeros((QB, 128), BF)
    for b in range(blocks):
        start, wide = window(b, blocks)
        q = qkv[pl.ds(base + b * QB, QB), pl.ds(col, 128)]
        k = qkv[pl.ds(base + start, wide), pl.ds(width + col, 128)]
        v = qkv[pl.ds(base + start, wide), pl.ds(2 * width + col, 128)]
        same = lane_tile(seg_col[pl.ds(base + b * QB, QB), :], wide // 128) == seg_row[r, 0:1, start : start + wide]
        q2 = jnp.concatenate([jnp.where(low, q, zero), jnp.where(low, zero, q)], axis=0)
        scores = mm_bt(q2, k)
        scores = jnp.concatenate(
            [jnp.where(same, scores[:QB], masked_score), jnp.where(same, scores[QB:], masked_score)], axis=0
        )
        peak = jnp.max(scores, axis=-1, keepdims=True)
        weights = jnp.exp(scores - peak)
        total = jnp.sum(weights, axis=-1, keepdims=True)
        probs = (weights * (1.0 / total)).astype(BF)
        prob_slot[:, offsets[b] : offsets[b] + wide] = probs
        out = mm(probs, v)
        mixed[pl.ds(base + b * QB, QB), pl.ds(col, 128)] = jnp.where(low, out[:QB], out[QB:]).astype(BF)


def attention_backward(rows, slots, pairs, width, qkv, prob_slot, mixed, grad_mixed, grads, r, pair):
    blocks = slots // QB
    offsets, _ = prob_offsets(blocks)
    low = lax.broadcasted_iota(jnp.int32, (QB, 128), 1) < HEAD_DIM
    low_all = lax.broadcasted_iota(jnp.int32, (slots, 128), 1) < HEAD_DIM
    factor = 1.0 / math.sqrt(HEAD_DIM)
    col = pl.multiple_of(pair * 128, 128)
    base = pl.multiple_of(r * slots, slots)
    zero = jnp.zeros((QB, 128), BF)
    grad_k = [None] * blocks
    grad_v = [None] * blocks
    for b in range(blocks):
        start, wide = window(b, blocks)
        q = qkv[pl.ds(base + b * QB, QB), pl.ds(col, 128)]
        k = qkv[pl.ds(base + start, wide), pl.ds(width + col, 128)]
        v = qkv[pl.ds(base + start, wide), pl.ds(2 * width + col, 128)]
        up = grad_mixed[pl.ds(base + b * QB, QB), pl.ds(col, 128)]
        out = mixed[pl.ds(base + b * QB, QB), pl.ds(col, 128)]
        probs = prob_slot[:, offsets[b] : offsets[b] + wide]
        q2 = jnp.concatenate([jnp.where(low, q, zero), jnp.where(low, zero, q)], axis=0)
        up2 = jnp.concatenate([jnp.where(low, up, zero), jnp.where(low, zero, up)], axis=0)
        out2 = jnp.concatenate([out, out], axis=0)
        inner = jnp.sum(up2.astype(F32) * out2.astype(F32), axis=-1, keepdims=True)
        grad_probs = mm_bt(up2, v)
        grad_scores = (probs.astype(F32) * (grad_probs - inner)).astype(BF)
        grad_q = mm(grad_scores, k) * factor
        grads[pl.ds(base + b * QB, QB), pl.ds(col, 128)] = jnp.where(low, grad_q[:QB], grad_q[QB:]).astype(BF)
        dk = mm_at(grad_scores, q2)
        dv = mm_at(probs, up2)
        for i in range(wide // QB):
            kb = start // QB + i
            piece_k, piece_v = dk[i * QB : (i + 1) * QB], dv[i * QB : (i + 1) * QB]
            grad_k[kb] = piece_k if grad_k[kb] is None else grad_k[kb] + piece_k
            grad_v[kb] = piece_v if grad_v[kb] is None else grad_v[kb] + piece_v
        done = [b - 1] if b > 0 else []
        if b == blocks - 1:
            done.append(b)
        for kb in done:
            grads[pl.ds(base + kb * QB, QB), pl.ds(width + col, 128)] = grad_k[kb].astype(BF)
            grads[pl.ds(base + kb * QB, QB), pl.ds(2 * width + col, 128)] = grad_v[kb].astype(BF)


def fold(values):
    return jnp.sum(values.reshape(values.shape[0] // 8, 8, values.shape[1]), axis=0)


def gelu_parts(values):
    cdf = 0.5 * (1.0 + lax.erf(values * math.sqrt(0.5)))
    pdf = jnp.exp(-0.5 * values * values) * (1.0 / math.sqrt(2.0 * math.pi))
    return values * cdf, cdf + values * pdf


def block(ref, c):
    value = ref[c // 2, c % 2]
    return value.reshape(-1, value.shape[-1])


def hidden_rows(ref, z):
    return jnp.concatenate([ref[x, c, z, y] for y in range(2) for x in range(2) for c in range(2)], axis=0)


def run_hooks(hooks, step):
    for k, turns in sorted(hooks.items()):

        @pl.when(step == k)
        def _(turns=turns):
            for turn in turns:
                turn()


def forward_phases(dims, refs):
    rows, slots, width, hidden = dims
    tokens = rows * slots
    tiles = tokens // TILE
    pairs = width // 128
    vec = refs["vec"]

    def row_of(i):
        return vec[i : i + 1, :].astype(F32)

    def norm_one(hooks):
        gain, shift = row_of(G1_ROW), row_of(B1_ROW)

        def body(i, _):
            at = pl.ds(pl.multiple_of(i * TILE, TILE), TILE)
            hat, _inv = norm_parts(refs["tok"][at, :])
            refs["n1"][at, :] = (hat * gain + shift).astype(BF)
            run_hooks(hooks, i)
            return 0

        lax.fori_loop(0, tiles, body, 0)

    def project(hooks):
        q_bias, v_bias = row_of(QB_ROW), row_of(VB_ROW)
        factor = 1.0 / math.sqrt(HEAD_DIM)

        def body(i, _):
            at = pl.ds(pl.multiple_of(i * TILE, TILE), TILE)
            normed = refs["n1"][at, :]
            query = (mm(normed, block(refs["wa"], 0)) + q_bias).astype(BF)
            refs["qkv"][at, :width] = (query.astype(F32) * factor).astype(BF)
            refs["qkv"][at, width : 2 * width] = mm(normed, block(refs["wa"], 1)).astype(BF)
            refs["qkv"][at, 2 * width : 3 * width] = (
                mm(normed, block(refs["wa"], 2)) + v_bias
            ).astype(BF)
            run_hooks(hooks, i)
            return 0

        lax.fori_loop(0, tiles, body, 0)

    def attend(hooks):
        steps = rows * pairs

        def out_copy(step):
            slot = lax.rem(step, 2)
            return pltpu.make_async_copy(refs["slot"].at[slot], refs["prob_out"].at[step], refs["slot_sem"].at[slot])

        def body(step, _):
            @pl.when(step >= 2)
            def _():
                out_copy(step - 2).wait()

            attention_forward(
                rows, slots, pairs, width, refs["qkv"], refs["seg_col"], refs["seg_row"],
                refs["slot"].at[lax.rem(step, 2)], refs["mixed"], lax.rem(step, rows), lax.div(step, rows),
            )
            out_copy(step).start()
            run_hooks(hooks, step)
            return 0

        lax.fori_loop(0, steps, body, 0)
        out_copy(steps - 2).wait()
        out_copy(steps - 1).wait()

    def feed_one(hooks):
        out_bias, scale_one = row_of(OB_ROW), row_of(SA_ROW)
        gain, shift = row_of(G2_ROW), row_of(B2_ROW)

        def body(i, _):
            at = pl.ds(pl.multiple_of(i * TILE, TILE), TILE)
            attn = mm(refs["mixed"][at, :], block(refs["wa"], 3)) + out_bias
            resid = refs["tok"][at, :] + scale_one * attn
            refs["resid"][at, :] = resid
            hat, _inv = norm_parts(resid)
            normed = (hat * gain + shift).astype(BF)
            refs["n2"][at, :] = normed
            for c in range(hidden // width):
                cols = slice(c * width, (c + 1) * width)
                pre = mm(normed, block(refs["w1"], c)) + row_of(FB1_ROW + c)
                act, slope = gelu_parts(pre)
                refs["act"][at, cols] = act.astype(BF)
                refs["slope"][at, cols] = slope.astype(BF)
            refs["tile_one"](i)
            run_hooks(hooks, i)
            return 0

        lax.fori_loop(0, tiles, body, 0)

    def feed_two():
        bias_two, scale_two = row_of(FB2_ROW), row_of(SF_ROW)
        refs["acc"][...] = jnp.zeros_like(refs["acc"])

        def body(i, _):
            at = pl.ds(pl.multiple_of(i * TILE, TILE), TILE)
            ffn = mm(refs["act"][at, :], jnp.concatenate([hidden_rows(refs["w2"], z) for z in range(4)], axis=0)) + bias_two
            valid = lane_tile(refs["seg_col"][at, :], width // 128) < refs["pad"]
            up = jnp.where(valid, refs["cot"][at, :], 0.0)
            grad = (scale_two * up).astype(BF)
            refs["gffn"][at, :] = grad
            refs["acc"][0] += fold(up * ffn)
            refs["acc"][1] += fold(grad.astype(F32))
            refs["tok"][at, :] = refs["resid"][at, :] + scale_two * ffn
            refs["tile_two"](i)
            return 0

        lax.fori_loop(0, tiles, body, 0)

    return norm_one, project, attend, feed_one, feed_two


def backward_phases(dims, refs):
    rows, slots, width, hidden = dims
    tokens = rows * slots
    tiles = tokens // TILE
    pairs = width // 128
    parts = hidden // width
    vec, acc = refs["vec"], refs["acc"]
    half = width // 2
    piece = width // 8

    def row_of(i):
        return vec[i : i + 1, :].astype(F32)

    def weight_two():
        per = hidden // 8

        def body(i, _):
            at = pl.ds(pl.multiple_of(i * per, per), per)
            refs["act_load"](i).wait()
            grad = mm_at(refs["act"][:, at], refs["gffn"][...]).astype(BF)
            refs["d2"][:, :, lax.div(i, 2), lax.rem(i, 2)] = grad.reshape(2, 2, per // 4, width)
            return 0

        lax.fori_loop(0, 8, body, 0)

    def through_ffn(hooks):
        gain, scale_one = row_of(G2_ROW), row_of(SA_ROW)

        def body(i, _):
            at = pl.ds(pl.multiple_of(i * TILE, TILE), TILE)
            grad_ffn = refs["gffn"][at, :]
            for c in range(parts):
                cols = slice(c * width, (c + 1) * width)
                grad_act = mm_bt(grad_ffn, hidden_rows(refs["w2"], c))
                pre = (grad_act * refs["slope"][at, cols].astype(F32)).astype(BF)
                refs["slope"][at, cols] = pre
                acc[FB1_ROW + c] += fold(pre.astype(F32))
            grad = mm_bt(refs["slope"][at, :], jnp.concatenate([block(refs["w1"], c) for c in range(parts)], axis=1))
            hat, inv = norm_parts(refs["resid"][at, :])
            acc[G2_ROW] += fold(grad * hat)
            acc[B2_ROW] += fold(grad)
            u = grad * gain
            back = inv * (u - jnp.mean(u, axis=-1, keepdims=True) - hat * jnp.mean(u * hat, axis=-1, keepdims=True))
            valid = lane_tile(refs["seg_col"][at, :], width // 128) < refs["pad"]
            grad_resid = jnp.where(valid, refs["cot"][at, :], 0.0) + back
            refs["resid"][at, :] = grad_resid
            grad_proj = (scale_one * grad_resid).astype(BF)
            refs["gproj"][at, :] = grad_proj
            acc[OB_ROW] += fold(grad_proj.astype(F32))
            refs["gmixed"][at, :] = mm_bt(grad_proj, block(refs["wa"], 3)).astype(BF)
            run_hooks(hooks, i)
            return 0

        lax.fori_loop(0, tiles, body, 0)

    def weight_one(side):
        def body(i, _):
            at = pl.ds(pl.multiple_of(i * half, half), half)
            for c in range(parts):
                first = c * width + side * half
                grad = mm_at(refs["n2"][:, at], refs["slope"][:, first : first + half]).astype(BF)
                refs["d1"][c // 2, c % 2, pl.ds(i * 2, 2), :, :, side * half : (side + 1) * half] = grad.reshape(
                    2, 2, piece, half
                )
            return 0

        lax.fori_loop(0, 2, body, 0)

    def weight_out():
        def body(i, _):
            at = pl.ds(pl.multiple_of(i * half, half), half)
            grad = mm_at(refs["mixed"][:, at], refs["gproj"][...])
            low = grad.astype(BF)
            for j in range(2):
                refs["da0"][1, j, pl.ds(i * 2, 2)] = low[:, j * half : (j + 1) * half].reshape(2, 2, piece, half)
            w_out = refs["wa"][1, 1, pl.ds(i * 2, 2)].reshape(half, width)
            acc[SA_ROW] += fold(grad * w_out.astype(F32))
            return 0

        lax.fori_loop(0, 2, body, 0)

    def attend_back(first, last, hooks):
        def in_copy(step):
            slot = lax.rem(step, 2)
            return pltpu.make_async_copy(refs["prob_in"].at[step], refs["slot"].at[slot], refs["slot_sem"].at[slot])

        if first == 0:
            in_copy(0).start()

        def body(step, _):
            @pl.when(step + 1 < rows * pairs)
            def _():
                in_copy(step + 1).start()

            in_copy(step).wait()
            attention_backward(
                rows, slots, pairs, width, refs["qkv"], refs["slot"].at[lax.rem(step, 2)], refs["mixed"],
                refs["gmixed"], refs["qkv"], lax.rem(step, rows), lax.div(step, rows),
            )
            run_hooks(hooks, step)
            return 0

        lax.fori_loop(first, last, body, 0)

    def weight_slabs(target, slabs, per):
        wide = per * 128

        def body(i, _):
            at = pl.ds(pl.multiple_of(i * half, half), half)
            found = [refs["qkv"][:, part * width + p * 128 : part * width + (p + 1) * 128] for part, p in slabs]
            grad = mm_at(refs["n1"][:, at], jnp.concatenate(found, axis=1)).astype(BF)
            for j in range(len(slabs) // per):
                target[j // 2, j % 2, pl.ds(i * 2, 2)] = grad[:, j * wide : (j + 1) * wide].reshape(2, 2, piece, wide)
            return 0

        lax.fori_loop(0, 2, body, 0)

    def finish_tokens(hooks):
        gain = row_of(G1_ROW)

        def body(i, _):
            at = pl.ds(pl.multiple_of(i * TILE, TILE), TILE)
            grad = mm_bt(refs["qkv"][at, :], jnp.concatenate([block(refs["wa"], c) for c in range(3)], axis=1))
            hat, inv = norm_parts(refs["tok"][at, :])
            acc[G1_ROW] += fold(grad * hat)
            acc[B1_ROW] += fold(grad)
            acc[QB_ROW] += fold(refs["qkv"][at, :width].astype(F32))
            acc[VB_ROW] += fold(refs["qkv"][at, 2 * width :].astype(F32))
            u = grad * gain
            back = inv * (u - jnp.mean(u, axis=-1, keepdims=True) - hat * jnp.mean(u * hat, axis=-1, keepdims=True))
            refs["tok"][at, :] = refs["resid"][at, :] + back
            refs["tile_out"](i)
            run_hooks(hooks, i)
            return 0

        lax.fori_loop(0, tiles, body, 0)

    def vector_sums():
        lines = [jnp.sum(acc[i], axis=0, keepdims=True) for i in range(VEC_ROWS)]
        lines[SA_ROW] = (lines[SA_ROW] + row_of(OB_ROW) * lines[OB_ROW]) / row_of(SA_ROW)
        return jnp.concatenate(lines, axis=0)

    return weight_two, through_ffn, weight_one, weight_out, attend_back, weight_slabs, finish_tokens, vector_sums


ANY = pl.BlockSpec(memory_space=pl.ANY)
INSIDE = pl.BlockSpec(memory_space=pltpu.VMEM)
SCALARS = pl.BlockSpec(memory_space=pltpu.SMEM)
DMA = pltpu.SemaphoreType.DMA


def position():
    f, d = lax.axis_index("fsdp"), lax.axis_index("dp")
    return lax.div(f, 2), lax.rem(f, 2), lax.div(d, 2), lax.rem(d, 2)


def device(z, y, x, c):
    return (z * 2 + y, x * 2 + c)


def z_partners(z):
    return [z + 1 - 2 * lax.rem(z, 2), 3 - z, lax.rem(z + 2, 4)]


def remote(src, dst, send, recv, target):
    return pltpu.make_async_remote_copy(
        src_ref=src, dst_ref=dst, send_sem=send, recv_sem=recv, device_id=target, device_id_type=MESH
    )


def greet(targets):
    barrier = pltpu.get_barrier_semaphore()
    for target in targets:
        pl.semaphore_signal(barrier, inc=1, device_id=target, device_id_type=MESH)


def meet(targets):
    pl.semaphore_wait(pltpu.get_barrier_semaphore(), len(targets))


class Gather:
    def __init__(self, t, buf, sems, place):
        self.t, self.buf, self.place = t, buf, place
        self.zs, self.zr, self.ys, self.yr, self.xs, self.xr, self.cs, self.cr = sems
        z = place[0]
        low = z < 2
        self.others = [z + 1 - 2 * lax.rem(z, 2), jnp.where(low, 2, 1), jnp.where(low, 3, 0)]
        self.inner = jnp.logical_or(z == 1, z == 2)

    def shard(self, j):
        z, y, _, _ = self.place
        if j == 7:
            return z, y
        if j < 3:
            return self.others[j], y
        return (z if j == 3 else self.others[j - 4]), 1 - y

    def part(self, z, y, p):
        _, _, x, c = self.place
        rows = self.buf.shape[4]
        if p == 0:
            return self.buf.at[x, c, z, y, pl.ds(0, SHARED)]
        return self.buf.at[:, c, z, y, pl.ds(SHARED, rows - SHARED)]

    def z_copy(self, origin, i, p, target):
        _, y, x, c = self.place
        ref = self.part(origin, y, p)
        return remote(ref, ref, self.zs.at[self.t, i, p], self.zr.at[self.t, origin, p], device(target, y, x, c))

    def outward(self, k, p):
        z = self.place[0]
        return self.z_copy(self.others[k], 2 + k, p, 3 - z if k == 0 else self.others[0])

    def y_copy(self, j, p):
        z, y, x, c = self.place
        zs, ys = self.shard(j)
        ref = self.part(zs, ys, p)
        return remote(ref, ref, self.ys.at[self.t, zs, p], self.yr.at[self.t, zs, p], device(z, 1 - y, x, c))

    def x_copy(self, j, qx):
        z, y, x, c = self.place
        zs, ys = self.shard(j)
        s = zs * 2 + ys
        ref = self.buf.at[qx, c, zs, ys, pl.ds(0, SHARED)]
        return remote(ref, ref, self.xs.at[self.t, s], self.xr.at[self.t, s], device(z, y, 1 - x, c))

    def c_copy(self, j, qx, qc):
        z, y, x, c = self.place
        zs, ys = self.shard(j)
        s = zs * 2 + ys
        ref = self.buf.at[qx, qc, zs, ys]
        return remote(ref, ref, self.cs.at[self.t, s, qx], self.cr.at[self.t, s, qx], device(z, y, x, 1 - c))

    def onward(self, j, p):
        _, _, x, c = self.place
        if p == 0:
            self.x_copy(j, x).start()
        else:
            self.c_copy(j, x, c).start()

    def send_z(self):
        z = self.place[0]
        for p in range(2):
            self.z_copy(z, 0, p, self.others[0]).start()

        @pl.when(self.inner)
        def _():
            for p in range(2):
                self.z_copy(z, 1, p, 3 - z).start()

    def send_y(self):
        for p in range(2):
            self.y_copy(7, p).start()

    def z_step(self, k, p):
        self.z_copy(self.others[k], 0, p, self.others[0]).wait_recv()

        @pl.when(self.inner)
        def _():
            self.outward(k, p).start()

        self.y_copy(k, p).start()
        self.onward(k, p)

    def y_step(self, k, p):
        self.y_copy(3 + k, p).wait_recv()
        self.onward(3 + k, p)

    def x_step(self, j):
        _, _, x, c = self.place
        self.x_copy(j, 1 - x).wait_recv()
        self.c_copy(j, 1 - x, c).start()

    def done(self):
        _, _, x, c = self.place
        for j in range(7):
            for qx in (x, 1 - x):
                self.c_copy(j, qx, 1 - c).wait_recv()

    def finish(self):
        z, _, x, c = self.place
        for p in range(2):
            self.z_copy(z, 0, p, self.others[0]).wait_send()

        @pl.when(self.inner)
        def _():
            for p in range(2):
                self.z_copy(z, 1, p, 3 - z).wait_send()
                for k in range(3):
                    self.outward(k, p).wait_send()

        for j in (7, 0, 1, 2):
            for p in range(2):
                self.y_copy(j, p).wait_send()
        for j in range(7):
            self.x_copy(j, x).wait_send()
            for qx in (x, 1 - x):
                self.c_copy(j, qx, c).wait_send()


START_TURNS = ("asz", "asy")
NORM_TURNS = {
    0: ("az00", "az10"),
    1: ("az11", "ay00", "ay01"),
    2: ("az20", "az01", "ax0", "az21", "bsz", "bsy", "ay10", "ax1", "ay20", "ax2", "ax3", "ay21"),
    3: ("ay30", "ay11", "ax5", "ay31", "bz10", "ax4", "ax6", "bz00", "by00", "bz01", "bz11"),
}
PROJECT_TURNS = {
    0: ("by01",),
    1: ("bz20",),
    3: ("by10", "bz21", "csz", "by20", "bx1"),
}
ATTEND_TURNS = {
    0: ("bx2", "csy"),
    1: ("bx0",),
    2: ("bx3",),
    4: ("by30", "by11", "cz10"),
    6: ("by21", "cz00"),
    7: ("by31", "bx6", "cz01", "cy00"),
    8: ("bx5",),
    9: ("cz20", "bx4"),
    11: ("cy10", "cz21", "cy01"),
}
FEED_TURNS = {
    0: ("cx3", "cx2", "cy20", "cy30", "cx0", "cz11", "cx1"),
    2: ("cy21", "cy31", "cy11", "cx6", "cx4", "cx5"),
}


def turn(gathers, name):
    gather, kind = gathers["abc".index(name[0])], name[1:]
    if kind == "sz":
        return gather.send_z
    if kind == "sy":
        return gather.send_y
    if kind[0] == "x":
        return functools.partial(gather.x_step, int(kind[1]))
    step = gather.z_step if kind[0] == "z" else gather.y_step
    return functools.partial(step, int(kind[1]), int(kind[2]))


def turns(gathers, table):
    return {k: [turn(gathers, name) for name in names] for k, names in table.items()}


def forward_kernel(dims, pad, comm, *all_refs):
    rows, slots, width, hidden = dims
    tokens = rows * slots
    tiles = tokens // TILE
    all_refs = list(all_refs)
    take = lambda n: [all_refs.pop(0) for _ in range(n)]
    lengths, vec_in, tok_in, cot_in = take(4)
    wqkv_in, wout_in, w1_in, w2_in = take(4) if comm else [None] + take(3)
    out, n1_out, qkv_out, prob_out, mixed_out, resid_out, n2_out, act_out, slope_out, gffn_out, acc, vec = take(12)
    weights_out = take(3) if comm else []
    tok, cot, wa, w1, w2, n1, qkv, slot, mixed, resid, n2, act, slope, gffn, seg_col, seg_row = take(16)
    slot_sem, in_sem, out_sem, tile_sem = take(4)
    moves = [(tok_in, tok), (cot_in, cot)]
    if comm:
        place = position()
        z, y, x, c = place
        vec_land, vs, vr = take(3)
        sems = take(8)
        ga, g1, g2 = [Gather(t, buf, sems, place) for t, buf in enumerate((wa, w1, w2))]
        for q in range(4):
            source = wqkv_in.at[:, q * width : (q + 1) * width] if q < 3 else wout_in
            moves.append((source, wa.at[q // 2, q % 2, z, y]))
        for q in range(4):
            moves.append((w1_in.at[:, q * width : (q + 1) * width], w1.at[q // 2, q % 2, z, y]))
        moves.append((w2_in, w2.at[:, :, z, y]))
    else:
        moves += [(wout_in, wa), (w1_in, w1), (w2_in, w2)]
    loads = [pltpu.make_async_copy(a, b, in_sem.at[i]) for i, (a, b) in enumerate(moves)]
    for copy in loads[2:] + loads[:2]:
        copy.start()

    def tile_copies(i, pairs, base):
        at = pl.ds(pl.multiple_of(i * TILE, TILE), TILE)
        return [pltpu.make_async_copy(a.at[at], b.at[at], tile_sem.at[i, base + j]) for j, (a, b) in enumerate(pairs)]

    ones = [(resid, resid_out), (n2, n2_out), (act, act_out), (slope, slope_out)]
    twos = [(tok, out), (gffn, gffn_out)]

    def tile_one(i):
        for copy in tile_copies(i, ones, 0):
            copy.start()

    def tile_two(i):
        for copy in tile_copies(i, twos, len(ones)):
            copy.start()

    refs = dict(
        vec=vec, tok=tok, cot=cot, wa=wa, w1=w1, w2=w2, n1=n1, qkv=qkv, slot=slot, mixed=mixed, resid=resid, n2=n2,
        act=act, slope=slope, gffn=gffn, seg_col=seg_col, seg_row=seg_row, slot_sem=slot_sem, prob_out=prob_out,
        acc=acc, pad=pad, tile_one=tile_one, tile_two=tile_two,
    )
    norm_one, project, attend, feed_one, feed_two = forward_phases(dims, refs)
    pairs_out = [(n1, n1_out), (qkv, qkv_out), (mixed, mixed_out)]
    if comm:
        pairs_out += list(zip((wa, w1, w2), weights_out))
    stores = [pltpu.make_async_copy(a, b, out_sem.at[i]) for i, (a, b) in enumerate(pairs_out)]
    if comm:
        others = z_partners(z)
        peers = [device(o, y, x, c) for o in others] + [device(o, 1 - y, x, c) for o in [z] + others]
        known = peers + [device(z, y, 1 - x, c), device(z, y, x, 1 - c)]
        greet(known)
        meet(known)
        mine = z * 2 + y
        vec_sends = [
            remote(vec_in, vec_land.at[mine], vs.at[k], vr.at[mine], peer) for k, peer in enumerate(peers)
        ]
        for copy in vec_sends:
            copy.start()
        gathers = (ga, g1, g2)
        for copy in loads[2:6]:
            copy.wait()
        for name in START_TURNS:
            turn(gathers, name)()
        fill_segments(lengths, rows, slots, seg_col, seg_row)
        vec_land[mine] = vec_in[...]
        vec[...] = jnp.zeros_like(vec)
        sources = [(o, y) for o in others] + [(o, 1 - y) for o in [z] + others]
        for k, (zs, ys) in enumerate(sources):
            remote(vec_in, vec_land.at[zs * 2 + ys], vs.at[k], vr.at[zs * 2 + ys], peers[k]).wait_recv()
        spread_vectors(vec_land, vec, width)
        for copy in loads[6:]:
            copy.wait()
        loads[0].wait()
        norm_one(turns(gathers, NORM_TURNS))
        stores[0].start()
        ga.done()
        stores[3].start()
        project(turns(gathers, PROJECT_TURNS))
        stores[1].start()
        attend(turns(gathers, ATTEND_TURNS))
        stores[2].start()
        g1.done()
        stores[4].start()
        feed_one(turns(gathers, FEED_TURNS))
        g2.done()
        stores[5].start()
        loads[1].wait()
        feed_two()
        for gather in (ga, g1, g2):
            gather.finish()
        for copy in vec_sends:
            copy.wait_send()
    else:
        fill_segments(lengths, rows, slots, seg_col, seg_row)
        vec[...] = vec_in[...].astype(F32)
        loads[0].wait()
        norm_one({})
        stores[0].start()
        loads[2].wait()
        project({})
        stores[1].start()
        attend({})
        stores[2].start()
        for copy in loads[3:] + loads[1:2]:
            copy.wait()
        feed_one({})
        feed_two()
    for copy in stores:
        copy.wait()

    def finish(i, _):
        for copy in tile_copies(i, ones, 0) + tile_copies(i, twos, len(ones)):
            copy.wait()
        return 0

    lax.fori_loop(0, tiles, finish, 0)


def spread_vectors(land, vec, width):
    shards = land.shape[0]
    piece = width // shards
    lines = jnp.concatenate([land[s].astype(F32)[:FB1_ROW, :piece] for s in range(shards)], axis=1)
    vec[:FB1_ROW, :] = lines
    per = 3
    tiles = [land[s, FB1_ROW + j : FB1_ROW + j + 1, :].astype(F32) for s in range(shards) for j in range(per)]
    wide = width // 128
    for r in range(len(tiles) // wide):
        vec[FB1_ROW + r : FB1_ROW + r + 1, :] = jnp.concatenate(tiles[r * wide : (r + 1) * wide], axis=1)


def forward_call(dims, pad, comm):
    rows, slots, width, hidden = dims
    tokens = rows * slots
    tiles, pairs = tokens // TILE, width // 128
    piece = width // 8
    wide = prob_offsets(slots // QB)[1]
    S = jax.ShapeDtypeStruct
    matrix = (2, 2, 4, 2, piece, width)
    shapes = [
        S((tokens, width), F32), S((tokens, width), BF), S((tokens, 3 * width), BF),
        S((rows * pairs, 2 * QB, wide), BF), S((tokens, width), BF), S((tokens, width), F32), S((tokens, width), BF),
        S((tokens, hidden), BF), S((tokens, hidden), BF), S((tokens, width), BF), S((2, 8, width), F32),
        S((VEC_ROWS, width), F32),
    ]
    V = pltpu.VMEM
    scratch = [
        V((tokens, width), F32), V((tokens, width), F32), V(matrix, BF), V(matrix, BF), V(matrix, BF),
        V((tokens, width), BF), V((tokens, 3 * width), BF), V((2, 2 * QB, wide), BF),
        V((tokens, width), BF), V((tokens, width), F32), V((tokens, width), BF), V((tokens, hidden), BF),
        V((tokens, hidden), BF), V((tokens, width), BF), V((tokens, 128), jnp.int32), V((rows, 8, slots), jnp.int32),
        DMA((2,)), DMA((11,)), DMA((6,)), DMA((tiles, 6)),
    ]
    params = dict(vmem_limit_bytes=VMEM_LIMIT)
    if comm:
        shapes += [S(matrix, BF)] * 3
        scratch += [V((8, VEC_ROWS, 128), BF), DMA((7,)), DMA((8,))]
        scratch += [DMA((3, 5, 2)), DMA((3, 4, 2)), DMA((3, 4, 2)), DMA((3, 4, 2)), DMA((3, 8)), DMA((3, 8)),
                    DMA((3, 8, 2)), DMA((3, 8, 2))]
        params.update(collective_id=0, has_side_effects=True)
    return pl.pallas_call(
        functools.partial(forward_kernel, dims, pad, comm),
        out_shape=shapes,
        in_specs=[SCALARS, INSIDE] + [ANY] * (6 if comm else 5),
        out_specs=[ANY] * 10 + [INSIDE, INSIDE] + ([ANY] * 3 if comm else []),
        scratch_shapes=scratch,
        compiler_params=pltpu.CompilerParams(**params),
        name="forward",
    )


class Reduce:
    def __init__(self, t, grad, land, final, sems, place):
        self.t, self.grad, self.final, self.place = t, grad, final, place
        self.from_core, self.from_x, self.from_y, self.from_yx, self.from_xy, self.from_z = land
        self.send, self.recv = sems
        rows = grad.shape[4]
        self.first, self.second = pl.ds(0, rows // 2), pl.ds(rows // 2, rows // 2)

    def copy(self, i, src, dst, target, slot=None):
        slot = i if slot is None else slot
        return remote(src, dst, self.send.at[self.t, i], self.recv.at[self.t, slot], target)

    def core_copy(self):
        z, y, x, c = self.place
        return [
            self.copy(i, self.grad.at[q, 1 - c], self.from_core.at[q], device(z, y, x, 1 - c)) for i, q in enumerate((0, 1))
        ]

    def one_copy(self):
        z, y, x, c = self.place
        g = self.grad
        return [
            self.copy(2, g.at[1 - x, c, :, :, self.first], self.from_x, device(z, y, 1 - x, c)),
            self.copy(3, g.at[:, c, :, 1 - y, self.second], self.from_y, device(z, 1 - y, x, c)),
        ]

    def two_copy(self):
        z, y, x, c = self.place
        g = self.grad
        return [
            self.copy(4, g.at[x, c, :, 1 - y, self.first], self.from_xy, device(z, 1 - y, x, c)),
            self.copy(5, g.at[1 - x, c, :, y, self.second], self.from_yx, device(z, y, 1 - x, c)),
        ]

    def z_copy(self):
        z, y, x, c = self.place
        return [
            self.copy(6 + k, self.grad.at[x, c, o, y], self.from_z.at[k], device(o, y, x, c))
            for k, o in enumerate(z_partners(z))
        ]

    def across_copy(self):
        z, y, x, c = self.place
        own = self.final.at[x, c]
        return self.copy(9, own, own, device(z, y, 1 - x, c))

    def beside_copy(self):
        z, y, x, c = self.place
        own = self.final.at[x, c]
        return self.copy(10, own, own, device(z, y, x, 1 - c))

    def relay_copy(self):
        z, y, x, c = self.place
        other = self.final.at[1 - x, c]
        return self.copy(11, other, other, device(z, y, x, 1 - c))

    def start(self):
        for copy in self.core_copy():
            copy.start()

    def core_done(self):
        z, y, x, c = self.place
        for copy in self.core_copy():
            copy.wait_recv()

        def body(i, _):
            q, zs = lax.div(i, 4), lax.rem(i, 4)
            total = self.grad[q, c, zs].astype(F32) + self.from_core[q, zs].astype(F32)
            self.grad[q, c, zs] = total.astype(BF)
            return 0

        lax.fori_loop(0, 8, body, 0)
        for copy in self.one_copy():
            copy.start()

    def one_done(self):
        z, y, x, c = self.place
        g = self.grad
        for copy in self.one_copy():
            copy.wait_recv()

        def body(zs, _):
            total = g[x, c, zs, :, self.first].astype(F32) + self.from_x[zs].astype(F32)
            g[x, c, zs, :, self.first] = total.astype(BF)
            total = g[:, c, zs, y, self.second].astype(F32) + self.from_y[:, zs].astype(F32)
            g[:, c, zs, y, self.second] = total.astype(BF)
            return 0

        lax.fori_loop(0, 4, body, 0)
        for copy in self.two_copy():
            copy.start()

    def two_done(self):
        z, y, x, c = self.place
        g = self.grad
        for copy in self.two_copy():
            copy.wait_recv()

        def body(zs, _):
            total = g[x, c, zs, y, self.first].astype(F32) + self.from_xy[zs].astype(F32)
            g[x, c, zs, y, self.first] = total.astype(BF)
            total = g[x, c, zs, y, self.second].astype(F32) + self.from_yx[zs].astype(F32)
            g[x, c, zs, y, self.second] = total.astype(BF)
            return 0

        lax.fori_loop(0, 4, body, 0)
        for copy in self.z_copy():
            copy.start()

    def z_done(self):
        z, y, x, c = self.place
        for copy in self.z_copy():
            copy.wait_recv()
        total = self.grad[x, c, z, y].astype(F32)
        for k in range(3):
            total = total + self.from_z[k].astype(F32)
        self.final[x, c] = total.astype(BF)
        self.across_copy().start()
        self.beside_copy().start()

    def relay(self):
        self.across_copy().wait_recv()
        self.relay_copy().start()

    def done(self):
        self.beside_copy().wait_recv()
        self.relay_copy().wait_recv()

    def finish(self):
        copies = self.core_copy() + self.one_copy() + self.two_copy() + self.z_copy()
        for copy in copies + [self.across_copy(), self.beside_copy(), self.relay_copy()]:
            copy.wait_send()


class VectorSum:
    def __init__(self, ref, land, z_land, send, recv, place):
        self.ref, self.land, self.z_land, self.send, self.recv, self.place = ref, land, z_land, send, recv, place
        z, y, x, c = place
        targets = [device(z, y, x, 1 - c), device(z, y, 1 - x, c), device(z, 1 - y, x, c)]
        self.pair = [
            remote(ref.at[i], land.at[i], send.at[i], recv.at[i], target) for i, target in enumerate(targets)
        ]
        self.along = [
            remote(ref.at[3], z_land.at[z], send.at[3 + k], recv.at[3 + z], device(o, y, x, c))
            for k, o in enumerate(z_partners(z))
        ]

    def start(self, value):
        self.ref[0] = value
        self.pair[0].start()

    def step(self, i):
        self.pair[i].wait_recv()
        self.ref[i + 1] = self.ref[i] + self.land[i]
        if i < 2:
            self.pair[i + 1].start()
        else:
            for copy in self.along:
                copy.start()

    def done(self):
        z, y, x, c = self.place
        self.z_land[z] = self.ref[3]
        for k, o in enumerate(z_partners(z)):
            remote(
                self.ref.at[3], self.z_land.at[o], self.send.at[3 + k], self.recv.at[3 + o], device(o, y, x, c)
            ).wait_recv()
        total = self.z_land[0] + self.z_land[1]
        total = total + self.z_land[2]
        return total + self.z_land[3]

    def finish(self):
        for copy in self.pair + self.along:
            copy.wait_send()


CHUNKS = ("2a", "2b", "1a", "1b", "a", "b", "c")
AFTER_PHASE = {
    "two": ("2a.start",),
    "one": ("2b.one", "1a.start"),
    "other": ("1a.core",),
    "out": ("1b.start",),
    "a": ("a.start",),
    "c": ("c.start", "b.core"),
    "end": ("1b.z", "c.one", "v.start", "b.two", "v.0", "1b.relay", "2b.z", "c.two", "1a.z", "v.1", "1b.done", "a.z",
        "v.2", "b.z", "c.z", "2a.relay", "a.relay", "2b.relay", "c.relay", "1a.relay", "a.done", "b.relay", "b.done",
        "2a.done", "1a.done", "v.done", "c.done", "2b.done"),
}
WITHIN_PHASE = {
    "ffn": {
        0: ("2a.core",),
        1: ("2b.start",),
        2: ("2b.core", "2a.one"),
    },
    "attend": {
        0: ("2b.two",),
        2: ("1b.core",),
        3: ("1a.one",),
        5: ("2a.two", "a.core"),
        7: ("1a.two", "1b.one"),
        9: ("2a.z",),
        10: ("b.start", "1b.two", "a.one"),
    },
    "tokens": {
        0: ("c.core", "a.two"),
        2: ("b.one",),
    },
}


def backward_kernel(dims, pad, comm, *all_refs):
    rows, slots, width, hidden = dims
    tokens = rows * slots
    tiles, pairs = tokens // TILE, width // 128
    half = width // 2
    all_refs = list(all_refs)
    take = lambda n: [all_refs.pop(0) for _ in range(n)]
    lengths, vec, acc_in, tok_in, cot_in, wa_in, w1_in, w2_in = take(8)
    n1_in, qkv_in, prob_in, mixed_in, resid_in, n2_in, act_in, slope_in, gffn_in = take(9)
    if comm:
        gtok_out, gqkv_out, gout_out, g1_out, g2_out, sums = take(6)
    else:
        gtok_out, da_out, d1_out, d2_out, sums = take(5)
    cot, wa, w1, w2, slot, mixed, resid, n2, act, slope, gffn, gproj, d2, acc, seg_col, seg_row = take(16)
    slot_sem, in_sem, out_sem, tile_sem, act_sem = take(5)
    qkv, n1, tok = act.at[:, : 3 * width], act.at[:, 3 * width :], cot
    da0, da1 = w2.at[:, :, :, :, :, :half], w2.at[:, :, :, :, :, half:]
    pair_slabs = [(part, p) for p in range(pairs) for part in range(3)]
    ahead, late = pair_slabs[:6], pair_slabs[6:]
    moves = [
        (gffn_in, gffn), (w2_in, w2), (slope_in, slope), (w1_in, w1), (resid_in, resid), (cot_in, cot),
        (wa_in, wa), (n2_in, n2), (mixed_in, mixed), (qkv_in, qkv), (n1_in, n1), (tok_in, tok),
    ]
    loads = [pltpu.make_async_copy(a, b, in_sem.at[i]) for i, (a, b) in enumerate(moves)]

    def act_load(i):
        per = hidden // 8
        at = pl.ds(pl.multiple_of(i * per, per), per)
        return pltpu.make_async_copy(act_in.at[:, at], act.at[:, at], act_sem.at[i])

    loads[0].start()
    for i in range(8):
        act_load(i).start()
    for copy in loads[1:9]:
        copy.start()

    def tile_copy(i):
        at = pl.ds(pl.multiple_of(i * TILE, TILE), TILE)
        return pltpu.make_async_copy(tok.at[at], gtok_out.at[at], tile_sem.at[i])

    refs = dict(
        vec=vec, acc=acc, tok=tok, cot=cot, wa=wa, w1=w1, w2=w2, n1=n1, qkv=qkv, slot=slot, mixed=mixed,
        resid=resid, n2=n2, act=act, slope=slope, gffn=gffn, gproj=gproj, gmixed=gffn, d2=d2, d1=w1, da0=da0, da1=da1,
        seg_col=seg_col, seg_row=seg_row, slot_sem=slot_sem, prob_in=prob_in, pad=pad,
        tile_out=lambda i: tile_copy(i).start(), act_load=act_load,
    )
    (
        weight_two, through_ffn, weight_one, weight_out, attend_back, weight_slabs, finish_tokens, vector_sums,
    ) = backward_phases(dims, refs)
    stores = []
    if comm:
        place = position()
        z, y, x, c = place
        core_land = take(2)
        lands = [take(5) for _ in CHUNKS]
        finals = take(len(CHUNKS))
        sems = take(2)
        vec_ref, vec_land, vec_z, vec_send, vec_recv, final_sem = take(6)
        sides = [(0, half), (half, half), (0, half), (half, half), (0, half), (half, 256), (half + 256, 128)]
        chunks = {}
        for t, (name, (first, wide)) in enumerate(zip(CHUNKS, sides)):
            side = (slice(None),) * 5 + (slice(first, first + wide),)
            grad, land = (d2, w1, w2)[t // 2 if t < 4 else 2], core_land[1 if name in ("1a", "1b") else 0]
            chunks[name] = Reduce(t, grad.at[side], [land.at[side[1:]]] + lands[t], finals[t], sems, place)
        vector = VectorSum(vec_ref, vec_land, vec_z, vec_send, vec_recv, place)
        known = [device(o, y, x, c) for o in z_partners(z)]
        known += [device(z, 1 - y, x, c), device(z, y, 1 - x, c), device(z, y, x, 1 - c)]
        greet(known)

    def targets(name):
        final = finals[CHUNKS.index(name)]
        if name in ("2a", "2b"):
            first = half * (name == "2b")
            return [(final, g2_out.at[:, :, :, first : first + half])]
        found = []
        for q in range(4):
            ref = final.at[q // 2, q % 2]
            if name in ("1a", "1b"):
                first = q * width + half * (name == "1b")
                found.append((ref, g1_out.at[:, first : first + half]))
            elif name == "a" and q >= 2:
                found.append((ref, gout_out.at[:, (q - 2) * half : (q - 1) * half]))
            else:
                slabs = {"a": ahead[q * 3 : q * 3 + 3], "b": late[q * 2 : q * 2 + 2], "c": late[8 + q : 9 + q]}[name]
                for j, (part, p) in enumerate(slabs):
                    at = part * width + p * 128
                    found.append((ref.at[:, j * 128 : (j + 1) * 128], gqkv_out.at[:, at : at + 128]))
        return found

    def deliver(name):
        chunks[name].done()
        for i, (a, b) in enumerate(targets(name)):
            copy = pltpu.make_async_copy(a, b, final_sem.at[CHUNKS.index(name), i])
            copy.start()
            stores.append(copy)

    def sum_vectors():
        sums[...] = vector.done()

    def turn_of(name):
        chunk, step = name.split(".")
        if chunk == "v":
            if step == "start":
                return lambda: vector.start(vector_sums())
            return sum_vectors if step == "done" else functools.partial(vector.step, int(step))
        if step == "done":
            return functools.partial(deliver, chunk)
        methods = dict(start="start", core="core_done", one="one_done", two="two_done", z="z_done", relay="relay")
        return getattr(chunks[chunk], methods[step])

    def after(phase):
        if comm:
            for name in AFTER_PHASE.get(phase, ()):
                turn_of(name)()

    def within(phase, first, last):
        table = WITHIN_PHASE.get(phase, {}) if comm else {}
        return {k: [turn_of(name) for name in names] for k, names in table.items() if first <= k < last}

    fill_segments(lengths, rows, slots, seg_col, seg_row)
    acc[...] = jnp.zeros_like(acc)
    acc[SF_ROW] = acc_in[0]
    acc[FB2_ROW] = acc_in[1]
    loads[0].wait()
    weight_two()
    for copy in loads[9:11]:
        copy.start()
    if comm:
        meet(known)
    after("two")
    for copy in loads[1:7]:
        copy.wait()
    through_ffn(within("ffn", 0, tiles))
    loads[11].start()
    loads[7].wait()
    for side in range(2):
        weight_one(side)
        after(("one", "other")[side])
    loads[8].wait()
    weight_out()
    after("out")
    loads[9].wait()
    early, most = rows * 2, rows * 5
    attend_back(0, early, within("attend", 0, early))
    loads[10].wait()
    weight_slabs(da0, ahead, 3)
    after("a")
    if comm:
        attend_back(early, most, within("attend", early, most))
        weight_slabs(da1.at[:, :, :, :, :, :256], late[:8], 2)
        after("b")
        attend_back(most, rows * pairs, within("attend", most, rows * pairs))
        weight_slabs(da1.at[:, :, :, :, :, 256:], late[8:], 1)
        after("c")
    else:
        attend_back(early, rows * pairs, {})
        weight_slabs(da1, late, 3)
    loads[11].wait()
    finish_tokens(within("tokens", 0, tiles))
    if comm:
        after("end")
        for chunk in chunks.values():
            chunk.finish()
        vector.finish()
    else:
        sums[...] = vector_sums()
        stores = [
            pltpu.make_async_copy(a, b, out_sem.at[i])
            for i, (a, b) in enumerate([(d2, d2_out), (w1, d1_out), (w2, da_out)])
        ]
        for copy in stores:
            copy.start()
    for copy in stores:
        copy.wait()

    def finish(i, _):
        tile_copy(i).wait()
        return 0

    lax.fori_loop(0, tiles, finish, 0)


def backward_call(dims, pad, comm):
    rows, slots, width, hidden = dims
    tokens = rows * slots
    tiles, pairs = tokens // TILE, width // 128
    piece, half = width // 8, width // 2
    wide = prob_offsets(slots // QB)[1]
    S = jax.ShapeDtypeStruct
    matrix = (2, 2, 4, 2, piece, width)
    V = pltpu.VMEM
    tall = lambda dtype: V((tokens, width), dtype)
    scratch = [
        tall(F32), V(matrix, BF), V(matrix, BF), V(matrix, BF), V((2, 2 * QB, wide), BF), tall(BF), tall(F32), tall(BF),
        V((tokens, hidden), BF), V((tokens, hidden), BF), tall(BF), tall(BF), V(matrix, BF), V((VEC_ROWS, 8, width), F32),
        V((tokens, 128), jnp.int32), V((rows, 8, slots), jnp.int32), DMA((2,)), DMA((12,)), DMA((3,)), DMA((tiles,)),
        DMA((8,)),
    ]
    params = dict(vmem_limit_bytes=VMEM_LIMIT)
    shapes = [S((tokens, width), F32)]
    if comm:
        shapes += [
            S((piece, 3 * width), BF), S((piece, width), BF), S((piece, hidden), BF), S((2, 2, piece, width), BF),
        ]
        scratch += [V((2, 4, 2, piece, width), BF)] * 2
        columns = (half,) * 5 + (256, 128)
        for cols in columns:
            scratch += [
                V((4, 2, piece // 2, cols), BF), V((2, 4, piece // 2, cols), BF), V((4, piece // 2, cols), BF),
                V((4, piece // 2, cols), BF), V((3, piece, cols), BF),
            ]
        scratch += [V((2, 2, piece, cols), BF) for cols in columns]
        scratch += [DMA((7, 12)), DMA((7, 12))]
        scratch += [V((4, VEC_ROWS, width), F32), V((3, VEC_ROWS, width), F32), V((4, VEC_ROWS, width), F32)]
        scratch += [DMA((6,)), DMA((7,)), DMA((7, 8))]
        params.update(collective_id=1, has_side_effects=True)
    else:
        shapes += [S(matrix, BF)] * 3
    shapes += [S((VEC_ROWS, width), F32)]
    return pl.pallas_call(
        functools.partial(backward_kernel, dims, pad, comm),
        out_shape=shapes,
        in_specs=[SCALARS, INSIDE, INSIDE] + [ANY] * 14,
        out_specs=[ANY] * (len(shapes) - 1) + [INSIDE],
        scratch_shapes=scratch,
        compiler_params=pltpu.CompilerParams(**params),
        name="backward",
    )


def last_kernel(dims, gtok_in, out_in, gqkv_in, gout_in, g1_in, g2_in, sums_ref, *refs):
    rows, slots, width, hidden = dims
    piece = width // 8
    gtok_out, out_out, gqkv_out, gout_out, g1_out, g2_out, bias_out = refs[:7]
    lines, refs = refs[7 : 7 + len(VECTOR_ROWS)], refs[7 + len(VECTOR_ROWS) :]
    gtok, out = refs[:2]
    low, high = refs[2:6], refs[6:10]
    in_sem, out_sem, tile_sem = refs[10:]
    sources, results = (gqkv_in, gout_in, g1_in, g2_in), (gqkv_out, gout_out, g1_out, g2_out)
    parts = 4
    size = rows * slots // parts

    def token_copies(a, b, k):
        return [
            pltpu.make_async_copy(a.at[pl.ds(i * size, size)], b.at[pl.ds(i * size, size)], tile_sem.at[k, i])
            for i in range(parts)
        ]

    loads = [pltpu.make_async_copy(a, b, in_sem.at[i]) for i, (a, b) in enumerate(zip(sources, low))]
    stores = [pltpu.make_async_copy(a, b, out_sem.at[i]) for i, (a, b) in enumerate(zip(high, results))]
    inward = token_copies(out_in, out, 0) + token_copies(gtok_in, gtok, 1)
    outward = token_copies(out, out_out, 2) + token_copies(gtok, gtok_out, 3)
    for copy in loads + inward:
        copy.start()
    me = lax.axis_index("fsdp")
    mine = sums_ref[:, :piece]
    bias = sums_ref[FB1_ROW : FB1_ROW + 1, : hidden // 8]
    for k in range(1, 8):
        mine = jnp.where(me == k, sums_ref[:, k * piece : (k + 1) * piece], mine)
        row, first = divmod(k * (hidden // 8), width)
        bias = jnp.where(me == k, sums_ref[FB1_ROW + row : FB1_ROW + row + 1, first : first + hidden // 8], bias)
    for ref, row in zip(lines, VECTOR_ROWS):
        ref[...] = mine[row]
    bias_out[...] = bias[0]
    for i in range(4):
        loads[i].wait()
        high[i][...] = low[i][...].astype(F32)
        stores[i].start()
    for a, b in zip(inward, outward):
        a.wait()
        b.start()
    for copy in stores + outward:
        copy.wait()


def last_call(dims, *arrays):
    rows, slots, width, hidden = dims
    tokens, piece = rows * slots, width // 8
    S, V = jax.ShapeDtypeStruct, pltpu.VMEM
    shapes = [(piece, 3 * width), (piece, width), (piece, hidden), (hidden // 8, width)]
    full = [S((tokens, width), F32)] * 2 + [S(shape, F32) for shape in shapes]
    return pl.pallas_call(
        functools.partial(last_kernel, dims),
        out_shape=full + [S((hidden // 8,), F32)] + [S((piece,), F32)] * len(VECTOR_ROWS),
        in_specs=[ANY] * 6 + [INSIDE],
        out_specs=[ANY] * 6 + [INSIDE] * (1 + len(VECTOR_ROWS)),
        scratch_shapes=[V((tokens, width), F32)] * 2 + [V(shape, BF) for shape in shapes] + [V(shape, F32) for shape in shapes]
        + [DMA((4,)), DMA((4,)), DMA((4, 4))],
        compiler_params=pltpu.CompilerParams(vmem_limit_bytes=VMEM_LIMIT),
        name="last",
    )(*arrays)


def local(
    fsdp, dp,
    tokens, lengths, cotangent, ln1_gain, ln1_bias, w_qkv, qkv_bias, w_out, out_bias, scale_attn, ln2_gain, ln2_bias,
    w_fc1, fc1_bias, w_fc2, fc2_bias, scale_ffn,
):
    rows = lengths.shape[0]
    slots, width = tokens.shape[0] // rows, tokens.shape[1]
    hidden = w_fc1.shape[1]
    dims = (rows, slots, width, hidden)
    pad = lengths.shape[1] - 1
    piece = width // 8
    comm = fsdp == 8 and dp == 4
    me = lax.axis_index("fsdp")
    lines = [
        ln1_gain, ln1_bias, qkv_bias[:, 0], qkv_bias[:, 1], out_bias, scale_attn, ln2_gain, ln2_bias, fc2_bias, scale_ffn,
    ]
    if comm:
        rest = fc1_bias.reshape(-1, 128)
        own = jnp.pad(rest, ((FB1_ROW, VEC_ROWS - FB1_ROW - rest.shape[0]), (0, 0)))
        for i, line in enumerate(lines):
            own = own + jnp.pad(line[None], ((i, VEC_ROWS - 1 - i), (0, 128 - piece)))
        forward = forward_call(dims, pad, True)(
            lengths, own, tokens, cotangent, w_qkv, w_out, w_fc1, w_fc2.reshape(2, 2, piece, width)
        )
        out, n1, qkv, prob, mixed, resid, n2, act, slope, gffn, acc, vec, full_a, full_1, full_2 = forward
    else:
        vec = lax.all_gather(jnp.stack(lines, axis=0), "fsdp", axis=1, tiled=True)
        bias_one = lax.all_gather(fc1_bias, "fsdp", axis=0, tiled=True).reshape(-1, width)
        vec = jnp.concatenate([vec, bias_one], axis=0)
        vec = jnp.concatenate([vec, jnp.zeros((VEC_ROWS - vec.shape[0], width), BF)], axis=0)

        def by_columns(shard):
            full = lax.all_gather(shard, "fsdp", axis=0, tiled=True)
            return full.reshape(4, 2, piece, 2, 2, width).transpose(3, 4, 0, 1, 2, 5)

        full_a = by_columns(jnp.concatenate([w_qkv, w_out], axis=1))
        full_1 = by_columns(w_fc1)
        full_2 = lax.all_gather(w_fc2, "fsdp", axis=0, tiled=True)
        full_2 = full_2.reshape(4, 2, 2, 2, piece, width).transpose(2, 3, 0, 1, 4, 5)
        forward = forward_call(dims, pad, False)(lengths, vec, tokens, cotangent, full_a, full_1, full_2)
        out, n1, qkv, prob, mixed, resid, n2, act, slope, gffn, acc, vec = forward
    backward = backward_call(dims, pad, comm)(
        lengths, vec, acc, tokens, cotangent, full_a, full_1, full_2, n1, qkv, prob, mixed, resid, n2, act, slope, gffn
    )
    if comm:
        grad_tokens, sum_qkv, sum_out, sum_1, sum_2, sums = backward
        grad_tokens, out, sum_qkv, sum_out, sum_1, sum_2, bias_one, *mine = last_call(
            dims, grad_tokens, out, sum_qkv, sum_out, sum_1, sum_2.reshape(-1, width), sums
        )
    else:
        grad_tokens, da, d1, d2, sums = backward

        def total(array):
            part = lax.psum_scatter(array, "fsdp", scatter_dimension=0, tiled=True)
            return lax.psum(part, "dp")

        d1 = d1.transpose(2, 3, 4, 0, 1, 5).reshape(width, hidden)
        d2 = d2.transpose(2, 3, 0, 1, 4, 5).reshape(hidden, width)
        first = da[..., : width // 2].transpose(2, 3, 4, 0, 1, 5).reshape(width, 4, 3, 128)
        second = da[..., width // 2 :].transpose(2, 3, 4, 0, 1, 5).reshape(width, 4, 3, 128)
        heads = jnp.concatenate([first[:, :2], second], axis=1).transpose(0, 2, 1, 3).reshape(width, 3 * width)
        sum_a = total(jnp.concatenate([heads, first[:, 2:].reshape(width, width)], axis=1))
        sum_qkv, sum_out = sum_a[:, : 3 * width], sum_a[:, 3 * width :]
        sum_1, sum_2 = total(d1), total(d2)
        sums = lax.psum(sums, ("fsdp", "dp"))
        own_piece = width // fsdp
        mine = lax.dynamic_slice(sums, (0, me * own_piece), (FB1_ROW, own_piece))
        bias_sums = sums[FB1_ROW : FB1_ROW + hidden // width].reshape(-1)
        bias_one = lax.dynamic_slice(bias_sums, (me * (hidden // fsdp),), (hidden // fsdp,))
    return (
        out, grad_tokens, mine[G1_ROW], mine[B1_ROW], sum_qkv.astype(F32),
        jnp.stack([mine[QB_ROW], mine[VB_ROW]], axis=1), sum_out.astype(F32), mine[OB_ROW], mine[SA_ROW],
        mine[G2_ROW], mine[B2_ROW], sum_1.astype(F32), bias_one, sum_2.astype(F32), mine[FB2_ROW], mine[SF_ROW],
    )


def solution(mesh):
    both, one, two = P(("fsdp", "dp"), None), P("fsdp"), P("fsdp", None)
    in_specs = (both, both, both, one, one, two, two, two, one, one, one, one, two, one, two, one, one)
    out_specs = (both, both, one, one, two, two, two, one, one, one, one, two, one, two, one, one)
    run = functools.partial(local, mesh.shape["fsdp"], mesh.shape["dp"])
    return jax.shard_map(run, mesh=mesh, in_specs=in_specs, out_specs=out_specs, check_vma=False)
```

```python
import functools
import math

import jax
import jax.numpy as jnp
from jax import lax
from jax.experimental import pallas as pl
from jax.experimental.pallas import tpu as pltpu
from jax.sharding import PartitionSpec as P

HEAD_DIM = 64
norm_eps = 1e-06
masked_score = -1e30
BF = jnp.bfloat16
F32 = jnp.float32
TILE = 256
QB = 128
VMEM_LIMIT = 67043328

MESH = pl.DeviceIdType.MESH
SHARED = 64

G1_ROW, B1_ROW, QB_ROW, VB_ROW, OB_ROW, SA_ROW, G2_ROW, B2_ROW, FB2_ROW, SF_ROW, FB1_ROW = range(11)
VEC_ROWS = 16
VECTOR_ROWS = range(10)


def mm(a, b):
    return lax.dot_general(a, b, (((1,), (0,)), ((), ())), preferred_element_type=F32)


def mm_bt(a, b):
    return lax.dot_general(a, b, (((1,), (1,)), ((), ())), preferred_element_type=F32)


def mm_at(a, b):
    return lax.dot_general(a, b, (((0,), (0,)), ((), ())), preferred_element_type=F32)


def norm_parts(values):
    centered = values - jnp.mean(values, axis=-1, keepdims=True)
    spread = jnp.mean(centered * centered, axis=-1, keepdims=True)
    inv = lax.rsqrt(spread + norm_eps)
    return centered * inv, inv


def window(block, blocks):
    first = max(block - 1, 0)
    last = min(block + 2, blocks)
    return first * QB, (last - first) * QB


def prob_offsets(blocks):
    offsets, total = [], 0
    for block in range(blocks):
        offsets.append(total)
        total += window(block, blocks)[1]
    return offsets, total


def lane_tile(values, times):
    return jnp.concatenate([values] * times, axis=1) if times > 1 else values


def fill_segments(lengths_ref, rows, slots, seg_col, seg_row):
    count = lengths_ref.shape[1]
    for r in range(rows):
        down = lax.broadcasted_iota(jnp.int32, (slots, 128), 0)
        along = lax.broadcasted_iota(jnp.int32, (8, slots), 1)
        col = jnp.zeros((slots, 128), jnp.int32)
        row = jnp.zeros((8, slots), jnp.int32)
        end = jnp.int32(0)
        for j in range(count):
            end = end + lengths_ref[r, j]
            col = col + (down >= end).astype(jnp.int32)
            row = row + (along >= end).astype(jnp.int32)
        seg_col[pl.ds(r * slots, slots), :] = col
        seg_row[r] = row


def attention_forward(rows, slots, pairs, width, qkv, seg_col, seg_row, prob_slot, mixed, r, pair):
    blocks = slots // QB
    offsets, _ = prob_offsets(blocks)
    low = lax.broadcasted_iota(jnp.int32, (QB, 128), 1) < HEAD_DIM
    col = pl.multiple_of(pair * 128, 128)
    base = pl.multiple_of(r * slots, slots)
    zero = jnp.zeros((QB, 128), BF)
    for b in range(blocks):
        start, wide = window(b, blocks)
        q = qkv[pl.ds(base + b * QB, QB), pl.ds(col, 128)]
        k = qkv[pl.ds(base + start, wide), pl.ds(width + col, 128)]
        v = qkv[pl.ds(base + start, wide), pl.ds(2 * width + col, 128)]
        same = lane_tile(seg_col[pl.ds(base + b * QB, QB), :], wide // 128) == seg_row[r, 0:1, start : start + wide]
        q2 = jnp.concatenate([jnp.where(low, q, zero), jnp.where(low, zero, q)], axis=0)
        scores = mm_bt(q2, k)
        scores = jnp.concatenate(
            [jnp.where(same, scores[:QB], masked_score), jnp.where(same, scores[QB:], masked_score)], axis=0
        )
        peak = jnp.max(scores, axis=-1, keepdims=True)
        weights = jnp.exp(scores - peak)
        total = jnp.sum(weights, axis=-1, keepdims=True)
        probs = (weights * (1.0 / total)).astype(BF)
        prob_slot[:, offsets[b] : offsets[b] + wide] = probs
        out = mm(probs, v)
        mixed[pl.ds(base + b * QB, QB), pl.ds(col, 128)] = jnp.where(low, out[:QB], out[QB:]).astype(BF)


def attention_backward(rows, slots, pairs, width, qkv, prob_slot, mixed, grad_mixed, grads, r, pair):
    blocks = slots // QB
    offsets, _ = prob_offsets(blocks)
    low = lax.broadcasted_iota(jnp.int32, (QB, 128), 1) < HEAD_DIM
    low_all = lax.broadcasted_iota(jnp.int32, (slots, 128), 1) < HEAD_DIM
    factor = 1.0 / math.sqrt(HEAD_DIM)
    col = pl.multiple_of(pair * 128, 128)
    base = pl.multiple_of(r * slots, slots)
    zero = jnp.zeros((QB, 128), BF)
    grad_k = [None] * blocks
    grad_v = [None] * blocks
    for b in range(blocks):
        start, wide = window(b, blocks)
        q = qkv[pl.ds(base + b * QB, QB), pl.ds(col, 128)]
        k = qkv[pl.ds(base + start, wide), pl.ds(width + col, 128)]
        v = qkv[pl.ds(base + start, wide), pl.ds(2 * width + col, 128)]
        up = grad_mixed[pl.ds(base + b * QB, QB), pl.ds(col, 128)]
        out = mixed[pl.ds(base + b * QB, QB), pl.ds(col, 128)]
        probs = prob_slot[:, offsets[b] : offsets[b] + wide]
        q2 = jnp.concatenate([jnp.where(low, q, zero), jnp.where(low, zero, q)], axis=0)
        up2 = jnp.concatenate([jnp.where(low, up, zero), jnp.where(low, zero, up)], axis=0)
        out2 = jnp.concatenate([out, out], axis=0)
        inner = jnp.sum(up2.astype(F32) * out2.astype(F32), axis=-1, keepdims=True)
        grad_probs = mm_bt(up2, v)
        grad_scores = (probs.astype(F32) * (grad_probs - inner)).astype(BF)
        grad_q = mm(grad_scores, k) * factor
        grads[pl.ds(base + b * QB, QB), pl.ds(col, 128)] = jnp.where(low, grad_q[:QB], grad_q[QB:]).astype(BF)
        dk = mm_at(grad_scores, q2)
        dv = mm_at(probs, up2)
        for i in range(wide // QB):
            kb = start // QB + i
            piece_k, piece_v = dk[i * QB : (i + 1) * QB], dv[i * QB : (i + 1) * QB]
            grad_k[kb] = piece_k if grad_k[kb] is None else grad_k[kb] + piece_k
            grad_v[kb] = piece_v if grad_v[kb] is None else grad_v[kb] + piece_v
        done = [b - 1] if b > 0 else []
        if b == blocks - 1:
            done.append(b)
        for kb in done:
            grads[pl.ds(base + kb * QB, QB), pl.ds(width + col, 128)] = grad_k[kb].astype(BF)
            grads[pl.ds(base + kb * QB, QB), pl.ds(2 * width + col, 128)] = grad_v[kb].astype(BF)


def fold(values):
    return jnp.sum(values.reshape(values.shape[0] // 8, 8, values.shape[1]), axis=0)


def gelu_parts(values):
    cdf = 0.5 * (1.0 + lax.erf(values * math.sqrt(0.5)))
    pdf = jnp.exp(-0.5 * values * values) * (1.0 / math.sqrt(2.0 * math.pi))
    return values * cdf, cdf + values * pdf


def block(ref, c):
    value = ref[c // 2, c % 2]
    return value.reshape(-1, value.shape[-1])


def hidden_rows(ref, z):
    return jnp.concatenate([ref[x, c, z, y] for y in range(2) for x in range(2) for c in range(2)], axis=0)


def run_hooks(hooks, step):
    for k, turns in sorted(hooks.items()):

        @pl.when(step == k)
        def _(turns=turns):
            for turn in turns:
                turn()


def forward_phases(dims, refs):
    rows, slots, width, hidden = dims
    tokens = rows * slots
    tiles = tokens // TILE
    pairs = width // 128
    vec = refs["vec"]

    def row_of(i):
        return vec[i : i + 1, :].astype(F32)

    def norm_one(hooks):
        gain, shift = row_of(G1_ROW), row_of(B1_ROW)

        def body(i, _):
            at = pl.ds(pl.multiple_of(i * TILE, TILE), TILE)
            hat, _inv = norm_parts(refs["tok"][at, :])
            refs["n1"][at, :] = (hat * gain + shift).astype(BF)
            run_hooks(hooks, i)
            return 0

        lax.fori_loop(0, tiles, body, 0)

    def project(hooks):
        q_bias, v_bias = row_of(QB_ROW), row_of(VB_ROW)
        factor = 1.0 / math.sqrt(HEAD_DIM)

        def body(i, _):
            at = pl.ds(pl.multiple_of(i * TILE, TILE), TILE)
            normed = refs["n1"][at, :]
            query = (mm(normed, block(refs["wa"], 0)) + q_bias).astype(BF)
            refs["qkv"][at, :width] = (query.astype(F32) * factor).astype(BF)
            refs["qkv"][at, width : 2 * width] = mm(normed, block(refs["wa"], 1)).astype(BF)
            refs["qkv"][at, 2 * width : 3 * width] = (
                mm(normed, block(refs["wa"], 2)) + v_bias
            ).astype(BF)
            run_hooks(hooks, i)
            return 0

        lax.fori_loop(0, tiles, body, 0)

    def attend(hooks):
        steps = rows * pairs

        def out_copy(step):
            slot = lax.rem(step, 2)
            return pltpu.make_async_copy(refs["slot"].at[slot], refs["prob_out"].at[step], refs["slot_sem"].at[slot])

        def body(step, _):
            @pl.when(step >= 2)
            def _():
                out_copy(step - 2).wait()

            attention_forward(
                rows, slots, pairs, width, refs["qkv"], refs["seg_col"], refs["seg_row"],
                refs["slot"].at[lax.rem(step, 2)], refs["mixed"], lax.rem(step, rows), lax.div(step, rows),
            )
            out_copy(step).start()
            run_hooks(hooks, step)
            return 0

        lax.fori_loop(0, steps, body, 0)
        out_copy(steps - 2).wait()
        out_copy(steps - 1).wait()

    def feed_one(hooks):
        out_bias, scale_one = row_of(OB_ROW), row_of(SA_ROW)
        gain, shift = row_of(G2_ROW), row_of(B2_ROW)

        def body(i, _):
            at = pl.ds(pl.multiple_of(i * TILE, TILE), TILE)
            attn = mm(refs["mixed"][at, :], block(refs["wa"], 3)) + out_bias
            resid = refs["tok"][at, :] + scale_one * attn
            refs["resid"][at, :] = resid
            hat, _inv = norm_parts(resid)
            normed = (hat * gain + shift).astype(BF)
            refs["n2"][at, :] = normed
            for c in range(hidden // width):
                cols = slice(c * width, (c + 1) * width)
                pre = mm(normed, block(refs["w1"], c)) + row_of(FB1_ROW + c)
                act, slope = gelu_parts(pre)
                refs["act"][at, cols] = act.astype(BF)
                refs["slope"][at, cols] = slope.astype(BF)
            refs["tile_one"](i)
            run_hooks(hooks, i)
            return 0

        lax.fori_loop(0, tiles, body, 0)

    def feed_two():
        bias_two, scale_two = row_of(FB2_ROW), row_of(SF_ROW)
        refs["acc"][...] = jnp.zeros_like(refs["acc"])

        def body(i, _):
            at = pl.ds(pl.multiple_of(i * TILE, TILE), TILE)
            ffn = mm(refs["act"][at, :], jnp.concatenate([hidden_rows(refs["w2"], z) for z in range(4)], axis=0)) + bias_two
            valid = lane_tile(refs["seg_col"][at, :], width // 128) < refs["pad"]
            up = jnp.where(valid, refs["cot"][at, :], 0.0)
            grad = (scale_two * up).astype(BF)
            refs["gffn"][at, :] = grad
            refs["acc"][0] += fold(up * ffn)
            refs["acc"][1] += fold(grad.astype(F32))
            refs["tok"][at, :] = refs["resid"][at, :] + scale_two * ffn
            refs["tile_two"](i)
            return 0

        lax.fori_loop(0, tiles, body, 0)

    return norm_one, project, attend, feed_one, feed_two


def backward_phases(dims, refs):
    rows, slots, width, hidden = dims
    tokens = rows * slots
    tiles = tokens // TILE
    pairs = width // 128
    parts = hidden // width
    vec, acc = refs["vec"], refs["acc"]
    half = width // 2
    piece = width // 8

    def row_of(i):
        return vec[i : i + 1, :].astype(F32)

    def weight_two():
        per = hidden // 8

        def body(i, _):
            at = pl.ds(pl.multiple_of(i * per, per), per)
            refs["act_load"](i).wait()
            grad = mm_at(refs["act"][:, at], refs["gffn"][...]).astype(BF)
            refs["d2"][:, :, lax.div(i, 2), lax.rem(i, 2)] = grad.reshape(2, 2, per // 4, width)
            return 0

        lax.fori_loop(0, 8, body, 0)

    def through_ffn(hooks):
        gain, scale_one = row_of(G2_ROW), row_of(SA_ROW)

        def body(i, _):
            at = pl.ds(pl.multiple_of(i * TILE, TILE), TILE)
            grad_ffn = refs["gffn"][at, :]
            for c in range(parts):
                cols = slice(c * width, (c + 1) * width)
                grad_act = mm_bt(grad_ffn, hidden_rows(refs["w2"], c))
                pre = (grad_act * refs["slope"][at, cols].astype(F32)).astype(BF)
                refs["slope"][at, cols] = pre
                acc[FB1_ROW + c] += fold(pre.astype(F32))
            grad = mm_bt(refs["slope"][at, :], jnp.concatenate([block(refs["w1"], c) for c in range(parts)], axis=1))
            hat, inv = norm_parts(refs["resid"][at, :])
            acc[G2_ROW] += fold(grad * hat)
            acc[B2_ROW] += fold(grad)
            u = grad * gain
            back = inv * (u - jnp.mean(u, axis=-1, keepdims=True) - hat * jnp.mean(u * hat, axis=-1, keepdims=True))
            valid = lane_tile(refs["seg_col"][at, :], width // 128) < refs["pad"]
            grad_resid = jnp.where(valid, refs["cot"][at, :], 0.0) + back
            refs["resid"][at, :] = grad_resid
            grad_proj = (scale_one * grad_resid).astype(BF)
            refs["gproj"][at, :] = grad_proj
            acc[OB_ROW] += fold(grad_proj.astype(F32))
            refs["gmixed"][at, :] = mm_bt(grad_proj, block(refs["wa"], 3)).astype(BF)
            run_hooks(hooks, i)
            return 0

        lax.fori_loop(0, tiles, body, 0)

    def weight_one(side):
        def body(i, _):
            at = pl.ds(pl.multiple_of(i * half, half), half)
            for c in range(parts):
                first = c * width + side * half
                grad = mm_at(refs["n2"][:, at], refs["slope"][:, first : first + half]).astype(BF)
                refs["d1"][c // 2, c % 2, pl.ds(i * 2, 2), :, :, side * half : (side + 1) * half] = grad.reshape(
                    2, 2, piece, half
                )
            return 0

        lax.fori_loop(0, 2, body, 0)

    def weight_out():
        def body(i, _):
            at = pl.ds(pl.multiple_of(i * half, half), half)
            grad = mm_at(refs["mixed"][:, at], refs["gproj"][...])
            low = grad.astype(BF)
            for j in range(2):
                refs["da0"][1, j, pl.ds(i * 2, 2)] = low[:, j * half : (j + 1) * half].reshape(2, 2, piece, half)
            w_out = refs["wa"][1, 1, pl.ds(i * 2, 2)].reshape(half, width)
            acc[SA_ROW] += fold(grad * w_out.astype(F32))
            return 0

        lax.fori_loop(0, 2, body, 0)

    def attend_back(first, last, hooks):
        def in_copy(step):
            slot = lax.rem(step, 2)
            return pltpu.make_async_copy(refs["prob_in"].at[step], refs["slot"].at[slot], refs["slot_sem"].at[slot])

        if first == 0:
            in_copy(0).start()

        def body(step, _):
            @pl.when(step + 1 < rows * pairs)
            def _():
                in_copy(step + 1).start()

            in_copy(step).wait()
            attention_backward(
                rows, slots, pairs, width, refs["qkv"], refs["slot"].at[lax.rem(step, 2)], refs["mixed"],
                refs["gmixed"], refs["qkv"], lax.rem(step, rows), lax.div(step, rows),
            )
            run_hooks(hooks, step)
            return 0

        lax.fori_loop(first, last, body, 0)

    def weight_slabs(target, slabs, per):
        wide = per * 128

        def body(i, _):
            at = pl.ds(pl.multiple_of(i * half, half), half)
            found = [refs["qkv"][:, part * width + p * 128 : part * width + (p + 1) * 128] for part, p in slabs]
            grad = mm_at(refs["n1"][:, at], jnp.concatenate(found, axis=1)).astype(BF)
            for j in range(len(slabs) // per):
                target[j // 2, j % 2, pl.ds(i * 2, 2)] = grad[:, j * wide : (j + 1) * wide].reshape(2, 2, piece, wide)
            return 0

        lax.fori_loop(0, 2, body, 0)

    def finish_tokens(hooks):
        gain = row_of(G1_ROW)

        def body(i, _):
            at = pl.ds(pl.multiple_of(i * TILE, TILE), TILE)
            grad = mm_bt(refs["qkv"][at, :], jnp.concatenate([block(refs["wa"], c) for c in range(3)], axis=1))
            hat, inv = norm_parts(refs["tok"][at, :])
            acc[G1_ROW] += fold(grad * hat)
            acc[B1_ROW] += fold(grad)
            acc[QB_ROW] += fold(refs["qkv"][at, :width].astype(F32))
            acc[VB_ROW] += fold(refs["qkv"][at, 2 * width :].astype(F32))
            u = grad * gain
            back = inv * (u - jnp.mean(u, axis=-1, keepdims=True) - hat * jnp.mean(u * hat, axis=-1, keepdims=True))
            refs["tok"][at, :] = refs["resid"][at, :] + back
            refs["tile_out"](i)
            run_hooks(hooks, i)
            return 0

        lax.fori_loop(0, tiles, body, 0)

    def vector_sums():
        lines = [jnp.sum(acc[i], axis=0, keepdims=True) for i in range(VEC_ROWS)]
        lines[SA_ROW] = (lines[SA_ROW] + row_of(OB_ROW) * lines[OB_ROW]) / row_of(SA_ROW)
        return jnp.concatenate(lines, axis=0)

    return weight_two, through_ffn, weight_one, weight_out, attend_back, weight_slabs, finish_tokens, vector_sums


ANY = pl.BlockSpec(memory_space=pl.ANY)
INSIDE = pl.BlockSpec(memory_space=pltpu.VMEM)
SCALARS = pl.BlockSpec(memory_space=pltpu.SMEM)
DMA = pltpu.SemaphoreType.DMA


def position():
    f, d = lax.axis_index("fsdp"), lax.axis_index("dp")
    return lax.div(f, 2), lax.rem(f, 2), lax.div(d, 2), lax.rem(d, 2)


def device(z, y, x, c):
    return (z * 2 + y, x * 2 + c)


def z_partners(z):
    return [z + 1 - 2 * lax.rem(z, 2), 3 - z, lax.rem(z + 2, 4)]


def remote(src, dst, send, recv, target):
    return pltpu.make_async_remote_copy(
        src_ref=src, dst_ref=dst, send_sem=send, recv_sem=recv, device_id=target, device_id_type=MESH
    )


def greet(targets):
    barrier = pltpu.get_barrier_semaphore()
    for target in targets:
        pl.semaphore_signal(barrier, inc=1, device_id=target, device_id_type=MESH)


def meet(targets):
    pl.semaphore_wait(pltpu.get_barrier_semaphore(), len(targets))


class Gather:
    def __init__(self, t, buf, sems, place):
        self.t, self.buf, self.place = t, buf, place
        self.zs, self.zr, self.ys, self.yr, self.xs, self.xr, self.cs, self.cr = sems
        z = place[0]
        low = z < 2
        self.others = [z + 1 - 2 * lax.rem(z, 2), jnp.where(low, 2, 1), jnp.where(low, 3, 0)]
        self.inner = jnp.logical_or(z == 1, z == 2)

    def shard(self, j):
        z, y, _, _ = self.place
        if j == 7:
            return z, y
        if j < 3:
            return self.others[j], y
        return (z if j == 3 else self.others[j - 4]), 1 - y

    def part(self, z, y, p):
        _, _, x, c = self.place
        rows = self.buf.shape[4]
        if p == 0:
            return self.buf.at[x, c, z, y, pl.ds(0, SHARED)]
        return self.buf.at[:, c, z, y, pl.ds(SHARED, rows - SHARED)]

    def z_copy(self, origin, i, p, target):
        _, y, x, c = self.place
        ref = self.part(origin, y, p)
        return remote(ref, ref, self.zs.at[self.t, i, p], self.zr.at[self.t, origin, p], device(target, y, x, c))

    def outward(self, k, p):
        z = self.place[0]
        return self.z_copy(self.others[k], 2 + k, p, 3 - z if k == 0 else self.others[0])

    def y_copy(self, j, p):
        z, y, x, c = self.place
        zs, ys = self.shard(j)
        ref = self.part(zs, ys, p)
        return remote(ref, ref, self.ys.at[self.t, zs, p], self.yr.at[self.t, zs, p], device(z, 1 - y, x, c))

    def x_copy(self, j, qx):
        z, y, x, c = self.place
        zs, ys = self.shard(j)
        s = zs * 2 + ys
        ref = self.buf.at[qx, c, zs, ys, pl.ds(0, SHARED)]
        return remote(ref, ref, self.xs.at[self.t, s], self.xr.at[self.t, s], device(z, y, 1 - x, c))

    def c_copy(self, j, qx, qc):
        z, y, x, c = self.place
        zs, ys = self.shard(j)
        s = zs * 2 + ys
        ref = self.buf.at[qx, qc, zs, ys]
        return remote(ref, ref, self.cs.at[self.t, s, qx], self.cr.at[self.t, s, qx], device(z, y, x, 1 - c))

    def onward(self, j, p):
        _, _, x, c = self.place
        if p == 0:
            self.x_copy(j, x).start()
        else:
            self.c_copy(j, x, c).start()

    def send_z(self):
        z = self.place[0]
        for p in range(2):
            self.z_copy(z, 0, p, self.others[0]).start()

        @pl.when(self.inner)
        def _():
            for p in range(2):
                self.z_copy(z, 1, p, 3 - z).start()

    def send_y(self):
        for p in range(2):
            self.y_copy(7, p).start()

    def z_step(self, k, p):
        self.z_copy(self.others[k], 0, p, self.others[0]).wait_recv()

        @pl.when(self.inner)
        def _():
            self.outward(k, p).start()

        self.y_copy(k, p).start()
        self.onward(k, p)

    def y_step(self, k, p):
        self.y_copy(3 + k, p).wait_recv()
        self.onward(3 + k, p)

    def x_step(self, j):
        _, _, x, c = self.place
        self.x_copy(j, 1 - x).wait_recv()
        self.c_copy(j, 1 - x, c).start()

    def done(self):
        _, _, x, c = self.place
        for j in range(7):
            for qx in (x, 1 - x):
                self.c_copy(j, qx, 1 - c).wait_recv()

    def finish(self):
        z, _, x, c = self.place
        for p in range(2):
            self.z_copy(z, 0, p, self.others[0]).wait_send()

        @pl.when(self.inner)
        def _():
            for p in range(2):
                self.z_copy(z, 1, p, 3 - z).wait_send()
                for k in range(3):
                    self.outward(k, p).wait_send()

        for j in (7, 0, 1, 2):
            for p in range(2):
                self.y_copy(j, p).wait_send()
        for j in range(7):
            self.x_copy(j, x).wait_send()
            for qx in (x, 1 - x):
                self.c_copy(j, qx, c).wait_send()


START_TURNS = ("asz", "asy")
NORM_TURNS = {
    0: ("az10", "az00"),
    1: ("ay00", "az11"),
    2: ("ay01", "az01", "az20", "az21", "ay20", "bsz", "ax3", "ay10"),
    3: ("ax1", "ay30", "ay21", "bsy", "ax2", "ay11", "ax4", "ax5", "ay31", "bz10", "ax0", "ax6", "bz11", "bz00",
        "bz01", "by00"),
}
PROJECT_TURNS = {
    1: ("bx0",),
    2: ("bz20", "by20"),
}
ATTEND_TURNS = {
    0: ("bz21", "csz"),
    2: ("by10",),
    3: ("csy", "by30"),
    4: ("by21",),
    6: ("cz10",),
    8: ("by01", "cz00", "by11", "cz01", "cy00", "cz11", "bx4", "bx5", "bx3", "bx1", "bx2", "by31"),
    9: ("bx6",),
    11: ("cy20", "cz20", "cy10"),
}
FEED_TURNS = {
    0: ("cz21",),
    1: ("cy30",),
    2: ("cx0", "cy01", "cx2", "cy11", "cy21", "cx5", "cx4", "cy31", "cx3", "cx1", "cx6"),
}


def turn(gathers, name):
    gather, kind = gathers["abc".index(name[0])], name[1:]
    if kind == "sz":
        return gather.send_z
    if kind == "sy":
        return gather.send_y
    if kind[0] == "x":
        return functools.partial(gather.x_step, int(kind[1]))
    step = gather.z_step if kind[0] == "z" else gather.y_step
    return functools.partial(step, int(kind[1]), int(kind[2]))


def turns(gathers, table):
    return {k: [turn(gathers, name) for name in names] for k, names in table.items()}


def forward_kernel(dims, pad, comm, *all_refs):
    rows, slots, width, hidden = dims
    tokens = rows * slots
    tiles = tokens // TILE
    all_refs = list(all_refs)
    take = lambda n: [all_refs.pop(0) for _ in range(n)]
    lengths, vec_in, tok_in, cot_in = take(4)
    wqkv_in, wout_in, w1_in, w2_in = take(4) if comm else [None] + take(3)
    out, n1_out, qkv_out, prob_out, mixed_out, resid_out, n2_out, act_out, slope_out, gffn_out, acc, vec = take(12)
    weights_out = take(3) if comm else []
    tok, cot, wa, w1, w2, n1, qkv, slot, mixed, resid, n2, act, slope, gffn, seg_col, seg_row = take(16)
    slot_sem, in_sem, out_sem, tile_sem = take(4)
    moves = [(tok_in, tok), (cot_in, cot)]
    if comm:
        place = position()
        z, y, x, c = place
        vec_land, vs, vr = take(3)
        sems = take(8)
        ga, g1, g2 = [Gather(t, buf, sems, place) for t, buf in enumerate((wa, w1, w2))]
        for q in range(4):
            source = wqkv_in.at[:, q * width : (q + 1) * width] if q < 3 else wout_in
            moves.append((source, wa.at[q // 2, q % 2, z, y]))
        for q in range(4):
            moves.append((w1_in.at[:, q * width : (q + 1) * width], w1.at[q // 2, q % 2, z, y]))
        moves.append((w2_in, w2.at[:, :, z, y]))
    else:
        moves += [(wout_in, wa), (w1_in, w1), (w2_in, w2)]
    loads = [pltpu.make_async_copy(a, b, in_sem.at[i]) for i, (a, b) in enumerate(moves)]
    for copy in loads[2:] + loads[:2]:
        copy.start()

    def tile_copies(i, pairs, base):
        at = pl.ds(pl.multiple_of(i * TILE, TILE), TILE)
        return [pltpu.make_async_copy(a.at[at], b.at[at], tile_sem.at[i, base + j]) for j, (a, b) in enumerate(pairs)]

    ones = [(resid, resid_out), (n2, n2_out), (act, act_out), (slope, slope_out)]
    twos = [(tok, out), (gffn, gffn_out)]

    def tile_one(i):
        for copy in tile_copies(i, ones, 0):
            copy.start()

    def tile_two(i):
        for copy in tile_copies(i, twos, len(ones)):
            copy.start()

    refs = dict(
        vec=vec, tok=tok, cot=cot, wa=wa, w1=w1, w2=w2, n1=n1, qkv=qkv, slot=slot, mixed=mixed, resid=resid, n2=n2,
        act=act, slope=slope, gffn=gffn, seg_col=seg_col, seg_row=seg_row, slot_sem=slot_sem, prob_out=prob_out,
        acc=acc, pad=pad, tile_one=tile_one, tile_two=tile_two,
    )
    norm_one, project, attend, feed_one, feed_two = forward_phases(dims, refs)
    pairs_out = [(n1, n1_out), (qkv, qkv_out), (mixed, mixed_out)]
    if comm:
        pairs_out += list(zip((wa, w1, w2), weights_out))
    stores = [pltpu.make_async_copy(a, b, out_sem.at[i]) for i, (a, b) in enumerate(pairs_out)]
    if comm:
        others = z_partners(z)
        peers = [device(o, y, x, c) for o in others] + [device(o, 1 - y, x, c) for o in [z] + others]
        known = peers + [device(z, y, 1 - x, c), device(z, y, x, 1 - c)]
        greet(known)
        meet(known)
        mine = z * 2 + y
        vec_sends = [
            remote(vec_in, vec_land.at[mine], vs.at[k], vr.at[mine], peer) for k, peer in enumerate(peers)
        ]
        for copy in vec_sends:
            copy.start()
        gathers = (ga, g1, g2)
        for copy in loads[2:6]:
            copy.wait()
        for name in START_TURNS:
            turn(gathers, name)()
        fill_segments(lengths, rows, slots, seg_col, seg_row)
        vec_land[mine] = vec_in[...]
        vec[...] = jnp.zeros_like(vec)
        sources = [(o, y) for o in others] + [(o, 1 - y) for o in [z] + others]
        for k, (zs, ys) in enumerate(sources):
            remote(vec_in, vec_land.at[zs * 2 + ys], vs.at[k], vr.at[zs * 2 + ys], peers[k]).wait_recv()
        spread_vectors(vec_land, vec, width)
        for copy in loads[6:]:
            copy.wait()
        loads[0].wait()
        norm_one(turns(gathers, NORM_TURNS))
        stores[0].start()
        ga.done()
        stores[3].start()
        project(turns(gathers, PROJECT_TURNS))
        stores[1].start()
        attend(turns(gathers, ATTEND_TURNS))
        stores[2].start()
        g1.done()
        stores[4].start()
        feed_one(turns(gathers, FEED_TURNS))
        g2.done()
        stores[5].start()
        loads[1].wait()
        feed_two()
        for gather in (ga, g1, g2):
            gather.finish()
        for copy in vec_sends:
            copy.wait_send()
    else:
        fill_segments(lengths, rows, slots, seg_col, seg_row)
        vec[...] = vec_in[...].astype(F32)
        loads[0].wait()
        norm_one({})
        stores[0].start()
        loads[2].wait()
        project({})
        stores[1].start()
        attend({})
        stores[2].start()
        for copy in loads[3:] + loads[1:2]:
            copy.wait()
        feed_one({})
        feed_two()
    for copy in stores:
        copy.wait()

    def finish(i, _):
        for copy in tile_copies(i, ones, 0) + tile_copies(i, twos, len(ones)):
            copy.wait()
        return 0

    lax.fori_loop(0, tiles, finish, 0)


def spread_vectors(land, vec, width):
    shards = land.shape[0]
    piece = width // shards
    lines = jnp.concatenate([land[s].astype(F32)[:FB1_ROW, :piece] for s in range(shards)], axis=1)
    vec[:FB1_ROW, :] = lines
    per = 3
    tiles = [land[s, FB1_ROW + j : FB1_ROW + j + 1, :].astype(F32) for s in range(shards) for j in range(per)]
    wide = width // 128
    for r in range(len(tiles) // wide):
        vec[FB1_ROW + r : FB1_ROW + r + 1, :] = jnp.concatenate(tiles[r * wide : (r + 1) * wide], axis=1)


def forward_call(dims, pad, comm):
    rows, slots, width, hidden = dims
    tokens = rows * slots
    tiles, pairs = tokens // TILE, width // 128
    piece = width // 8
    wide = prob_offsets(slots // QB)[1]
    S = jax.ShapeDtypeStruct
    matrix = (2, 2, 4, 2, piece, width)
    shapes = [
        S((tokens, width), F32), S((tokens, width), BF), S((tokens, 3 * width), BF),
        S((rows * pairs, 2 * QB, wide), BF), S((tokens, width), BF), S((tokens, width), F32), S((tokens, width), BF),
        S((tokens, hidden), BF), S((tokens, hidden), BF), S((tokens, width), BF), S((2, 8, width), F32),
        S((VEC_ROWS, width), F32),
    ]
    V = pltpu.VMEM
    scratch = [
        V((tokens, width), F32), V((tokens, width), F32), V(matrix, BF), V(matrix, BF), V(matrix, BF),
        V((tokens, width), BF), V((tokens, 3 * width), BF), V((2, 2 * QB, wide), BF),
        V((tokens, width), BF), V((tokens, width), F32), V((tokens, width), BF), V((tokens, hidden), BF),
        V((tokens, hidden), BF), V((tokens, width), BF), V((tokens, 128), jnp.int32), V((rows, 8, slots), jnp.int32),
        DMA((2,)), DMA((11,)), DMA((6,)), DMA((tiles, 6)),
    ]
    params = dict(vmem_limit_bytes=VMEM_LIMIT)
    if comm:
        shapes += [S(matrix, BF)] * 3
        scratch += [V((8, VEC_ROWS, 128), BF), DMA((7,)), DMA((8,))]
        scratch += [DMA((3, 5, 2)), DMA((3, 4, 2)), DMA((3, 4, 2)), DMA((3, 4, 2)), DMA((3, 8)), DMA((3, 8)),
                    DMA((3, 8, 2)), DMA((3, 8, 2))]
        params.update(collective_id=0, has_side_effects=True)
    return pl.pallas_call(
        functools.partial(forward_kernel, dims, pad, comm),
        out_shape=shapes,
        in_specs=[SCALARS, INSIDE] + [ANY] * (6 if comm else 5),
        out_specs=[ANY] * 10 + [INSIDE, INSIDE] + ([ANY] * 3 if comm else []),
        scratch_shapes=scratch,
        compiler_params=pltpu.CompilerParams(**params),
        name="forward",
    )


class Reduce:
    def __init__(self, t, grad, land, final, sems, place):
        self.t, self.grad, self.final, self.place = t, grad, final, place
        self.from_core, self.from_x, self.from_y, self.from_yx, self.from_xy, self.from_z = land
        self.send, self.recv = sems
        rows = grad.shape[4]
        self.first, self.second = pl.ds(0, rows // 2), pl.ds(rows // 2, rows // 2)

    def copy(self, i, src, dst, target, slot=None):
        slot = i if slot is None else slot
        return remote(src, dst, self.send.at[self.t, i], self.recv.at[self.t, slot], target)

    def core_copy(self):
        z, y, x, c = self.place
        return [
            self.copy(i, self.grad.at[q, 1 - c], self.from_core.at[q], device(z, y, x, 1 - c)) for i, q in enumerate((0, 1))
        ]

    def one_copy(self):
        z, y, x, c = self.place
        g = self.grad
        return [
            self.copy(2, g.at[1 - x, c, :, :, self.first], self.from_x, device(z, y, 1 - x, c)),
            self.copy(3, g.at[:, c, :, 1 - y, self.second], self.from_y, device(z, 1 - y, x, c)),
        ]

    def two_copy(self):
        z, y, x, c = self.place
        g = self.grad
        return [
            self.copy(4, g.at[x, c, :, 1 - y, self.first], self.from_xy, device(z, 1 - y, x, c)),
            self.copy(5, g.at[1 - x, c, :, y, self.second], self.from_yx, device(z, y, 1 - x, c)),
        ]

    def z_copy(self):
        z, y, x, c = self.place
        return [
            self.copy(6 + k, self.grad.at[x, c, o, y], self.from_z.at[k], device(o, y, x, c))
            for k, o in enumerate(z_partners(z))
        ]

    def across_copy(self):
        z, y, x, c = self.place
        own = self.final.at[x, c]
        return self.copy(9, own, own, device(z, y, 1 - x, c))

    def beside_copy(self):
        z, y, x, c = self.place
        own = self.final.at[x, c]
        return self.copy(10, own, own, device(z, y, x, 1 - c))

    def relay_copy(self):
        z, y, x, c = self.place
        other = self.final.at[1 - x, c]
        return self.copy(11, other, other, device(z, y, x, 1 - c))

    def start(self):
        for copy in self.core_copy():
            copy.start()

    def core_done(self):
        z, y, x, c = self.place
        for copy in self.core_copy():
            copy.wait_recv()

        def body(i, _):
            q, zs = lax.div(i, 4), lax.rem(i, 4)
            total = self.grad[q, c, zs].astype(F32) + self.from_core[q, zs].astype(F32)
            self.grad[q, c, zs] = total.astype(BF)
            return 0

        lax.fori_loop(0, 8, body, 0)
        for copy in self.one_copy():
            copy.start()

    def one_done(self):
        z, y, x, c = self.place
        g = self.grad
        for copy in self.one_copy():
            copy.wait_recv()

        def body(zs, _):
            total = g[x, c, zs, :, self.first].astype(F32) + self.from_x[zs].astype(F32)
            g[x, c, zs, :, self.first] = total.astype(BF)
            total = g[:, c, zs, y, self.second].astype(F32) + self.from_y[:, zs].astype(F32)
            g[:, c, zs, y, self.second] = total.astype(BF)
            return 0

        lax.fori_loop(0, 4, body, 0)
        for copy in self.two_copy():
            copy.start()

    def two_done(self):
        z, y, x, c = self.place
        g = self.grad
        for copy in self.two_copy():
            copy.wait_recv()

        def body(zs, _):
            total = g[x, c, zs, y, self.first].astype(F32) + self.from_xy[zs].astype(F32)
            g[x, c, zs, y, self.first] = total.astype(BF)
            total = g[x, c, zs, y, self.second].astype(F32) + self.from_yx[zs].astype(F32)
            g[x, c, zs, y, self.second] = total.astype(BF)
            return 0

        lax.fori_loop(0, 4, body, 0)
        for copy in self.z_copy():
            copy.start()

    def z_done(self):
        z, y, x, c = self.place
        for copy in self.z_copy():
            copy.wait_recv()
        total = self.grad[x, c, z, y].astype(F32)
        for k in range(3):
            total = total + self.from_z[k].astype(F32)
        self.final[x, c] = total.astype(BF)
        self.across_copy().start()
        self.beside_copy().start()

    def relay(self):
        self.across_copy().wait_recv()
        self.relay_copy().start()

    def done(self):
        self.beside_copy().wait_recv()
        self.relay_copy().wait_recv()

    def finish(self):
        copies = self.core_copy() + self.one_copy() + self.two_copy() + self.z_copy()
        for copy in copies + [self.across_copy(), self.beside_copy(), self.relay_copy()]:
            copy.wait_send()


class VectorSum:
    def __init__(self, ref, land, z_land, send, recv, place):
        self.ref, self.land, self.z_land, self.send, self.recv, self.place = ref, land, z_land, send, recv, place
        z, y, x, c = place
        targets = [device(z, y, x, 1 - c), device(z, y, 1 - x, c), device(z, 1 - y, x, c)]
        self.pair = [
            remote(ref.at[i], land.at[i], send.at[i], recv.at[i], target) for i, target in enumerate(targets)
        ]
        self.along = [
            remote(ref.at[3], z_land.at[z], send.at[3 + k], recv.at[3 + z], device(o, y, x, c))
            for k, o in enumerate(z_partners(z))
        ]

    def start(self, value):
        self.ref[0] = value
        self.pair[0].start()

    def step(self, i):
        self.pair[i].wait_recv()
        self.ref[i + 1] = self.ref[i] + self.land[i]
        if i < 2:
            self.pair[i + 1].start()
        else:
            for copy in self.along:
                copy.start()

    def done(self):
        z, y, x, c = self.place
        self.z_land[z] = self.ref[3]
        for k, o in enumerate(z_partners(z)):
            remote(
                self.ref.at[3], self.z_land.at[o], self.send.at[3 + k], self.recv.at[3 + o], device(o, y, x, c)
            ).wait_recv()
        total = self.z_land[0] + self.z_land[1]
        total = total + self.z_land[2]
        return total + self.z_land[3]

    def finish(self):
        for copy in self.pair + self.along:
            copy.wait_send()


CHUNKS = ("2a", "2b", "1a", "1b", "a", "b", "c")
AFTER_PHASE = {
    "two": ("2a.start",),
    "one": ("1a.start", "2b.one"),
    "other": ("1a.core", "1b.start"),
    "out": ("2b.two",),
    "b": ("b.start", "1b.two", "a.one"),
    "c": ("c.start", "a.two"),
    "end": ("v.start", "c.one", "b.two", "v.0", "1b.z", "2b.z", "a.z", "v.1", "c.two", "v.2", "b.z", "1a.z",
        "2a.relay", "c.z", "2b.relay", "a.relay", "1b.relay", "b.relay", "2b.done", "1b.done", "1a.relay", "2a.done",
        "c.relay", "v.done", "c.done", "a.done", "1a.done", "b.done"),
}
WITHIN_PHASE = {
    "ffn": {
        0: ("2a.core",),
        1: ("2b.start",),
        2: ("2b.core",),
        3: ("2a.one",),
    },
    "attend": {
        0: ("1b.core",),
        2: ("1a.one",),
        4: ("2a.two", "a.start", "1b.one"),
        6: ("1a.two", "a.core"),
        8: ("2a.z",),
        11: ("b.core",),
    },
    "tokens": {
        0: ("c.core",),
        1: ("b.one",),
    },
}


def backward_kernel(dims, pad, comm, *all_refs):
    rows, slots, width, hidden = dims
    tokens = rows * slots
    tiles, pairs = tokens // TILE, width // 128
    half = width // 2
    all_refs = list(all_refs)
    take = lambda n: [all_refs.pop(0) for _ in range(n)]
    lengths, vec, acc_in, tok_in, cot_in, wa_in, w1_in, w2_in = take(8)
    n1_in, qkv_in, prob_in, mixed_in, resid_in, n2_in, act_in, slope_in, gffn_in = take(9)
    if comm:
        gtok_out, gqkv_out, gout_out, g1_out, g2_out, sums = take(6)
    else:
        gtok_out, da_out, d1_out, d2_out, sums = take(5)
    cot, wa, w1, w2, slot, mixed, resid, n2, act, slope, gffn, gproj, d2, acc, seg_col, seg_row = take(16)
    slot_sem, in_sem, out_sem, tile_sem, act_sem = take(5)
    qkv, n1, tok = act.at[:, : 3 * width], act.at[:, 3 * width :], cot
    da0, da1 = w2.at[:, :, :, :, :, :half], w2.at[:, :, :, :, :, half:]
    pair_slabs = [(part, p) for p in range(pairs) for part in range(3)]
    ahead, late = pair_slabs[:6], pair_slabs[6:]
    moves = [
        (gffn_in, gffn), (w2_in, w2), (slope_in, slope), (w1_in, w1), (resid_in, resid), (cot_in, cot),
        (wa_in, wa), (n2_in, n2), (mixed_in, mixed), (qkv_in, qkv), (n1_in, n1), (tok_in, tok),
    ]
    loads = [pltpu.make_async_copy(a, b, in_sem.at[i]) for i, (a, b) in enumerate(moves)]

    def act_load(i):
        per = hidden // 8
        at = pl.ds(pl.multiple_of(i * per, per), per)
        return pltpu.make_async_copy(act_in.at[:, at], act.at[:, at], act_sem.at[i])

    loads[0].start()
    for i in range(8):
        act_load(i).start()
    for copy in loads[1:9]:
        copy.start()

    def tile_copy(i):
        at = pl.ds(pl.multiple_of(i * TILE, TILE), TILE)
        return pltpu.make_async_copy(tok.at[at], gtok_out.at[at], tile_sem.at[i])

    refs = dict(
        vec=vec, acc=acc, tok=tok, cot=cot, wa=wa, w1=w1, w2=w2, n1=n1, qkv=qkv, slot=slot, mixed=mixed,
        resid=resid, n2=n2, act=act, slope=slope, gffn=gffn, gproj=gproj, gmixed=gffn, d2=d2, d1=w1, da0=da0, da1=da1,
        seg_col=seg_col, seg_row=seg_row, slot_sem=slot_sem, prob_in=prob_in, pad=pad,
        tile_out=lambda i: tile_copy(i).start(), act_load=act_load,
    )
    (
        weight_two, through_ffn, weight_one, weight_out, attend_back, weight_slabs, finish_tokens, vector_sums,
    ) = backward_phases(dims, refs)
    stores = []
    if comm:
        place = position()
        z, y, x, c = place
        core_land = take(2)
        lands = [take(5) for _ in CHUNKS]
        finals = take(len(CHUNKS))
        sems = take(2)
        vec_ref, vec_land, vec_z, vec_send, vec_recv, final_sem = take(6)
        sides = [(0, half), (half, half), (0, half), (half, half), (0, half), (half, 256), (half + 256, 128)]
        chunks = {}
        for t, (name, (first, wide)) in enumerate(zip(CHUNKS, sides)):
            side = (slice(None),) * 5 + (slice(first, first + wide),)
            grad, land = (d2, w1, w2)[t // 2 if t < 4 else 2], core_land[1 if name in ("1a", "1b") else 0]
            chunks[name] = Reduce(t, grad.at[side], [land.at[side[1:]]] + lands[t], finals[t], sems, place)
        vector = VectorSum(vec_ref, vec_land, vec_z, vec_send, vec_recv, place)
        known = [device(o, y, x, c) for o in z_partners(z)]
        known += [device(z, 1 - y, x, c), device(z, y, 1 - x, c), device(z, y, x, 1 - c)]
        greet(known)

    def targets(name):
        final = finals[CHUNKS.index(name)]
        if name in ("2a", "2b"):
            first = half * (name == "2b")
            return [(final, g2_out.at[:, :, :, first : first + half])]
        found = []
        for q in range(4):
            ref = final.at[q // 2, q % 2]
            if name in ("1a", "1b"):
                first = q * width + half * (name == "1b")
                found.append((ref, g1_out.at[:, first : first + half]))
            elif name == "a" and q >= 2:
                found.append((ref, gout_out.at[:, (q - 2) * half : (q - 1) * half]))
            else:
                slabs = {"a": ahead[q * 3 : q * 3 + 3], "b": late[q * 2 : q * 2 + 2], "c": late[8 + q : 9 + q]}[name]
                for j, (part, p) in enumerate(slabs):
                    at = part * width + p * 128
                    found.append((ref.at[:, j * 128 : (j + 1) * 128], gqkv_out.at[:, at : at + 128]))
        return found

    def deliver(name):
        chunks[name].done()
        for i, (a, b) in enumerate(targets(name)):
            copy = pltpu.make_async_copy(a, b, final_sem.at[CHUNKS.index(name), i])
            copy.start()
            stores.append(copy)

    def sum_vectors():
        sums[...] = vector.done()

    def turn_of(name):
        chunk, step = name.split(".")
        if chunk == "v":
            if step == "start":
                return lambda: vector.start(vector_sums())
            return sum_vectors if step == "done" else functools.partial(vector.step, int(step))
        if step == "done":
            return functools.partial(deliver, chunk)
        methods = dict(start="start", core="core_done", one="one_done", two="two_done", z="z_done", relay="relay")
        return getattr(chunks[chunk], methods[step])

    def after(phase):
        if comm:
            for name in AFTER_PHASE.get(phase, ()):
                turn_of(name)()

    def within(phase, first, last):
        table = WITHIN_PHASE.get(phase, {}) if comm else {}
        return {k: [turn_of(name) for name in names] for k, names in table.items() if first <= k < last}

    fill_segments(lengths, rows, slots, seg_col, seg_row)
    acc[...] = jnp.zeros_like(acc)
    acc[SF_ROW] = acc_in[0]
    acc[FB2_ROW] = acc_in[1]
    loads[0].wait()
    weight_two()
    for copy in loads[9:11]:
        copy.start()
    if comm:
        meet(known)
    after("two")
    for copy in loads[1:7]:
        copy.wait()
    through_ffn(within("ffn", 0, tiles))
    loads[11].start()
    loads[7].wait()
    for side in range(2):
        weight_one(side)
        after(("one", "other")[side])
    loads[8].wait()
    weight_out()
    after("out")
    loads[9].wait()
    early, most = rows * 2, rows * 5
    attend_back(0, early, within("attend", 0, early))
    loads[10].wait()
    weight_slabs(da0, ahead, 3)
    after("a")
    if comm:
        attend_back(early, most, within("attend", early, most))
        weight_slabs(da1.at[:, :, :, :, :, :256], late[:8], 2)
        after("b")
        attend_back(most, rows * pairs, within("attend", most, rows * pairs))
        weight_slabs(da1.at[:, :, :, :, :, 256:], late[8:], 1)
        after("c")
    else:
        attend_back(early, rows * pairs, {})
        weight_slabs(da1, late, 3)
    loads[11].wait()
    finish_tokens(within("tokens", 0, tiles))
    if comm:
        after("end")
        for chunk in chunks.values():
            chunk.finish()
        vector.finish()
    else:
        sums[...] = vector_sums()
        stores = [
            pltpu.make_async_copy(a, b, out_sem.at[i])
            for i, (a, b) in enumerate([(d2, d2_out), (w1, d1_out), (w2, da_out)])
        ]
        for copy in stores:
            copy.start()
    for copy in stores:
        copy.wait()

    def finish(i, _):
        tile_copy(i).wait()
        return 0

    lax.fori_loop(0, tiles, finish, 0)


def backward_call(dims, pad, comm):
    rows, slots, width, hidden = dims
    tokens = rows * slots
    tiles, pairs = tokens // TILE, width // 128
    piece, half = width // 8, width // 2
    wide = prob_offsets(slots // QB)[1]
    S = jax.ShapeDtypeStruct
    matrix = (2, 2, 4, 2, piece, width)
    V = pltpu.VMEM
    tall = lambda dtype: V((tokens, width), dtype)
    scratch = [
        tall(F32), V(matrix, BF), V(matrix, BF), V(matrix, BF), V((2, 2 * QB, wide), BF), tall(BF), tall(F32), tall(BF),
        V((tokens, hidden), BF), V((tokens, hidden), BF), tall(BF), tall(BF), V(matrix, BF), V((VEC_ROWS, 8, width), F32),
        V((tokens, 128), jnp.int32), V((rows, 8, slots), jnp.int32), DMA((2,)), DMA((12,)), DMA((3,)), DMA((tiles,)),
        DMA((8,)),
    ]
    params = dict(vmem_limit_bytes=VMEM_LIMIT)
    shapes = [S((tokens, width), F32)]
    if comm:
        shapes += [
            S((piece, 3 * width), BF), S((piece, width), BF), S((piece, hidden), BF), S((2, 2, piece, width), BF),
        ]
        scratch += [V((2, 4, 2, piece, width), BF)] * 2
        columns = (half,) * 5 + (256, 128)
        for cols in columns:
            scratch += [
                V((4, 2, piece // 2, cols), BF), V((2, 4, piece // 2, cols), BF), V((4, piece // 2, cols), BF),
                V((4, piece // 2, cols), BF), V((3, piece, cols), BF),
            ]
        scratch += [V((2, 2, piece, cols), BF) for cols in columns]
        scratch += [DMA((7, 12)), DMA((7, 12))]
        scratch += [V((4, VEC_ROWS, width), F32), V((3, VEC_ROWS, width), F32), V((4, VEC_ROWS, width), F32)]
        scratch += [DMA((6,)), DMA((7,)), DMA((7, 8))]
        params.update(collective_id=1, has_side_effects=True)
    else:
        shapes += [S(matrix, BF)] * 3
    shapes += [S((VEC_ROWS, width), F32)]
    return pl.pallas_call(
        functools.partial(backward_kernel, dims, pad, comm),
        out_shape=shapes,
        in_specs=[SCALARS, INSIDE, INSIDE] + [ANY] * 14,
        out_specs=[ANY] * (len(shapes) - 1) + [INSIDE],
        scratch_shapes=scratch,
        compiler_params=pltpu.CompilerParams(**params),
        name="backward",
    )


def last_kernel(dims, gtok_in, out_in, gqkv_in, gout_in, g1_in, g2_in, sums_ref, *refs):
    rows, slots, width, hidden = dims
    piece = width // 8
    gtok_out, out_out, gqkv_out, gout_out, g1_out, g2_out, bias_out = refs[:7]
    lines, refs = refs[7 : 7 + len(VECTOR_ROWS)], refs[7 + len(VECTOR_ROWS) :]
    gtok, out = refs[:2]
    low, high = refs[2:6], refs[6:10]
    in_sem, out_sem, tile_sem = refs[10:]
    sources, results = (gqkv_in, gout_in, g1_in, g2_in), (gqkv_out, gout_out, g1_out, g2_out)
    parts = 4
    size = rows * slots // parts

    def token_copies(a, b, k):
        return [
            pltpu.make_async_copy(a.at[pl.ds(i * size, size)], b.at[pl.ds(i * size, size)], tile_sem.at[k, i])
            for i in range(parts)
        ]

    loads = [pltpu.make_async_copy(a, b, in_sem.at[i]) for i, (a, b) in enumerate(zip(sources, low))]
    stores = [pltpu.make_async_copy(a, b, out_sem.at[i]) for i, (a, b) in enumerate(zip(high, results))]
    inward = token_copies(out_in, out, 0) + token_copies(gtok_in, gtok, 1)
    outward = token_copies(out, out_out, 2) + token_copies(gtok, gtok_out, 3)
    for copy in loads + inward:
        copy.start()
    me = lax.axis_index("fsdp")
    mine = sums_ref[:, :piece]
    bias = sums_ref[FB1_ROW : FB1_ROW + 1, : hidden // 8]
    for k in range(1, 8):
        mine = jnp.where(me == k, sums_ref[:, k * piece : (k + 1) * piece], mine)
        row, first = divmod(k * (hidden // 8), width)
        bias = jnp.where(me == k, sums_ref[FB1_ROW + row : FB1_ROW + row + 1, first : first + hidden // 8], bias)
    for ref, row in zip(lines, VECTOR_ROWS):
        ref[...] = mine[row]
    bias_out[...] = bias[0]
    for i in range(4):
        loads[i].wait()
        high[i][...] = low[i][...].astype(F32)
        stores[i].start()
    for a, b in zip(inward, outward):
        a.wait()
        b.start()
    for copy in stores + outward:
        copy.wait()


def last_call(dims, *arrays):
    rows, slots, width, hidden = dims
    tokens, piece = rows * slots, width // 8
    S, V = jax.ShapeDtypeStruct, pltpu.VMEM
    shapes = [(piece, 3 * width), (piece, width), (piece, hidden), (hidden // 8, width)]
    full = [S((tokens, width), F32)] * 2 + [S(shape, F32) for shape in shapes]
    return pl.pallas_call(
        functools.partial(last_kernel, dims),
        out_shape=full + [S((hidden // 8,), F32)] + [S((piece,), F32)] * len(VECTOR_ROWS),
        in_specs=[ANY] * 6 + [INSIDE],
        out_specs=[ANY] * 6 + [INSIDE] * (1 + len(VECTOR_ROWS)),
        scratch_shapes=[V((tokens, width), F32)] * 2 + [V(shape, BF) for shape in shapes] + [V(shape, F32) for shape in shapes]
        + [DMA((4,)), DMA((4,)), DMA((4, 4))],
        compiler_params=pltpu.CompilerParams(vmem_limit_bytes=VMEM_LIMIT),
        name="last",
    )(*arrays)


def local(
    fsdp, dp,
    tokens, lengths, cotangent, ln1_gain, ln1_bias, w_qkv, qkv_bias, w_out, out_bias, scale_attn, ln2_gain, ln2_bias,
    w_fc1, fc1_bias, w_fc2, fc2_bias, scale_ffn,
):
    rows = lengths.shape[0]
    slots, width = tokens.shape[0] // rows, tokens.shape[1]
    hidden = w_fc1.shape[1]
    dims = (rows, slots, width, hidden)
    pad = lengths.shape[1] - 1
    piece = width // 8
    comm = fsdp == 8 and dp == 4
    me = lax.axis_index("fsdp")
    lines = [
        ln1_gain, ln1_bias, qkv_bias[:, 0], qkv_bias[:, 1], out_bias, scale_attn, ln2_gain, ln2_bias, fc2_bias, scale_ffn,
    ]
    if comm:
        rest = fc1_bias.reshape(-1, 128)
        own = jnp.pad(rest, ((FB1_ROW, VEC_ROWS - FB1_ROW - rest.shape[0]), (0, 0)))
        for i, line in enumerate(lines):
            own = own + jnp.pad(line[None], ((i, VEC_ROWS - 1 - i), (0, 128 - piece)))
        forward = forward_call(dims, pad, True)(
            lengths, own, tokens, cotangent, w_qkv, w_out, w_fc1, w_fc2.reshape(2, 2, piece, width)
        )
        out, n1, qkv, prob, mixed, resid, n2, act, slope, gffn, acc, vec, full_a, full_1, full_2 = forward
    else:
        vec = lax.all_gather(jnp.stack(lines, axis=0), "fsdp", axis=1, tiled=True)
        bias_one = lax.all_gather(fc1_bias, "fsdp", axis=0, tiled=True).reshape(-1, width)
        vec = jnp.concatenate([vec, bias_one], axis=0)
        vec = jnp.concatenate([vec, jnp.zeros((VEC_ROWS - vec.shape[0], width), BF)], axis=0)

        def by_columns(shard):
            full = lax.all_gather(shard, "fsdp", axis=0, tiled=True)
            return full.reshape(4, 2, piece, 2, 2, width).transpose(3, 4, 0, 1, 2, 5)

        full_a = by_columns(jnp.concatenate([w_qkv, w_out], axis=1))
        full_1 = by_columns(w_fc1)
        full_2 = lax.all_gather(w_fc2, "fsdp", axis=0, tiled=True)
        full_2 = full_2.reshape(4, 2, 2, 2, piece, width).transpose(2, 3, 0, 1, 4, 5)
        forward = forward_call(dims, pad, False)(lengths, vec, tokens, cotangent, full_a, full_1, full_2)
        out, n1, qkv, prob, mixed, resid, n2, act, slope, gffn, acc, vec = forward
    backward = backward_call(dims, pad, comm)(
        lengths, vec, acc, tokens, cotangent, full_a, full_1, full_2, n1, qkv, prob, mixed, resid, n2, act, slope, gffn
    )
    if comm:
        grad_tokens, sum_qkv, sum_out, sum_1, sum_2, sums = backward
        grad_tokens, out, sum_qkv, sum_out, sum_1, sum_2, bias_one, *mine = last_call(
            dims, grad_tokens, out, sum_qkv, sum_out, sum_1, sum_2.reshape(-1, width), sums
        )
    else:
        grad_tokens, da, d1, d2, sums = backward

        def total(array):
            part = lax.psum_scatter(array, "fsdp", scatter_dimension=0, tiled=True)
            return lax.psum(part, "dp")

        d1 = d1.transpose(2, 3, 4, 0, 1, 5).reshape(width, hidden)
        d2 = d2.transpose(2, 3, 0, 1, 4, 5).reshape(hidden, width)
        first = da[..., : width // 2].transpose(2, 3, 4, 0, 1, 5).reshape(width, 4, 3, 128)
        second = da[..., width // 2 :].transpose(2, 3, 4, 0, 1, 5).reshape(width, 4, 3, 128)
        heads = jnp.concatenate([first[:, :2], second], axis=1).transpose(0, 2, 1, 3).reshape(width, 3 * width)
        sum_a = total(jnp.concatenate([heads, first[:, 2:].reshape(width, width)], axis=1))
        sum_qkv, sum_out = sum_a[:, : 3 * width], sum_a[:, 3 * width :]
        sum_1, sum_2 = total(d1), total(d2)
        sums = lax.psum(sums, ("fsdp", "dp"))
        own_piece = width // fsdp
        mine = lax.dynamic_slice(sums, (0, me * own_piece), (FB1_ROW, own_piece))
        bias_sums = sums[FB1_ROW : FB1_ROW + hidden // width].reshape(-1)
        bias_one = lax.dynamic_slice(bias_sums, (me * (hidden // fsdp),), (hidden // fsdp,))
    return (
        out, grad_tokens, mine[G1_ROW], mine[B1_ROW], sum_qkv.astype(F32),
        jnp.stack([mine[QB_ROW], mine[VB_ROW]], axis=1), sum_out.astype(F32), mine[OB_ROW], mine[SA_ROW],
        mine[G2_ROW], mine[B2_ROW], sum_1.astype(F32), bias_one, sum_2.astype(F32), mine[FB2_ROW], mine[SF_ROW],
    )


def solution(mesh):
    both, one, two = P(("fsdp", "dp"), None), P("fsdp"), P("fsdp", None)
    in_specs = (both, both, both, one, one, two, two, two, one, one, one, one, two, one, two, one, one)
    out_specs = (both, both, one, one, two, two, two, one, one, one, one, two, one, two, one, one)
    run = functools.partial(local, mesh.shape["fsdp"], mesh.shape["dp"])
    return jax.shard_map(run, mesh=mesh, in_specs=in_specs, out_specs=out_specs, check_vma=False)
```
